32 devices in a mesh: dp: 16 (over z, y, core), seq: 2 (over x).
Axes of the slice: x: 2, y: 2, z: 4, core: 2. Of those that a mesh axis runs over, the one named last changes fastest.
Arguments:
- images: bfloat16 [48, 640, 512], P('dp', 'seq'), may hold values from -6 to 6
- cotangent: bfloat16 [48, 640, 512], P('dp', 'seq'), may hold values from -8 to 8
- lengths: int32 [48], P('dp'), may hold values from 320 to 640, as said below
- routes: int32 [16, 3, 2, 320, 2], P('dp', None, 'seq'), may hold values from 0 to 15, all different within a row; in each aligned block of 320 rows (0 to 319, 320 to 639, ..., all dimensions but the last counted through in order) at most 50 rows name the same one
- attn_norm_gain: bfloat16 [512], P('dp'), may hold values from 0.5 to 1.5
- attn_norm_bias: bfloat16 [512], P('dp'), may hold values from -1.25 to 1.25
- qkv_weight: bfloat16 [512, 1536], P('dp'), may hold values from -0.375 to 0.375
- query_value_bias: bfloat16 [2, 512], P(None, 'dp'), may hold values from -1.25 to 1.25
- proj_weight: bfloat16 [512, 512], P('dp'), may hold values from -0.75 to 0.75
- proj_bias: bfloat16 [512], P('dp'), may hold values from -1.25 to 1.25
- moe_norm_gain: bfloat16 [512], P('dp'), may hold values from 0.5 to 1.5
- moe_norm_bias: bfloat16 [512], P('dp'), may hold values from -1.25 to 1.25
- router_weight: bfloat16 [512, 16], P('dp'), may hold values from -0.25 to 0.25
- up_weight: bfloat16 [16, 512, 2048], P('dp'), may hold values from -0.25 to 0.25
- up_bias: bfloat16 [16, 2048], P('dp'), may hold values from -3 to 3
- down_weight: bfloat16 [16, 2048, 512], P('dp'), may hold values from -1 to 1
- down_bias: bfloat16 [16, 512], P('dp'), may hold values from -6 to 6
Outputs:
- block_out: bfloat16 [48, 640, 512], P('dp', 'seq')
- input_grad: bfloat16 [48, 640, 512], P('dp', 'seq')
- grad_attn_norm_gain: float32 [512], P('dp')
- grad_attn_norm_bias: float32 [512], P('dp')
- grad_qkv_weight: float32 [512, 1536], P('dp')
- grad_query_value_bias: float32 [2, 512], P(None, 'dp')
- grad_proj_weight: float32 [512, 512], P('dp')
- grad_proj_bias: float32 [512], P('dp')
- grad_moe_norm_gain: float32 [512], P('dp')
- grad_moe_norm_bias: float32 [512], P('dp')
- grad_router_weight: float32 [512, 16], P('dp')
- grad_up_weight: float32 [16, 512, 2048], P('dp')
- grad_up_bias: float32 [16, 2048], P('dp')
- grad_down_weight: float32 [16, 2048, 512], P('dp')
- grad_down_bias: float32 [16, 512], P('dp')
The draws below stay inside these ranges and needn't reach their ends.
Inputs may be any that keep to these rules, and one draw needn't show every extreme that they name: `lengths`: real tokens of each image; its later slots are pads, masked as keys; some image is full and some has half of its slots. `routes`: the 2 experts of a row differ; in each aligned block of 320 rows (one group) no expert is named by more than 50 rows, a bound that some block reaches.
All inputs are finite; a program needn't handle non-finite values.
Results may differ from the reference program's by a relative error of at most 0.023.
Values may be sent and summed in bfloat16 or wider, within the bound.
No kernel may reach another device: no remote copies, remote signals or barrier semaphores. Data moves between devices by JAX's collectives and lax.ppermute only.
A program may use at most 192 MiB of HBM per device.

```python
import math
import jax
import jax.numpy as jnp
import numpy as np
from jax import lax

D = 512
H = 8
HD = 64
FF = 2048
TOP = 2
L = 640
TOK_MB = 320
MICRO = 3
E = 16
LS = 320
IMG_MB = 1
IMAGES = 48
C = 50
N_DP = 16
N_SEQ = 2


def draw_lengths(key, part):
    drawn = jax.random.randint(key, (IMAGES,), L // 2, L + 1, dtype=jnp.int32)
    drawn = drawn.at[0].set(L)
    drawn = drawn.at[1].set(L // 2)
    return drawn


def strengthened(values, rng, source, target, shards_of, factor):
    owner, partner = [(jnp.arange(values.shape[position]) // (values.shape[position] // shards_of)).reshape([-1 if axis == position else 1 for axis in range(values.ndim)]) for position in (source, target)]
    chosen = jax.random.permutation(rng, shards_of)[partner]
    strong = (owner == chosen) | (owner == (partner + shards_of // 2) % shards_of)
    return jnp.where(strong, factor * values, values)


def block_levels(own_key, shape, cuts, least, high):
    factor_of, own = 1.0, jax.random.fold_in(own_key, 6)
    for axis_at, blocks in cuts:
        heights = jnp.exp(jax.random.uniform(jax.random.fold_in(own, axis_at), (blocks,), jnp.float32, least / len(cuts), high / len(cuts)))
        factor_of = factor_of * jnp.repeat(heights, shape[axis_at] // blocks).reshape([-1 if axis == axis_at else 1 for axis in range(len(shape))])
    return factor_of


def routed_block(key, own, number, rows, number_of, top, bound, lean):
    order = jax.random.permutation(key, number_of)
    packed, usual = portions_of(number_of, rows * top, bound, lean, True), portions_of(number_of, rows * top, bound, lean, False)
    places = jnp.arange(number_of)

    def named(sizes, turn):
        used = int((sizes > 0).sum())
        fixed = max(1, used // 4)
        moved = fixed + (places - fixed + turn * (used - fixed)) % max(1, number_of - fixed)
        return jnp.zeros((number_of,), jnp.int32).at[order[jnp.where(places < fixed, places, moved)]].set(jnp.asarray(sizes, jnp.int32))

    sizes = jnp.where(number % 4 == 0, named(packed, number // 4), named(usual, number - number // 4 - 1))
    mixed = jax.random.permutation(jax.random.fold_in(own, 3), number_of)
    donor, receiver = mixed[0:number_of // 2 * 2:2], mixed[1:number_of // 2 * 2:2]
    room = jnp.minimum(sizes[donor] - 1, bound - sizes[receiver]) // 2
    room = jnp.where((donor == order[0]) | (receiver == order[0]) | (sizes[receiver] == 0), 0, jnp.maximum(room, 0))
    moved = jax.random.randint(jax.random.fold_in(own, 4), (number_of // 2,), 0, 1 << 20) % (room + 1)
    sizes = sizes.at[donor].add(-moved).at[receiver].add(moved)
    members = jnp.searchsorted(jnp.cumsum(sizes), jnp.arange(rows * top), side="right").astype(jnp.int32)
    listing = members.reshape(top, rows).T
    listing = listing[jax.random.permutation(jax.random.fold_in(own, 1), rows)]
    turn = jax.random.randint(jax.random.fold_in(own, 2), (rows, 1), 0, top)
    return jnp.take_along_axis(listing, (jnp.arange(top)[None, :] + turn) % top, axis=1)


def portions_of(amount, total, reach, slope, full):
    weights = [(1 << 20) // math.isqrt(grade ** slope) + 1 for grade in range(1, amount + 1)]
    largest = reach if full else min(reach, max(-(-total // amount), total * weights[0] // sum(weights)))
    least = 1 if total - largest >= amount - 1 else 0
    given, rest = [largest] + [least] * (amount - 1), total - largest - least * (amount - 1)
    while rest > 0:
        free = [i for i in range(1, amount) if given[i] < largest] or [i for i in range(1, amount) if given[i] < reach]
        whole, budget = sum([weights[i] for i in free]), rest
        for i in free:
            more = min(reach - given[i], max(1, budget * weights[i] // whole), rest)
            given[i] = given[i] + more
            rest = rest - more
    return np.array(given)


def noise(own_key, dims, deviation, reach, cuts=(), kind=jnp.bfloat16):
    array = deviation * jax.random.normal(own_key, dims, jnp.float32)
    if cuts:
        array = array * block_levels(own_key, dims, cuts, -0.22, 0.18)
    return jnp.clip(array, -reach, reach).astype(kind)


def gaussian_with(stream_key, shape, width, most, pieces, heavy, kind=jnp.bfloat16):
    values = width * jax.random.normal(stream_key, shape, jnp.float32)
    if pieces:
        values = values * block_levels(stream_key, shape, pieces, -0.22, 0.18)
    return jnp.clip(strengthened(values, jax.random.fold_in(stream_key, 3), *heavy), -most, most).astype(kind)


def setup_inputs(seed: int = 0) -> dict:
    splits = jax.random.split(jax.random.key(seed), 18)
    images = noise(splits[0], (IMAGES, L, D), 1.0, 6.0, ((0, 16), (1, 2)))
    cotangent = gaussian_with(splits[1], (IMAGES, L, D), 1.0, 8.0, ((0, 16), (1, 2)), (0, 2, 16, 2.0))
    lengths = draw_lengths(jax.random.fold_in(splits[17], 71), 0)
    routes_keys = jax.random.split(jax.random.fold_in(splits[3], 1), N_DP * MICRO * N_SEQ * TOK_MB // TOK_MB)
    routes_turns = jax.random.permutation(jax.random.fold_in(splits[3], 3), N_DP * MICRO * N_SEQ * TOK_MB // TOK_MB)
    routes = jax.vmap(lambda own, number: routed_block(jax.random.fold_in(splits[3], 2), own, number, TOK_MB, E, TOP, C, 1))(routes_keys, routes_turns).reshape((N_DP, MICRO, N_SEQ, TOK_MB, TOP))
    attn_norm_gain = jnp.clip(1.0 + 0.1 * jax.random.normal(splits[4], (D,), jnp.float32), 0.5, 1.5).astype(jnp.bfloat16)
    attn_norm_bias = noise(splits[5], (D,), 0.2, 1.25, ((0, 16),))
    qkv_weight = noise(splits[6], (D, 3 * D), (D // 2) ** -0.5, 0.375, ((0, 16),))
    query_value_bias = noise(splits[7], (2, D), 0.2, 1.25, ((1, 16),))
    proj_weight = noise(splits[8], (D, D), (D // 8) ** -0.5, 0.75, ((0, 16),))
    proj_bias = noise(splits[9], (D,), 0.2, 1.25, ((0, 16),))
    moe_norm_gain = jnp.clip(1.0 + 0.1 * jax.random.normal(splits[10], (D,), jnp.float32), 0.5, 1.5).astype(jnp.bfloat16)
    moe_norm_bias = noise(splits[11], (D,), 0.2, 1.25, ((0, 16),))
    router_weight = noise(splits[12], (D, E), D ** -0.5, 0.25, ((0, 16),))
    up_weight = noise(splits[13], (E, D, FF), D ** -0.5, 0.25, ((0, 16),))
    up_bias = noise(splits[14], (E, FF), 0.5, 3.0, ((0, 16),))
    down_weight = noise(splits[15], (E, FF, D), (max(4 * FF // (E * E), 1)) ** -0.5, 1.0, ((0, 16),))
    down_bias = noise(splits[16], (E, D), 1.0, 6.0, ((0, 16),))
    return dict(images=images, cotangent=cotangent, lengths=lengths, routes=routes, attn_norm_gain=attn_norm_gain, attn_norm_bias=attn_norm_bias, qkv_weight=qkv_weight, query_value_bias=query_value_bias, proj_weight=proj_weight, proj_bias=proj_bias, moe_norm_gain=moe_norm_gain, moe_norm_bias=moe_norm_bias, router_weight=router_weight, up_weight=up_weight, up_bias=up_bias, down_weight=down_weight, down_bias=down_bias)


@jax.custom_vjp
def low(v):
    return lax.optimization_barrier(v.astype(jnp.bfloat16)).astype(jnp.float32)

@jax.custom_vjp
def low_back(v):
    return v

def low_keep(v):
    return (low(v), None)

def low_pass(kept, grad):
    return (grad,)

def back_keep(v):
    return (v, None)

def back_low(kept, grad):
    return (low(grad),)
low.defvjp(low_keep, low_pass)
low_back.defvjp(back_keep, back_low)

def layer_norm(values, gain_vec, shift_vec):
    average = lax.optimization_barrier(jnp.mean(values, axis=-1, keepdims=True))
    centred = values - average
    spread = lax.optimization_barrier(jnp.mean(centred * centred, axis=-1, keepdims=True))
    return centred * lax.rsqrt(spread + 1e-06) * gain_vec + shift_vec

def exact_gelu(values):
    return jax.nn.gelu(values, approximate=False)

def slot_places(expert_ids):
    flattened = expert_ids.reshape(TOK_MB * TOP)
    onehot = (flattened[:, None] == jnp.arange(E, dtype=jnp.int32)[None, :]).astype(jnp.int32)
    before = (jnp.cumsum(onehot, axis=0) - onehot).astype(jnp.int32)
    within = lax.optimization_barrier(jnp.sum(before * onehot, axis=1)).astype(jnp.int32)
    places = (flattened * C + within).astype(jnp.int32)
    owners = (jnp.arange(TOK_MB * TOP, dtype=jnp.int32) // TOP).astype(jnp.int32)
    slot_table = jnp.full((E * C,), TOK_MB, jnp.int32).at[places].set(owners)
    return (places, slot_table)

def forward(images_f, params, key_valid, expert_ids, places, slot_table):
    gain_first, shift_first, qkv_full, qv_full, proj_full, proj_shift, gain_second, shift_second, router_full, up_full, up_shift, down_full, down_shift = params
    image_count = images_f.shape[0]
    score_scale = HD ** (-0.5)
    highest_precision = lax.Precision.HIGHEST
    normed_one = low(layer_norm(images_f, gain_first, shift_first))
    qkv_bias = jnp.concatenate([qv_full[0], jnp.zeros((D,), jnp.float32), qv_full[1]])
    projected = jnp.einsum('nld,de->nle', normed_one, qkv_full, precision=highest_precision) + qkv_bias
    projected = low_back(low(projected)).reshape(image_count, L, 3, H, HD)
    queries = projected[:, :, 0]
    keys_in = projected[:, :, 1]
    values = projected[:, :, 2]
    scores = low_back(jnp.einsum('nqhd,nkhd->nhqk', queries, keys_in, precision=highest_precision) * score_scale)
    scores = jnp.where(key_valid[:, None, None, :], scores, -1e+30)
    attn_probs = low(jax.nn.softmax(scores, axis=-1))
    attended = jnp.einsum('nhqk,nkhd->nqhd', attn_probs, values, precision=highest_precision)
    attended = low_back(low(attended)).reshape(image_count, L, D)
    branch = low_back(jnp.einsum('nld,de->nle', attended, proj_full, precision=highest_precision) + proj_shift)
    middle = images_f + branch
    normed_two = low(layer_norm(middle, gain_second, shift_second))
    logits = low_back(jnp.einsum('nld,de->nle', normed_two, router_full, precision=highest_precision))
    gate_probs = jax.nn.softmax(logits, axis=-1)
    grouped = normed_two.reshape(image_count, N_SEQ, LS, D).transpose(1, 0, 2, 3).reshape(N_SEQ, TOK_MB, D)
    grouped_probs = gate_probs.reshape(image_count, N_SEQ, LS, E).transpose(1, 0, 2, 3).reshape(N_SEQ, TOK_MB, E)
    padded = jnp.concatenate([grouped, jnp.zeros((N_SEQ, 1, D), jnp.float32)], axis=1)
    buffers = low_back(jnp.take_along_axis(padded, slot_table[:, :, None], axis=1)).reshape(N_SEQ, E, C, D)
    hidden = jnp.einsum('gecd,edf->gecf', buffers, up_full, precision=highest_precision) + up_shift[None, :, None, :]
    hidden = low_back(hidden)
    active = low(exact_gelu(hidden))
    result = jnp.einsum('gecf,efd->gecd', active, down_full, precision=highest_precision) + down_shift[None, :, None, :]
    result = low_back(low(result)).reshape(N_SEQ, E * C, D)
    picked = jnp.take_along_axis(result, places[:, :, None], axis=1).reshape(N_SEQ, TOK_MB, TOP, D)
    gate_now = jnp.take_along_axis(grouped_probs, expert_ids, axis=2)
    mixture = lax.optimization_barrier(jnp.sum(gate_now[:, :, :, None] * picked, axis=2))
    mixture = mixture.reshape(N_SEQ, image_count, LS, D).transpose(1, 0, 2, 3).reshape(image_count, L, D)
    return middle + mixture

def reference(images, cotangent, lengths, routes, attn_norm_gain, attn_norm_bias, qkv_weight, query_value_bias, proj_weight, proj_bias, moe_norm_gain, moe_norm_bias, router_weight, up_weight, up_bias, down_weight, down_bias):
    params = tuple((weight_arg.astype(jnp.float32) for weight_arg in (attn_norm_gain, attn_norm_bias, qkv_weight, query_value_bias, proj_weight, proj_bias, moe_norm_gain, moe_norm_bias, router_weight, up_weight, up_bias, down_weight, down_bias)))
    step_count = N_DP * MICRO
    image_steps = images.reshape(step_count, IMG_MB, L, D)
    cot_steps = cotangent.reshape(step_count, IMG_MB, L, D)
    length_steps = lengths.reshape(step_count, IMG_MB)
    route_steps = routes.reshape(step_count, N_SEQ, TOK_MB, TOP)

    def one_step(totals, inputs):
        image_block, cot_block, length_block, route_block = inputs
        key_valid = jnp.arange(L, dtype=jnp.int32)[None, :] < length_block[:, None]
        places, slot_table = jax.vmap(slot_places)(route_block)

        def run_block(image_f, weights_in):
            return forward(image_f, weights_in, key_valid, route_block, places, slot_table)
        outputs, pullback = jax.vjp(run_block, image_block.astype(jnp.float32), params)
        grad_images, grad_params = pullback(cot_block.astype(jnp.float32))
        totals = jax.tree.map(lambda first_term, second_term: first_term + second_term, totals, grad_params)
        return (totals, (outputs.astype(jnp.bfloat16), grad_images.astype(jnp.bfloat16)))
    zero_init = tuple((jnp.zeros(weight_arg.shape, jnp.float32) for weight_arg in params))
    totals, (out_steps, grad_steps) = lax.scan(one_step, zero_init, (image_steps, cot_steps, length_steps, route_steps))
    grad_gain_first, grad_shift_first, grad_qkv, grad_qv, grad_proj, grad_proj_shift, grad_gain_second, grad_shift_second, grad_router, grad_up, grad_up_shift, grad_down, grad_down_shift = totals
    return (out_steps.reshape(IMAGES, L, D), grad_steps.reshape(IMAGES, L, D), grad_gain_first, grad_shift_first, grad_qkv, grad_qv, grad_proj, grad_proj_shift, grad_gain_second, grad_shift_second, grad_router, grad_up, grad_up_shift, grad_down, grad_down_shift)
```

```python
import functools

import jax
import jax.numpy as jnp
from jax import lax
from jax.experimental import pallas as pl
from jax.experimental.pallas import tpu as pltpu
from jax.sharding import PartitionSpec as P

HD = 64
TOP = 2
MICRO = 3
BF = jnp.bfloat16
F32 = jnp.float32
EPS = 1e-06
LANES = 128
VEC = 7
FF_BLOCK = 512
VMEM_LIMIT = 60 * 1024 * 1024


def mm(left, right):
    return jnp.dot(left, right, preferred_element_type=F32)


def mm_nt(left, right):
    return lax.dot_general(
        left, right, (((1,), (1,)), ((), ())), preferred_element_type=F32
    )


def iota(shape, dim):
    return lax.broadcasted_iota(jnp.int32, shape, dim)


def norm_parts(values):
    average = jnp.mean(values, axis=-1, keepdims=True)
    centred = values - average
    spread = jnp.mean(centred * centred, axis=-1, keepdims=True)
    scale = lax.rsqrt(spread + EPS)
    return centred * scale, scale


def norm_pull(unit, scale, gain, cotangent):
    inner = cotangent * gain
    mean_inner = jnp.mean(inner, axis=-1, keepdims=True)
    mean_unit = jnp.mean(inner * unit, axis=-1, keepdims=True)
    return scale * (inner - mean_inner - unit * mean_unit)


def misc_rows(w_ref, start):
    return jnp.transpose(w_ref[:, start : start + LANES].astype(F32))


def place_kernel(experts, room, cols_ref, rows_ref, dy_ref, send_ref, prow_ref, pcol_ref):
    tokens = cols_ref.shape[1]
    slots = experts * room
    first_row = rows_ref[0, 0:1, :]
    second_row = rows_ref[0, 1:2, :]
    hot_first = (iota((experts, tokens), 0) == first_row).astype(F32)
    hot_second = (iota((experts, tokens), 0) == second_row).astype(F32)
    earlier = (iota((tokens, tokens), 0) < iota((tokens, tokens), 1)).astype(BF)
    before = mm((hot_first + hot_second).astype(BF), earlier)
    in_first = jnp.sum(before * hot_first, axis=0, keepdims=True).astype(jnp.int32)
    in_second = jnp.sum((before + hot_first) * hot_second, axis=0, keepdims=True).astype(jnp.int32)
    place_first = first_row * room + in_first
    place_second = second_row * room + in_second
    prow_ref[0:1, :] = place_first
    prow_ref[1:2, :] = place_second
    slot_of = iota((slots, tokens), 0)
    hot = jnp.where((slot_of == place_first) | (slot_of == place_second), 1.0, 0.0).astype(BF)
    flat = dy_ref[...].reshape(tokens, dy_ref.shape[-1])
    rows = mm(hot, flat)
    for e in range(experts):
        send_ref[e] = rows[e * room : (e + 1) * room].astype(BF)
    first_col = cols_ref[0, :, 0:1]
    second_col = cols_ref[0, :, 1:2]
    hot_first = (iota((tokens, experts), 1) == first_col).astype(F32)
    hot_second = (iota((tokens, experts), 1) == second_col).astype(F32)
    later = (iota((tokens, tokens), 1) < iota((tokens, tokens), 0)).astype(BF)
    before = mm(later, (hot_first + hot_second).astype(BF))
    in_first = jnp.sum(before * hot_first, axis=1, keepdims=True).astype(jnp.int32)
    in_second = jnp.sum((before + hot_first) * hot_second, axis=1, keepdims=True).astype(jnp.int32)
    lane = iota((tokens, 8), 1)
    table = jnp.zeros((tokens, 8), jnp.int32)
    for at, col in enumerate(
        (
            first_col * room + in_first,
            second_col * room + in_second,
            first_col,
            second_col,
            in_first,
            in_second,
        )
    ):
        table = jnp.where(lane == at, col, table)
    pcol_ref[...] = table


def forward_kernel(
    cfg,
    mb,
    meta_ref,
    len_ref,
    own_ref,
    oth_ref,
    w_ref,
    prow_ref,
    send_ref,
    middle_ref,
    gate_ref,
    second_ref,
    oT_ref,
    q_ref,
    k_ref,
    v_ref,
    lse_ref,
    n1T_ref,
    att_ref,
    logs_ref,
):
    images, local_len, seq_count, width, experts, room = cfg
    full_len = local_len * seq_count
    tokens = images * local_len
    slots = experts * room
    misc_at = 4 * width
    rows = misc_rows(w_ref, misc_at)

    def vec(j):
        return rows[experts + j : experts + j + 1, :]

    here = meta_ref[1]
    lane = iota((1, LANES), 1)
    low_half = (lane < HD).astype(BF)
    high_half = (lane >= HD).astype(BF)
    for b in range(images):
        blocks = [own_ref[b]] + [oth_ref[j, b] for j in range(seq_count - 1)]
        full = jnp.concatenate(blocks, axis=0).astype(F32)
        unit, _ = norm_parts(full)
        normed = (unit * vec(0) + vec(1)).astype(BF)
        n1T_ref[:, b * full_len : (b + 1) * full_len] = jnp.transpose(normed)
        span = slice(b * local_len, (b + 1) * local_len)
        wide = slice(b * full_len, (b + 1) * full_len)
        queries = (mm(normed[:local_len], w_ref[:, :width]) + vec(2)).astype(BF)
        q_ref[span, :] = queries * jnp.asarray(HD**-0.5, BF)
        k_ref[wide, :] = mm(normed, w_ref[:, width : 2 * width]).astype(BF)
        v_ref[wide, :] = (mm(normed, w_ref[:, 2 * width : 3 * width]) + vec(3)).astype(BF)
        kpos = iota((1, full_len), 1)
        shift = jnp.zeros((1, full_len), jnp.int32)
        for j in range(seq_count):
            origin = lax.rem(here + j, seq_count) * local_len - j * local_len
            shift = jnp.where(kpos >= j * local_len, origin, shift)
        valid = (kpos + shift) < len_ref[mb * images + b]
        logs_ref[...] = jnp.zeros_like(logs_ref)

        def heads(blk, carry):
            at = pl.ds(pl.multiple_of(blk * LANES, LANES), LANES)
            q_blk = q_ref[span, at]
            k_blk = k_ref[wide, at]
            v_blk = v_ref[wide, at]
            outs = []
            for side, keep in enumerate((low_half, high_half)):
                scores = mm_nt(q_blk * keep, k_blk)
                scores = jnp.where(valid, scores, -1e30)
                highest = jnp.max(scores, axis=1, keepdims=True)
                powers = jnp.exp(scores - highest)
                total = jnp.sum(powers, axis=1, keepdims=True)
                probs = (powers * (1.0 / total)).astype(BF)
                outs.append(mm(probs, v_blk))
                logs_ref[...] = jnp.where(
                    lane == 2 * blk + side, highest + jnp.log(total), logs_ref[...]
                )
            att_ref[span, at] = jnp.where(lane < HD, outs[0], outs[1]).astype(BF)
            return carry

        lax.fori_loop(0, width // LANES, heads, 0)
        lse_ref[b * 8 : b * 8 + 8, :] = jnp.transpose(logs_ref[...])[0:8, :]
    attended = att_ref[...]
    oT_ref[...] = jnp.transpose(attended)
    branch = mm(attended, w_ref[:, 3 * width : 4 * width]) + vec(4)
    middle = own_ref[...].reshape(tokens, width).astype(F32) + branch
    middle_ref[...] = middle
    unit, _ = norm_parts(middle)
    second = (unit * vec(5) + vec(6)).astype(BF)
    second_ref[...] = second
    gate_ref[...] = gates(mm(second, w_ref[:, misc_at : misc_at + LANES]), experts)
    slot_of = iota((slots, tokens), 0)
    hot = jnp.where(
        (slot_of == prow_ref[0:1, :]) | (slot_of == prow_ref[1:2, :]), 1.0, 0.0
    ).astype(BF)
    sent = mm(hot, second)
    for e in range(experts):
        send_ref[e] = sent[e * room : (e + 1) * room].astype(BF)


def gates(logits, experts):
    real = iota((1, LANES), 1) < experts
    logits = jnp.where(real, logits, -1e30)
    powers = jnp.where(real, jnp.exp(logits - jnp.max(logits, axis=1, keepdims=True)), 0.0)
    return powers / jnp.sum(powers, axis=1, keepdims=True)


def expert_kernel(cfg, first, *refs):
    groups, room, capacity, width = cfg
    meta_ref, buf_ref, dyb_ref, wm_ref, up_ref, ub_ref, down_ref, db_ref = refs[:8]
    refs = refs[8:]
    if not first:
        gup_in, gdn_in, gb_in, gdb_in = refs[:4]
        refs = refs[4:]
    (
        r_ref,
        dbuf_ref,
        gup_ref,
        gdn_ref,
        gb_ref,
        gdb_ref,
        flat_s,
        flatT_s,
        dr_s,
        drT_s,
        racc_s,
        dacc_s,
    ) = refs
    slots = groups * room
    step = pl.program_id(0)
    experts = groups

    @pl.when(step == 0)
    def _():
        flat = buf_ref[...].astype(F32).reshape(slots, width).astype(BF)
        flat_s[...] = flat
        flatT_s[...] = jnp.transpose(flat)
        gate = gates(mm(flat, wm_ref[...]), experts)
        mine = iota((1, LANES), 1) == meta_ref[0]
        mine_gate = jnp.sum(jnp.where(mine, gate, 0.0), axis=1, keepdims=True)
        dr = (dyb_ref[...].astype(F32).reshape(slots, width) * mine_gate).astype(BF)
        dr_s[...] = dr
        drT_s[...] = jnp.transpose(dr)
        shift_sum = jnp.sum(dr.astype(F32), axis=0, keepdims=True)
        gdb_ref[...] = shift_sum if first else gdb_in[...] + shift_sum
        racc_s[...] = jnp.zeros_like(racc_s)
        dacc_s[...] = jnp.zeros_like(dacc_s)

    flat = flat_s[...]
    dr = dr_s[...]
    hidden = mm(flat, up_ref[0]) + ub_ref[...].astype(F32)
    half_erf = 0.5 * lax.erf(hidden * (0.5**0.5)) + 0.5
    active = (hidden * half_erf).astype(BF)
    slope = half_erf + hidden * (jnp.exp(-0.5 * hidden * hidden) * 0.3989422804014327)
    racc_s[...] += mm(active, down_ref[0])
    grad_pre = mm_nt(dr, down_ref[0]) * slope
    low_pre = grad_pre.astype(BF)
    dacc_s[...] += mm_nt(low_pre, up_ref[0])
    gup = mm(flatT_s[...], low_pre)
    gdn = mm(drT_s[...], active)
    gbias = jnp.sum(low_pre.astype(F32), axis=0, keepdims=True)
    if first:
        gup_ref[...] = gup
        gdn_ref[...] = gdn
        gb_ref[...] = gbias
    else:
        gup_ref[...] = gup_in[...] + gup
        gdn_ref[...] = gdn_in[...] + gdn
        gb_ref[...] = gb_in[...] + gbias

    @pl.when(step == pl.num_programs(0) - 1)
    def _():
        result = (racc_s[...] + db_ref[...].astype(F32)).astype(BF)
        for e in range(groups):
            r_ref[e] = result[e * room : (e + 1) * room]
        dy = dyb_ref[...].astype(F32).reshape(slots, width)
        dgate = jnp.sum(dy * result.astype(F32), axis=1, keepdims=True).reshape(groups, room, 1)
        spread = jnp.where(
            iota((groups, room, LANES), 2) == iota((groups, room, LANES), 1), dgate, 0.0
        )
        as_row = jnp.sum(spread, axis=1, keepdims=True)
        high = as_row.astype(BF).astype(F32)
        tail = jnp.zeros((groups, 1, width - 2 * LANES), F32)
        as_row = jnp.concatenate([high, as_row - high, tail], axis=2)
        back = dacc_s[...].reshape(groups, room, width)
        back = jnp.where(iota((groups, room, 1), 1) == capacity, as_row, back).astype(BF)
        for e in range(groups):
            dbuf_ref[e] = back[e]


def backward_kernel(cfg, mb, first, *refs):
    images, local_len, seq_count, width, experts, room, capacity = cfg
    (
        meta_ref,
        len_ref,
        dback_ref,
        pcol_ref,
        gate_ref,
        middle_ref,
        second_ref,
        dy_ref,
        oT_ref,
        w_ref,
        q_ref,
        k_ref,
        v_ref,
        lse_ref,
        n1T_ref,
    ) = refs[:15]
    refs = refs[15:]
    if not first:
        g_in, mrow_in = refs[:2]
        refs = refs[2:]
    down_own, down_oth, dm_ref, g_ref, mrow_ref, do_s, dqT_s, dkv_s = refs
    full_len = local_len * seq_count
    tokens = images * local_len
    slots = experts * room
    misc_at = 4 * width
    rows = misc_rows(w_ref, misc_at)
    here = meta_ref[1]

    def vec(j):
        return rows[experts + j : experts + j + 1, :]

    dback = dback_ref[...].astype(F32)
    back_rows = dback.reshape(slots, width).astype(BF)
    slot_of = iota((tokens, slots), 1)
    hot = jnp.where(
        (slot_of == pcol_ref[:, 0:1]) | (slot_of == pcol_ref[:, 1:2]), 1.0, 0.0
    ).astype(BF)
    from_experts = mm(hot, back_rows)
    spare = jnp.where(iota((experts, room, 1), 1) == capacity, dback[:, :, : 2 * LANES], 0.0)
    spare = jnp.sum(spare, axis=1)
    spare = jnp.concatenate(
        [spare, jnp.zeros((LANES - experts, 2 * LANES), F32)], axis=0
    ).astype(BF)
    lane = iota((tokens, LANES), 1)
    pulled = jnp.zeros((tokens, LANES), F32)
    for k in range(TOP):
        within = jnp.where(lane == pcol_ref[:, 4 + k : 5 + k], 1.0, 0.0).astype(BF)
        found = mm_nt(jnp.concatenate([within, within], axis=1), spare)
        pulled = pulled + jnp.where(lane == pcol_ref[:, 2 + k : 3 + k], found, 0.0)
    gate = gate_ref[...]
    dlogit = gate * (pulled - jnp.sum(gate * pulled, axis=1, keepdims=True))
    dlogit_low = dlogit.astype(BF)
    mrow_ref[...] = mm(jnp.transpose(dlogit_low.astype(F32)).astype(BF), second_ref[...])
    dn2 = from_experts + mm_nt(dlogit_low, w_ref[:, misc_at : misc_at + LANES])
    unit, scale = norm_parts(middle_ref[...])
    dy = dy_ref[...].reshape(tokens, width).astype(F32)
    dm = dy + norm_pull(unit, scale, vec(5), dn2)
    dm_ref[...] = dm
    da = dm.astype(BF)
    gproj = mm(oT_ref[...], da)
    proj = slice(3 * width, 4 * width)
    if first:
        g_ref[:, proj] = gproj
    else:
        g_ref[:, proj] = g_in[:, proj] + gproj
    do_s[...] = mm_nt(da, w_ref[:, proj]).astype(BF)
    half_lane = iota((1, LANES), 1)
    low_half = (half_lane < HD).astype(BF)
    high_half = (half_lane >= HD).astype(BF)
    gqkv = [None, None]
    bias_q = jnp.zeros((1, width), F32)
    bias_v = jnp.zeros((1, width), F32)
    for b in range(images):
        span = slice(b * local_len, (b + 1) * local_len)
        wide = slice(b * full_len, (b + 1) * full_len)
        kpos = iota((full_len, 1), 0)
        shift = jnp.zeros((full_len, 1), jnp.int32)
        for j in range(seq_count):
            origin = lax.rem(here + j, seq_count) * local_len - j * local_len
            shift = jnp.where(kpos >= j * local_len, origin, shift)
        valid = (kpos + shift) < len_ref[mb * images + b]

        def heads(blk, carry):
            at = pl.ds(pl.multiple_of(blk * LANES, LANES), LANES)
            q_blk = q_ref[span, at]
            k_blk = k_ref[wide, at]
            v_blk = v_ref[wide, at]
            do_blk = do_s[span, at]
            kT_blk = jnp.transpose(k_blk)
            dvs = []
            dks = []
            dqs = []
            for side, keep in enumerate((low_half, high_half)):
                scores = mm_nt(k_blk, q_blk * keep)
                logs = lse_ref[pl.ds(b * 8 + 2 * blk + side, 1), :]
                probs = jnp.where(valid, jnp.exp(scores - logs), 0.0)
                dprobs = mm_nt(v_blk, do_blk * keep)
                inner = jnp.sum(probs * dprobs, axis=0, keepdims=True)
                dscores = (probs * (dprobs - inner)).astype(BF)
                dvs.append(mm(probs.astype(BF), do_blk))
                dks.append(mm(dscores, q_blk))
                dqs.append(mm(kT_blk[side * HD : (side + 1) * HD], dscores))
            dqT_s[pl.ds(pl.multiple_of(blk * LANES, LANES), HD), :] = dqs[0]
            dqT_s[pl.ds(pl.multiple_of(blk * LANES + HD, HD), HD), :] = dqs[1]
            left = half_lane < HD
            dkv_s[:, at] = jnp.where(left, dks[0], dks[1]).astype(BF)
            vat = pl.ds(pl.multiple_of(width + blk * LANES, LANES), LANES)
            dkv_s[:, vat] = jnp.where(left, dvs[0], dvs[1]).astype(BF)
            return carry

        lax.fori_loop(0, width // LANES, heads, 0)
        dq = (jnp.transpose(dqT_s[...]) * HD**-0.5).astype(BF)
        dkv = dkv_s[...]
        part_q = mm(n1T_ref[:, b * full_len : b * full_len + local_len], dq)
        part_kv = mm(n1T_ref[:, wide], dkv)
        gqkv[0] = part_q if b == 0 else gqkv[0] + part_q
        gqkv[1] = part_kv if b == 0 else gqkv[1] + part_kv
        bias_q = bias_q + jnp.sum(dq.astype(F32), axis=0, keepdims=True)
        bias_v = bias_v + jnp.sum(dkv[:, width:].astype(F32), axis=0, keepdims=True)
        down = mm_nt(dkv, w_ref[:, width : 3 * width])
        down_own[span, :] = mm_nt(dq, w_ref[:, :width])
        down_own[span, :] += down[:local_len]
        for j in range(seq_count - 1):
            down_oth[j, span, :] = down[(j + 1) * local_len : (j + 2) * local_len].astype(BF)
    if first:
        g_ref[:, :width] = gqkv[0]
        g_ref[:, width : 3 * width] = gqkv[1]
    else:
        g_ref[:, :width] = g_in[:, :width] + gqkv[0]
        g_ref[:, width : 3 * width] = g_in[:, width : 3 * width] + gqkv[1]
    row = iota((LANES, 1), 0)
    mrow = jnp.where(row < experts, mrow_ref[...], 0.0)
    sums = (
        bias_q,
        bias_v,
        jnp.sum(da.astype(F32), axis=0, keepdims=True),
        jnp.sum(dn2 * unit, axis=0, keepdims=True),
        jnp.sum(dn2, axis=0, keepdims=True),
    )
    for j, value in enumerate(sums):
        mrow = jnp.where(row == experts + 2 + j, value, mrow)
    mrow_ref[...] = mrow if first else mrow_in[...] + mrow


def input_kernel(cfg, own_ref, got_ref, x_ref, dm_ref, wm_ref, mrow_in, out_ref, mrow_ref):
    images, local_len, seq_count, width, experts = cfg
    tokens = images * local_len
    rows = jnp.transpose(wm_ref[...].astype(F32))
    dn1 = own_ref[...]
    for j in range(seq_count - 1):
        dn1 = dn1 + got_ref[j].astype(F32)
    unit, scale = norm_parts(x_ref[...].reshape(tokens, width).astype(F32))
    grad = dm_ref[...] + norm_pull(unit, scale, rows[experts : experts + 1, :], dn1)
    out_ref[...] = grad.astype(BF).reshape(images, local_len, width)
    row = iota((LANES, 1), 0)
    mrow = jnp.where(row == experts, jnp.sum(dn1 * unit, axis=0, keepdims=True), 0.0)
    mrow = jnp.where(row == experts + 1, jnp.sum(dn1, axis=0, keepdims=True), mrow)
    mrow_ref[...] = mrow_in[...] + mrow


def mix_kernel(cfg, back_ref, pcol_ref, gate_ref, middle_ref, out_ref):
    images, local_len, width, experts, room = cfg
    tokens = images * local_len
    slots = experts * room
    back = back_ref[...].astype(F32).reshape(slots, width).astype(BF)
    slot_of = iota((tokens, slots), 1)
    lane = iota((tokens, LANES), 1)
    gate = gate_ref[...]
    total = middle_ref[...]
    for k in range(TOP):
        hot = jnp.where(slot_of == pcol_ref[:, k : k + 1], 1.0, 0.0).astype(BF)
        chosen = jnp.where(lane == pcol_ref[:, 2 + k : 3 + k], gate, 0.0)
        total = total + jnp.sum(chosen, axis=1, keepdims=True) * mm(hot, back)
    out_ref[...] = total.astype(BF).reshape(images, local_len, width)


def sum_kernel(gup_ref, gdn_ref, got_up, got_dn, up_ref, dn_ref):
    up_ref[0] = gup_ref[...] + got_up[...].astype(F32)
    dn_ref[0] = jnp.transpose(gdn_ref[...] + got_dn[...].astype(F32))


def whole_spec():
    return pl.BlockSpec(memory_space=pltpu.VMEM)


def smem_spec():
    return pl.BlockSpec(memory_space=pltpu.SMEM)


def params():
    return pltpu.CompilerParams(vmem_limit_bytes=VMEM_LIMIT)


def struct(shape, kind):
    return jax.ShapeDtypeStruct(shape, kind)


def on_device(
    images,
    cotangent,
    lengths,
    routes,
    attn_norm_gain,
    attn_norm_bias,
    qkv_weight,
    query_value_bias,
    proj_weight,
    proj_bias,
    moe_norm_gain,
    moe_norm_bias,
    router_weight,
    up_weight,
    up_bias,
    down_weight,
    down_bias,
):
    seq_count = lax.axis_size("seq")
    dp_count = lax.axis_size("dp")
    count = images.shape[0] // MICRO
    local_len = images.shape[1]
    width = images.shape[2]
    tokens = count * local_len
    full_len = local_len * seq_count
    experts = router_weight.shape[1]
    hidden = up_weight.shape[2]
    capacity = (5 * tokens * TOP + 4 * experts - 1) // (4 * experts)
    room = (capacity + 1 + 7) // 8 * 8
    slots = experts * room
    assert up_weight.shape[0] == 1 and experts == dp_count
    assert experts + VEC <= LANES and capacity <= LANES
    meta = jnp.stack([lax.axis_index("dp"), lax.axis_index("seq")]).astype(jnp.int32)

    shard = router_weight.shape[0]
    pieces = [
        qkv_weight,
        proj_weight,
        router_weight,
        attn_norm_gain[:, None],
        attn_norm_bias[:, None],
        query_value_bias[0][:, None],
        query_value_bias[1][:, None],
        proj_bias[:, None],
        moe_norm_gain[:, None],
        moe_norm_bias[:, None],
        jnp.zeros((shard, LANES - experts - VEC), BF),
    ]
    packed = lax.all_gather(jnp.concatenate(pieces, axis=1), "dp", axis=0, tiled=True)
    packed_width = 4 * width + LANES

    others = jnp.stack(
        [
            lax.ppermute(
                images, "seq", [((i + j) % seq_count, i) for i in range(seq_count)]
            )
            for j in range(1, seq_count)
        ]
    )
    cols = routes.reshape(MICRO, tokens, TOP)
    rows = jnp.swapaxes(cols, 1, 2)

    def exchange(array):
        return lax.all_to_all(array, "dp", split_axis=0, concat_axis=0, tiled=True)

    def token_spec(mb):
        return pl.BlockSpec((count, local_len, width), lambda i: (mb, 0, 0))

    def full(shape):
        return pl.BlockSpec(shape, lambda i: (0,) * len(shape))

    misc_spec = pl.BlockSpec((width, LANES), lambda i: (0, 4 * width // LANES))
    moved = struct((experts, room, width), BF)

    def place(mb):
        return pl.pallas_call(
            functools.partial(place_kernel, experts, room),
            grid=(1,),
            in_specs=[
                pl.BlockSpec((1, tokens, TOP), lambda i: (mb, 0, 0)),
                pl.BlockSpec((1, TOP, tokens), lambda i: (mb, 0, 0)),
                token_spec(mb),
            ],
            out_specs=[
                full((experts, room, width)),
                full((TOP, tokens)),
                full((tokens, 8)),
            ],
            out_shape=[
                moved,
                struct((TOP, tokens), jnp.int32),
                struct((tokens, 8), jnp.int32),
            ],
            compiler_params=params(),
            name="place",
        )(cols, rows, cotangent)

    def forward(mb, prow):
        cfg = (count, local_len, seq_count, width, experts, room)
        outs = [
            ((experts, room, width), BF),
            ((tokens, width), F32),
            ((tokens, LANES), F32),
            ((tokens, width), BF),
            ((width, tokens), BF),
            ((tokens, width), BF),
            ((count * full_len, width), BF),
            ((count * full_len, width), BF),
            ((count * 8, local_len), F32),
            ((width, count * full_len), BF),
        ]
        return pl.pallas_call(
            functools.partial(forward_kernel, cfg, mb),
            grid=(1,),
            in_specs=[
                smem_spec(),
                smem_spec(),
                token_spec(mb),
                pl.BlockSpec((seq_count - 1, count, local_len, width), lambda i: (0, mb, 0, 0)),
                full((width, packed_width)),
                full((TOP, tokens)),
            ],
            out_specs=[full(s) for s, _ in outs],
            out_shape=[struct(s, k) for s, k in outs],
            scratch_shapes=[
                pltpu.VMEM((tokens, width), BF),
                pltpu.VMEM((local_len, LANES), F32),
            ],
            compiler_params=params(),
            name="forward",
        )(meta, lengths, images, others, packed, prow)

    def expert(buf, dyb, totals):
        first = totals is None
        cfg = (experts, room, capacity, width)
        wide = lambda: pl.BlockSpec((width, FF_BLOCK), lambda i: (0, i))
        thin = lambda: pl.BlockSpec((1, FF_BLOCK), lambda i: (0, i))
        in_specs = [
            smem_spec(),
            full((experts, room, width)),
            full((experts, room, width)),
            misc_spec,
            pl.BlockSpec((1, width, FF_BLOCK), lambda i: (0, 0, i)),
            thin(),
            pl.BlockSpec((1, FF_BLOCK, width), lambda i: (0, i, 0)),
            full((1, width)),
        ]
        total_specs = [wide(), wide(), thin(), full((1, width))]
        args = [meta, buf, dyb, packed, up_weight, up_bias, down_weight, down_bias]
        aliases = {}
        if not first:
            aliases = {len(args) + j: 2 + j for j in range(4)}
            in_specs += total_specs
            args += list(totals)
        outs = pl.pallas_call(
            functools.partial(expert_kernel, cfg, first),
            grid=(hidden // FF_BLOCK,),
            in_specs=in_specs,
            out_specs=[full((experts, room, width))] * 2 + total_specs,
            out_shape=[
                moved,
                moved,
                struct((width, hidden), F32),
                struct((width, hidden), F32),
                struct((1, hidden), F32),
                struct((1, width), F32),
            ],
            scratch_shapes=[
                pltpu.VMEM((slots, width), BF),
                pltpu.VMEM((width, slots), BF),
                pltpu.VMEM((slots, width), BF),
                pltpu.VMEM((width, slots), BF),
                pltpu.VMEM((slots, width), F32),
                pltpu.VMEM((slots, width), F32),
            ],
            input_output_aliases=aliases,
            compiler_params=params(),
            name="expert",
        )(*args)
        return outs[0], outs[1], tuple(outs[2:])

    def backward(mb, dback, pcol, saved, totals):
        first = totals is None
        cfg = (count, local_len, seq_count, width, experts, room, capacity)
        middle, gate, second, oT, q, k, v, lse, n1T = saved
        args = [
            meta,
            lengths,
            dback,
            pcol,
            gate,
            middle,
            second,
            cotangent,
            oT,
            packed,
            q,
            k,
            v,
            lse,
            n1T,
        ]
        in_specs = [smem_spec(), smem_spec()]
        in_specs += [token_spec(mb) if a is cotangent else full(a.shape) for a in args[2:]]
        aliases = {}
        if not first:
            aliases = {len(args) + j: 3 + j for j in range(2)}
            in_specs += [full(a.shape) for a in totals]
            args += list(totals)
        outs = [
            ((tokens, width), F32),
            ((seq_count - 1, tokens, width), BF),
            ((tokens, width), F32),
            ((width, 4 * width), F32),
            ((LANES, width), F32),
        ]
        return pl.pallas_call(
            functools.partial(backward_kernel, cfg, mb, first),
            grid=(1,),
            in_specs=in_specs,
            out_specs=[full(s) for s, _ in outs],
            out_shape=[struct(s, t) for s, t in outs],
            scratch_shapes=[
                pltpu.VMEM((tokens, width), BF),
                pltpu.VMEM((width, local_len), F32),
                pltpu.VMEM((full_len, 2 * width), BF),
            ],
            input_output_aliases=aliases,
            compiler_params=params(),
            name="backward",
        )(*args)

    def finish(mb, own, got, dm, mrow):
        cfg = (count, local_len, seq_count, width, experts)
        return pl.pallas_call(
            functools.partial(input_kernel, cfg),
            grid=(1,),
            in_specs=[
                full((tokens, width)),
                full((seq_count - 1, tokens, width)),
                token_spec(mb),
                full((tokens, width)),
                misc_spec,
                full((LANES, width)),
            ],
            out_specs=[full((count, local_len, width)), full((LANES, width))],
            out_shape=[struct((count, local_len, width), BF), struct((LANES, width), F32)],
            compiler_params=params(),
            name="finish",
        )(own, got, images, dm, packed, mrow)

    def mix(back, pcol, gate, middle):
        cfg = (count, local_len, width, experts, room)
        args = (back, pcol, gate, middle)
        return pl.pallas_call(
            functools.partial(mix_kernel, cfg),
            grid=(1,),
            in_specs=[full(a.shape) for a in args],
            out_specs=full((count, local_len, width)),
            out_shape=struct((count, local_len, width), BF),
            compiler_params=params(),
            name="mix",
        )(*args)

    placed = [place(mb) for mb in range(MICRO)]
    dyb = [exchange(p[0]) for p in placed]
    saved = []
    bufs = []
    for mb in range(MICRO):
        outs = forward(mb, placed[mb][1])
        bufs.append(exchange(outs[0]))
        saved.append(outs[1:])
    totals = None
    results = []
    dbacks = []
    for mb in range(MICRO):
        result, dback, totals = expert(bufs[mb], dyb[mb], totals)
        results.append(result)
        dbacks.append(exchange(dback))
    dense = None
    mrows = []
    grads = []
    for mb in range(MICRO):
        own, oth, dm, *dense = backward(mb, dbacks[mb], placed[mb][2], saved[mb], dense)
        got = jnp.stack(
            [
                lax.ppermute(
                    oth[j - 1], "seq", [(i, (i + j) % seq_count) for i in range(seq_count)]
                )
                for j in range(1, seq_count)
            ]
        )
        grad, dense[1] = finish(mb, own, got, dm, dense[1])
        grads.append(grad)
    out_blocks = []
    for mb in range(MICRO):
        back = exchange(results[mb])
        out_blocks.append(mix(back, placed[mb][2], saved[mb][1], saved[mb][0]))

    gup, gdn, gbias, gdbias = totals
    swap = [(i, (i + 1) % seq_count) for i in range(seq_count)]

    def seq_sum(value):
        if seq_count == 2:
            return value + lax.ppermute(value.astype(BF), "seq", swap).astype(F32)
        return lax.psum(value.astype(BF), "seq").astype(F32)

    if seq_count == 2:
        got_up = lax.ppermute(gup.astype(BF), "seq", swap)
        got_dn = lax.ppermute(gdn.astype(BF), "seq", swap)
        wide = lambda: pl.BlockSpec((width, FF_BLOCK), lambda i: (0, i))
        final_up, final_down = pl.pallas_call(
            sum_kernel,
            grid=(hidden // FF_BLOCK,),
            in_specs=[wide(), wide(), wide(), wide()],
            out_specs=[
                pl.BlockSpec((1, width, FF_BLOCK), lambda i: (0, 0, i)),
                pl.BlockSpec((1, FF_BLOCK, width), lambda i: (0, i, 0)),
            ],
            out_shape=[struct((1, width, hidden), F32), struct((1, hidden, width), F32)],
            compiler_params=params(),
            name="sum_experts",
        )(gup, gdn, got_up, got_dn)
    else:
        final_up = seq_sum(gup)[None]
        final_down = jnp.swapaxes(seq_sum(gdn), 0, 1)[None]
    biases = seq_sum(jnp.concatenate([gbias, gdbias], axis=1))
    final_up_shift = biases[:, :hidden]
    final_down_shift = biases[:, hidden:]

    grand = jnp.concatenate([dense[0], jnp.transpose(dense[1])], axis=1).astype(BF)
    shards = lax.psum_scatter(grand, "dp", scatter_dimension=0, tiled=True)
    shards = seq_sum(shards.astype(F32))
    misc = 4 * width + experts
    return (
        jnp.concatenate(out_blocks, axis=0),
        jnp.concatenate(grads, axis=0),
        shards[:, misc],
        shards[:, misc + 1],
        shards[:, : 3 * width],
        jnp.stack([shards[:, misc + 2], shards[:, misc + 3]]),
        shards[:, 3 * width : 4 * width],
        shards[:, misc + 4],
        shards[:, misc + 5],
        shards[:, misc + 6],
        shards[:, 4 * width : misc],
        final_up,
        final_up_shift,
        final_down,
        final_down_shift,
    )


def solution(mesh):
    return jax.shard_map(
        on_device,
        mesh=mesh,
        in_specs=(
            P("dp", "seq", None),
            P("dp", "seq", None),
            P("dp"),
            P("dp", None, "seq", None, None),
            P("dp"),
            P("dp"),
            P("dp", None),
            P(None, "dp"),
            P("dp", None),
            P("dp"),
            P("dp"),
            P("dp"),
            P("dp", None),
            P("dp", None, None),
            P("dp", None),
            P("dp", None, None),
            P("dp", None),
        ),
        out_specs=(
            P("dp", "seq", None),
            P("dp", "seq", None),
            P("dp"),
            P("dp"),
            P("dp", None),
            P(None, "dp"),
            P("dp", None),
            P("dp"),
            P("dp"),
            P("dp"),
            P("dp", None),
            P("dp", None, None),
            P("dp", None),
            P("dp", None, None),
            P("dp", None),
        ),
        check_vma=False,
    )
```

```python
import functools

import jax
import jax.numpy as jnp
from jax import lax
from jax.experimental import pallas as pl
from jax.experimental.pallas import tpu as pltpu
from jax.sharding import PartitionSpec as P

HD = 64
TOP = 2
MICRO = 3
BF = jnp.bfloat16
F32 = jnp.float32
EPS = 1e-06
LANES = 128
VEC = 8
FF_BLOCK = 512
VMEM_LIMIT = 60 * 1024 * 1024


def mm(left, right):
    return jnp.dot(left, right, preferred_element_type=F32)


def mm_nt(left, right):
    return lax.dot_general(
        left, right, (((1,), (1,)), ((), ())), preferred_element_type=F32
    )


def iota(shape, dim):
    return lax.broadcasted_iota(jnp.int32, shape, dim)


def norm_parts(values):
    average = jnp.mean(values, axis=-1, keepdims=True)
    centred = values - average
    spread = jnp.mean(centred * centred, axis=-1, keepdims=True)
    scale = lax.rsqrt(spread + EPS)
    return centred * scale, scale


def norm_pull(unit, scale, gain, cotangent):
    inner = cotangent * gain
    mean_inner = jnp.mean(inner, axis=-1, keepdims=True)
    mean_unit = jnp.mean(inner * unit, axis=-1, keepdims=True)
    return scale * (inner - mean_inner - unit * mean_unit)


def misc_rows(w_ref, start):
    return jnp.transpose(w_ref[:, start : start + LANES].astype(F32))


def pack_kernel(experts, qkv_ref, proj_ref, router_ref, vec_ref, out_ref):
    width = proj_ref.shape[1]
    shard = proj_ref.shape[0]
    out_ref[:, : 3 * width] = qkv_ref[...]
    out_ref[:, 3 * width : 4 * width] = proj_ref[...]
    columns = jnp.transpose(vec_ref[...].astype(F32))
    tail = jnp.zeros((shard, LANES - experts - columns.shape[1]), F32)
    out_ref[:, 4 * width :] = jnp.concatenate(
        [router_ref[...].astype(F32), columns, tail], axis=1
    ).astype(BF)


def place_kernel(experts, room, routes_ref, dy_ref, send_ref, prow_ref, pcol_ref):
    tokens = routes_ref.shape[3]
    slots = experts * room
    cols = routes_ref[0, 0, 0]
    wide = jnp.concatenate([cols.astype(F32), jnp.zeros((tokens, LANES - TOP), F32)], axis=1)
    across = jnp.transpose(wide)[0:8, :].astype(jnp.int32)
    first_row = across[0:1, :]
    second_row = across[1:2, :]
    hot_first = (iota((experts, tokens), 0) == first_row).astype(F32)
    hot_second = (iota((experts, tokens), 0) == second_row).astype(F32)
    earlier = (iota((tokens, tokens), 0) < iota((tokens, tokens), 1)).astype(BF)
    before = mm((hot_first + hot_second).astype(BF), earlier)
    in_first = jnp.sum(before * hot_first, axis=0, keepdims=True).astype(jnp.int32)
    in_second = jnp.sum((before + hot_first) * hot_second, axis=0, keepdims=True).astype(jnp.int32)
    place_first = first_row * room + in_first
    place_second = second_row * room + in_second
    prow_ref[0, 0:1, :] = place_first
    prow_ref[0, 1:2, :] = place_second
    slot_of = iota((slots, tokens), 0)
    hot = jnp.where((slot_of == place_first) | (slot_of == place_second), 1.0, 0.0).astype(BF)
    flat = dy_ref[...].reshape(tokens, dy_ref.shape[-1])
    rows = mm(hot, flat)
    for e in range(experts):
        send_ref[e] = rows[e * room : (e + 1) * room].astype(BF)
    first_col = cols[:, 0:1]
    second_col = cols[:, 1:2]
    hot_first = (iota((tokens, experts), 1) == first_col).astype(F32)
    hot_second = (iota((tokens, experts), 1) == second_col).astype(F32)
    later = (iota((tokens, tokens), 1) < iota((tokens, tokens), 0)).astype(BF)
    before = mm(later, (hot_first + hot_second).astype(BF))
    in_first = jnp.sum(before * hot_first, axis=1, keepdims=True).astype(jnp.int32)
    in_second = jnp.sum((before + hot_first) * hot_second, axis=1, keepdims=True).astype(jnp.int32)
    lane = iota((tokens, 8), 1)
    table = jnp.zeros((tokens, 8), jnp.int32)
    for at, col in enumerate(
        (
            first_col * room + in_first,
            second_col * room + in_second,
            first_col,
            second_col,
            in_first,
            in_second,
        )
    ):
        table = jnp.where(lane == at, col, table)
    pcol_ref[0] = table


def forward_kernel(
    cfg,
    mb,
    meta_ref,
    len_ref,
    own_ref,
    oth_ref,
    w_ref,
    prow_ref,
    send_ref,
    middle_ref,
    gate_ref,
    second_ref,
    oT_ref,
    q_ref,
    k_ref,
    v_ref,
    lse_ref,
    n1T_ref,
    att_ref,
    logs_ref,
):
    images, local_len, seq_count, width, experts, room = cfg
    full_len = local_len * seq_count
    tokens = images * local_len
    slots = experts * room
    misc_at = 4 * width
    rows = misc_rows(w_ref, misc_at)

    def vec(j):
        return rows[experts + j : experts + j + 1, :]

    here = meta_ref[1]
    lane = iota((1, LANES), 1)
    low_half = (lane < HD).astype(BF)
    high_half = (lane >= HD).astype(BF)
    for b in range(images):
        blocks = [own_ref[b]] + [oth_ref[j, b] for j in range(seq_count - 1)]
        full = jnp.concatenate(blocks, axis=0).astype(F32)
        unit, _ = norm_parts(full)
        normed = (unit * vec(0) + vec(1)).astype(BF)
        n1T_ref[:, b * full_len : (b + 1) * full_len] = jnp.transpose(normed)
        span = slice(b * local_len, (b + 1) * local_len)
        wide = slice(b * full_len, (b + 1) * full_len)
        queries = (mm(normed[:local_len], w_ref[:, :width]) + vec(2)).astype(BF)
        q_ref[span, :] = queries * jnp.asarray(HD**-0.5, BF)
        k_ref[wide, :] = mm(normed, w_ref[:, width : 2 * width]).astype(BF)
        v_ref[wide, :] = (mm(normed, w_ref[:, 2 * width : 3 * width]) + vec(3)).astype(BF)
        kpos = iota((1, full_len), 1)
        shift = jnp.zeros((1, full_len), jnp.int32)
        for j in range(seq_count):
            origin = lax.rem(here + j, seq_count) * local_len - j * local_len
            shift = jnp.where(kpos >= j * local_len, origin, shift)
        valid = (kpos + shift) < len_ref[mb * images + b]
        logs_ref[...] = jnp.zeros_like(logs_ref)

        def heads(blk, carry):
            at = pl.ds(pl.multiple_of(blk * LANES, LANES), LANES)
            q_blk = q_ref[span, at]
            k_blk = k_ref[wide, at]
            v_blk = v_ref[wide, at]
            outs = []
            for side, keep in enumerate((low_half, high_half)):
                scores = mm_nt(q_blk * keep, k_blk)
                scores = jnp.where(valid, scores, -1e30)
                highest = jnp.max(scores, axis=1, keepdims=True)
                powers = jnp.exp(scores - highest)
                total = jnp.sum(powers, axis=1, keepdims=True)
                probs = (powers * (1.0 / total)).astype(BF)
                outs.append(mm(probs, v_blk))
                logs_ref[...] = jnp.where(
                    lane == 2 * blk + side, highest + jnp.log(total), logs_ref[...]
                )
            att_ref[span, at] = jnp.where(lane < HD, outs[0], outs[1]).astype(BF)
            return carry

        lax.fori_loop(0, width // LANES, heads, 0)
        lse_ref[b * 8 : b * 8 + 8, :] = jnp.transpose(logs_ref[...])[0:8, :]
    attended = att_ref[...]
    oT_ref[...] = jnp.transpose(attended)
    branch = mm(attended, w_ref[:, 3 * width : 4 * width]) + vec(4)
    middle = own_ref[...].reshape(tokens, width).astype(F32) + branch
    middle_ref[...] = middle
    unit, _ = norm_parts(middle)
    second = (unit * vec(5) + vec(6)).astype(BF)
    second_ref[...] = second
    gate_ref[...] = gates(mm(second, w_ref[:, misc_at : misc_at + LANES]), experts)
    slot_of = iota((slots, tokens), 0)
    hot = jnp.where(
        (slot_of == prow_ref[0, 0:1, :]) | (slot_of == prow_ref[0, 1:2, :]), 1.0, 0.0
    ).astype(BF)
    sent = mm(hot, second)
    for e in range(experts):
        send_ref[e] = sent[e * room : (e + 1) * room].astype(BF)


def gates(logits, experts):
    real = iota((1, LANES), 1) < experts
    logits = jnp.where(real, logits, -1e30)
    powers = jnp.where(real, jnp.exp(logits - jnp.max(logits, axis=1, keepdims=True)), 0.0)
    return powers / jnp.sum(powers, axis=1, keepdims=True)


def expert_kernel(cfg, first, last, *refs):
    groups, room, capacity, width = cfg
    meta_ref, buf_ref, dyb_ref, wm_ref, up_ref, ub_ref, down_ref, db_ref = refs[:8]
    refs = refs[8:]
    if not first:
        _, gup_in, gdn_in, gb_in, gdb_in = refs[:5]
        refs = refs[5:]
    r_ref, dbuf_ref, gup_ref, gdn_ref, gb_ref, gdb_ref = refs[:6]
    refs = refs[6:]
    if last:
        lows = refs[:4]
        refs = refs[4:]
    (
        flat_s,
        flatT_s,
        dr_s,
        drT_s,
        racc_s,
        dacc_s,
    ) = refs
    slots = groups * room
    step = pl.program_id(0)
    experts = groups

    @pl.when(step == 0)
    def _():
        flat = buf_ref[...].astype(F32).reshape(slots, width).astype(BF)
        flat_s[...] = flat
        flatT_s[...] = jnp.transpose(flat)
        gate = gates(mm(flat, wm_ref[...]), experts)
        mine = iota((1, LANES), 1) == meta_ref[0]
        mine_gate = jnp.sum(jnp.where(mine, gate, 0.0), axis=1, keepdims=True)
        dr = (dyb_ref[...].astype(F32).reshape(slots, width) * mine_gate).astype(BF)
        dr_s[...] = dr
        drT_s[...] = jnp.transpose(dr)
        shift_sum = jnp.sum(dr.astype(F32), axis=0, keepdims=True)
        gdb_ref[...] = shift_sum if first else gdb_in[...] + shift_sum
        racc_s[...] = jnp.zeros_like(racc_s)
        dacc_s[...] = jnp.zeros_like(dacc_s)

    flat = flat_s[...]
    dr = dr_s[...]
    hidden = mm(flat, up_ref[0]) + ub_ref[...].astype(F32)
    half_erf = 0.5 * lax.erf(hidden * (0.5**0.5)) + 0.5
    active = (hidden * half_erf).astype(BF)
    slope = half_erf + hidden * (jnp.exp(-0.5 * hidden * hidden) * 0.3989422804014327)
    racc_s[...] += mm(active, down_ref[0])
    grad_pre = mm_nt(dr, down_ref[0]) * slope
    low_pre = grad_pre.astype(BF)
    dacc_s[...] += mm_nt(low_pre, up_ref[0])
    gup = mm(flatT_s[...], low_pre)
    gdn = mm(drT_s[...], active)
    gbias = jnp.sum(low_pre.astype(F32), axis=0, keepdims=True)
    if not first:
        gup = gup_in[...] + gup
        gdn = gdn_in[...] + gdn
        gbias = gb_in[...] + gbias
    gup_ref[...] = gup
    gdn_ref[...] = gdn
    gb_ref[...] = gbias
    if last:
        early = step < pl.num_programs(0) // 2

        @pl.when(early)
        def _():
            lows[0][...] = gup.astype(BF)
            lows[2][...] = gdn.astype(BF)

        @pl.when(jnp.logical_not(early))
        def _():
            lows[1][...] = gup.astype(BF)
            lows[3][...] = gdn.astype(BF)

    @pl.when(step == pl.num_programs(0) - 1)
    def _():
        result = (racc_s[...] + db_ref[...].astype(F32)).astype(BF)
        for e in range(groups):
            r_ref[e] = result[e * room : (e + 1) * room]
        dy = dyb_ref[...].astype(F32).reshape(slots, width)
        dgate = jnp.sum(dy * result.astype(F32), axis=1, keepdims=True).reshape(groups, room, 1)
        spread = jnp.where(
            iota((groups, room, LANES), 2) == iota((groups, room, LANES), 1), dgate, 0.0
        )
        as_row = jnp.sum(spread, axis=1, keepdims=True)
        high = as_row.astype(BF).astype(F32)
        tail = jnp.zeros((groups, 1, width - 2 * LANES), F32)
        as_row = jnp.concatenate([high, as_row - high, tail], axis=2)
        back = dacc_s[...].reshape(groups, room, width)
        back = jnp.where(iota((groups, room, 1), 1) == capacity, as_row, back).astype(BF)
        for e in range(groups):
            dbuf_ref[e] = back[e]


def backward_kernel(cfg, mb, first, last, *refs):
    images, local_len, seq_count, width, experts, room, capacity = cfg
    (
        meta_ref,
        len_ref,
        dback_ref,
        pcol_ref,
        gate_ref,
        middle_ref,
        second_ref,
        dy_ref,
        oT_ref,
        w_ref,
        q_ref,
        k_ref,
        v_ref,
        lse_ref,
        n1T_ref,
        own_ref,
        oth_ref,
    ) = refs[:17]
    refs = refs[17:]
    if not first:
        g_in, mrow_in = refs[:2]
        refs = refs[2:]
    down_own, down_oth, dm_ref = refs[:3]
    refs = refs[3:]
    if last:
        low_ref = refs[0]
        refs = refs[1:]
    else:
        g_ref = refs[0]
        refs = refs[1:]
    mrow_ref, do_s, dqT_s, dkv_s = refs

    def add_dense(at, value):
        if not first:
            value = g_in[:, at] + value
        if last:
            low_ref[:, at] = value.astype(BF)
        else:
            g_ref[:, at] = value

    full_len = local_len * seq_count
    tokens = images * local_len
    slots = experts * room
    misc_at = 4 * width
    rows = misc_rows(w_ref, misc_at)
    here = meta_ref[1]

    def vec(j):
        return rows[experts + j : experts + j + 1, :]

    dback = dback_ref[...].astype(F32)
    back_rows = dback.reshape(slots, width).astype(BF)
    slot_of = iota((tokens, slots), 1)
    hot = jnp.where(
        (slot_of == pcol_ref[0, :, 0:1]) | (slot_of == pcol_ref[0, :, 1:2]), 1.0, 0.0
    ).astype(BF)
    from_experts = mm(hot, back_rows)
    spare = jnp.where(iota((experts, room, 1), 1) == capacity, dback[:, :, : 2 * LANES], 0.0)
    spare = jnp.sum(spare, axis=1)
    spare = jnp.concatenate(
        [spare, jnp.zeros((LANES - experts, 2 * LANES), F32)], axis=0
    ).astype(BF)
    lane = iota((tokens, LANES), 1)
    pulled = jnp.zeros((tokens, LANES), F32)
    for k in range(TOP):
        within = jnp.where(lane == pcol_ref[0, :, 4 + k : 5 + k], 1.0, 0.0).astype(BF)
        found = mm_nt(jnp.concatenate([within, within], axis=1), spare)
        pulled = pulled + jnp.where(lane == pcol_ref[0, :, 2 + k : 3 + k], found, 0.0)
    gate = gate_ref[...]
    dlogit = gate * (pulled - jnp.sum(gate * pulled, axis=1, keepdims=True))
    dlogit_low = dlogit.astype(BF)
    mrow_ref[...] = mm(jnp.transpose(dlogit_low.astype(F32)).astype(BF), second_ref[...])
    dn2 = from_experts + mm_nt(dlogit_low, w_ref[:, misc_at : misc_at + LANES])
    unit, scale = norm_parts(middle_ref[...])
    dy = dy_ref[...].reshape(tokens, width).astype(F32)
    dm = dy + norm_pull(unit, scale, vec(5), dn2)
    dm_ref[...] = dm
    da = dm.astype(BF)
    gproj = mm(oT_ref[...], da)
    proj = slice(3 * width, 4 * width)
    add_dense(proj, gproj)
    do_s[...] = mm_nt(da, w_ref[:, proj]).astype(BF)
    half_lane = iota((1, LANES), 1)
    low_half = (half_lane < HD).astype(BF)
    high_half = (half_lane >= HD).astype(BF)
    gqkv = [None, None]
    bias_q = jnp.zeros((1, width), F32)
    bias_v = jnp.zeros((1, width), F32)
    gain_sum = jnp.zeros((1, width), F32)
    shift_sum = jnp.zeros((1, width), F32)
    for b in range(images):
        span = slice(b * local_len, (b + 1) * local_len)
        wide = slice(b * full_len, (b + 1) * full_len)
        kpos = iota((full_len, 1), 0)
        shift = jnp.zeros((full_len, 1), jnp.int32)
        for j in range(seq_count):
            origin = lax.rem(here + j, seq_count) * local_len - j * local_len
            shift = jnp.where(kpos >= j * local_len, origin, shift)
        valid = (kpos + shift) < len_ref[mb * images + b]

        def heads(blk, carry):
            at = pl.ds(pl.multiple_of(blk * LANES, LANES), LANES)
            q_blk = q_ref[span, at]
            k_blk = k_ref[wide, at]
            v_blk = v_ref[wide, at]
            do_blk = do_s[span, at]
            kT_blk = jnp.transpose(k_blk)
            dvs = []
            dks = []
            dqs = []
            for side, keep in enumerate((low_half, high_half)):
                scores = mm_nt(k_blk, q_blk * keep)
                logs = lse_ref[pl.ds(b * 8 + 2 * blk + side, 1), :]
                probs = jnp.where(valid, jnp.exp(scores - logs), 0.0)
                dprobs = mm_nt(v_blk, do_blk * keep)
                inner = jnp.sum(probs * dprobs, axis=0, keepdims=True)
                dscores = (probs * (dprobs - inner)).astype(BF)
                dvs.append(mm(probs.astype(BF), do_blk))
                dks.append(mm(dscores, q_blk))
                dqs.append(mm(kT_blk[side * HD : (side + 1) * HD], dscores))
            dqT_s[pl.ds(pl.multiple_of(blk * LANES, LANES), HD), :] = dqs[0]
            dqT_s[pl.ds(pl.multiple_of(blk * LANES + HD, HD), HD), :] = dqs[1]
            left = half_lane < HD
            dkv_s[:, at] = jnp.where(left, dks[0], dks[1]).astype(BF)
            vat = pl.ds(pl.multiple_of(width + blk * LANES, LANES), LANES)
            dkv_s[:, vat] = jnp.where(left, dvs[0], dvs[1]).astype(BF)
            return carry

        lax.fori_loop(0, width // LANES, heads, 0)
        dq = (jnp.transpose(dqT_s[...]) * HD**-0.5).astype(BF)
        dkv = dkv_s[...]
        part_q = mm(n1T_ref[:, b * full_len : b * full_len + local_len], dq)
        part_kv = mm(n1T_ref[:, wide], dkv)
        gqkv[0] = part_q if b == 0 else gqkv[0] + part_q
        gqkv[1] = part_kv if b == 0 else gqkv[1] + part_kv
        bias_q = bias_q + jnp.sum(dq.astype(F32), axis=0, keepdims=True)
        bias_v = bias_v + jnp.sum(dkv[:, width:].astype(F32), axis=0, keepdims=True)
        down = mm_nt(dkv, w_ref[:, width : 3 * width])
        down_own[span, :] = mm_nt(dq, w_ref[:, :width])
        down_own[span, :] += down[:local_len]
        for j in range(seq_count):
            part = down_own[span, :] if j == 0 else down[j * local_len : (j + 1) * local_len]
            tokens_in = own_ref[b] if j == 0 else oth_ref[j - 1, b]
            first_unit, _ = norm_parts(tokens_in.astype(F32))
            gain_sum = gain_sum + jnp.sum(part * first_unit, axis=0, keepdims=True)
            shift_sum = shift_sum + jnp.sum(part, axis=0, keepdims=True)
            if j > 0:
                down_oth[j - 1, span, :] = part.astype(BF)
    add_dense(slice(0, width), gqkv[0])
    add_dense(slice(width, 3 * width), gqkv[1])
    row = iota((LANES, 1), 0)
    mrow = jnp.where(row < experts, mrow_ref[...], 0.0)
    sums = (
        gain_sum,
        shift_sum,
        bias_q,
        bias_v,
        jnp.sum(da.astype(F32), axis=0, keepdims=True),
        jnp.sum(dn2 * unit, axis=0, keepdims=True),
        jnp.sum(dn2, axis=0, keepdims=True),
    )
    for j, value in enumerate(sums):
        mrow = jnp.where(row == experts + j, value, mrow)
    if not first:
        mrow = mrow_in[...] + mrow
    mrow_ref[...] = mrow
    if last:
        low_ref[:, misc_at : misc_at + LANES] = jnp.transpose(mrow).astype(BF)


def input_kernel(cfg, own_ref, got_ref, x_ref, dm_ref, wm_ref, *refs):
    out_ref = refs[-1]
    images, local_len, seq_count, width, experts = cfg
    tokens = images * local_len
    rows = jnp.transpose(wm_ref[...].astype(F32))
    dn1 = own_ref[...]
    for j in range(seq_count - 1):
        dn1 = dn1 + got_ref[j].astype(F32)
    unit, scale = norm_parts(x_ref[...].reshape(tokens, width).astype(F32))
    grad = dm_ref[...] + norm_pull(unit, scale, rows[experts : experts + 1, :], dn1)
    out_ref[...] = grad.astype(BF).reshape(images, local_len, width)


def mix_kernel(cfg, back_ref, pcol_ref, gate_ref, middle_ref, *refs):
    out_ref = refs[-1]
    images, local_len, width, experts, room = cfg
    tokens = images * local_len
    slots = experts * room
    back = back_ref[...].astype(F32).reshape(slots, width).astype(BF)
    slot_of = iota((tokens, slots), 1)
    lane = iota((tokens, LANES), 1)
    gate = gate_ref[...]
    total = middle_ref[...]
    for k in range(TOP):
        hot = jnp.where(slot_of == pcol_ref[0, :, k : k + 1], 1.0, 0.0).astype(BF)
        chosen = jnp.where(lane == pcol_ref[0, :, 2 + k : 3 + k], gate, 0.0)
        total = total + jnp.sum(chosen, axis=1, keepdims=True) * mm(hot, back)
    out_ref[...] = total.astype(BF).reshape(images, local_len, width)


def sum_kernel(gup_ref, gdn_ref, up_early, up_late, dn_early, dn_late, up_ref, dn_ref):
    late = pl.program_id(0) >= pl.num_programs(0) // 2
    got_up = jnp.where(late, up_late[...], up_early[...])
    got_dn = jnp.where(late, dn_late[...], dn_early[...])
    up_ref[0] = gup_ref[...] + got_up.astype(F32)
    dn_ref[0] = jnp.transpose(gdn_ref[...] + got_dn.astype(F32))


def smem_spec():
    return pl.BlockSpec(memory_space=pltpu.SMEM)


def params():
    return pltpu.CompilerParams(vmem_limit_bytes=VMEM_LIMIT)


def cost(micros):
    return pl.CostEstimate(
        flops=int(micros * 1e9), transcendentals=0, bytes_accessed=int(micros * 2e6)
    )


def struct(shape, kind):
    return jax.ShapeDtypeStruct(shape, kind)


def after(value, *others):
    return lax.optimization_barrier((value, *others))[0]


def on_device(
    images,
    cotangent,
    lengths,
    routes,
    attn_norm_gain,
    attn_norm_bias,
    qkv_weight,
    query_value_bias,
    proj_weight,
    proj_bias,
    moe_norm_gain,
    moe_norm_bias,
    router_weight,
    up_weight,
    up_bias,
    down_weight,
    down_bias,
):
    seq_count = lax.axis_size("seq")
    dp_count = lax.axis_size("dp")
    count = images.shape[0] // MICRO
    local_len = images.shape[1]
    width = images.shape[2]
    tokens = count * local_len
    full_len = local_len * seq_count
    experts = router_weight.shape[1]
    hidden = up_weight.shape[2]
    capacity = (5 * tokens * TOP + 4 * experts - 1) // (4 * experts)
    room = (capacity + 1 + 7) // 8 * 8
    slots = experts * room
    assert up_weight.shape[0] == 1 and experts == dp_count
    assert experts + VEC <= LANES and capacity <= LANES
    meta = jnp.stack([lax.axis_index("dp"), lax.axis_index("seq")]).astype(jnp.int32)
    packed_width = 4 * width + LANES

    def full(shape):
        return pl.BlockSpec(shape, lambda i: (0,) * len(shape))

    def token_spec(mb):
        return pl.BlockSpec((count, local_len, width), lambda i: (mb, 0, 0))

    def table_spec(mb, shape):
        return pl.BlockSpec((1, *shape), lambda i: (mb, 0, 0))

    def block_spec(mb):
        return pl.BlockSpec((experts, room, width), lambda i: (0, mb, 0))

    any_spec = pl.BlockSpec(memory_space=pl.ANY)
    other_spec = lambda mb: pl.BlockSpec(
        (seq_count - 1, count, local_len, width), lambda i: (0, mb, 0, 0)
    )
    halved = hidden // FF_BLOCK // 2
    early_spec = lambda: pl.BlockSpec(
        (width, FF_BLOCK), lambda i: (0, jnp.minimum(i, halved - 1))
    )
    late_spec = lambda: pl.BlockSpec(
        (width, FF_BLOCK), lambda i: (0, jnp.maximum(i - halved, 0))
    )
    misc_spec = pl.BlockSpec((width, LANES), lambda i: (0, 4 * width // LANES))
    moved = struct((experts, room, width), BF)
    merged = struct((experts, MICRO * room, width), BF)

    others = jnp.stack(
        [
            lax.ppermute(
                images, "seq", [((i + j) % seq_count, i) for i in range(seq_count)]
            )
            for j in range(1, seq_count)
        ]
    )
    vectors = jnp.concatenate(
        [
            jnp.stack([attn_norm_gain, attn_norm_bias]),
            query_value_bias,
            jnp.stack([proj_bias, moe_norm_gain, moe_norm_bias, jnp.zeros_like(proj_bias)]),
        ],
        axis=0,
    )
    shard = router_weight.shape[0]
    pack_args = (qkv_weight, proj_weight, router_weight, vectors)
    packed_shard = pl.pallas_call(
        functools.partial(pack_kernel, experts),
        grid=(1,),
        in_specs=[full(a.shape) for a in pack_args],
        out_specs=full((shard, packed_width)),
        out_shape=struct((shard, packed_width), BF),
        compiler_params=params(),
        cost_estimate=cost(1),
        name="pack",
    )(*pack_args)
    packed = lax.all_gather(packed_shard, "dp", axis=0, tiled=True)

    def exchange(array):
        return lax.all_to_all(array, "dp", split_axis=0, concat_axis=0, tiled=True)

    sent_dy, prow, pcol = pl.pallas_call(
        functools.partial(place_kernel, experts, room),
        grid=(MICRO,),
        in_specs=[
            pl.BlockSpec((1, 1, 1, tokens, TOP), lambda i: (0, i, 0, 0, 0)),
            pl.BlockSpec((count, local_len, width), lambda i: (i, 0, 0)),
        ],
        out_specs=[
            pl.BlockSpec((experts, room, width), lambda i: (0, i, 0)),
            pl.BlockSpec((1, TOP, tokens), lambda i: (i, 0, 0)),
            pl.BlockSpec((1, tokens, 8), lambda i: (i, 0, 0)),
        ],
        out_shape=[
            merged,
            struct((MICRO, TOP, tokens), jnp.int32),
            struct((MICRO, tokens, 8), jnp.int32),
        ],
        compiler_params=params(),
        cost_estimate=cost(8),
        name="place",
    )(after(routes, packed_shard), cotangent)

    def forward(mb):
        cfg = (count, local_len, seq_count, width, experts, room)
        outs = [
            ((experts, room, width), BF),
            ((tokens, width), F32),
            ((tokens, LANES), F32),
            ((tokens, width), BF),
            ((width, tokens), BF),
            ((tokens, width), BF),
            ((count * full_len, width), BF),
            ((count * full_len, width), BF),
            ((count * 8, local_len), F32),
            ((width, count * full_len), BF),
        ]
        return pl.pallas_call(
            functools.partial(forward_kernel, cfg, mb),
            grid=(1,),
            in_specs=[
                smem_spec(),
                smem_spec(),
                token_spec(mb),
                other_spec(mb),
                full((width, packed_width)),
                table_spec(mb, (TOP, tokens)),
            ],
            out_specs=[full(s) for s, _ in outs],
            out_shape=[struct(s, k) for s, k in outs],
            scratch_shapes=[
                pltpu.VMEM((tokens, width), BF),
                pltpu.VMEM((local_len, LANES), F32),
            ],
            compiler_params=params(),
            cost_estimate=cost(11),
            name="forward",
        )(meta, lengths, images, others, packed, prow)

    def expert(mb, buf, results, totals):
        first = mb == 0
        last = mb == MICRO - 1
        cfg = (experts, room, capacity, width)
        wide = lambda: pl.BlockSpec((width, FF_BLOCK), lambda i: (0, i))
        thin = lambda: pl.BlockSpec((1, FF_BLOCK), lambda i: (0, i))
        in_specs = [
            smem_spec(),
            full((experts, room, width)),
            block_spec(mb),
            misc_spec,
            pl.BlockSpec((1, width, FF_BLOCK), lambda i: (0, 0, i)),
            thin(),
            pl.BlockSpec((1, FF_BLOCK, width), lambda i: (0, i, 0)),
            full((1, width)),
        ]
        total_specs = [wide(), wide(), thin(), full((1, width))]
        args = [meta, buf, dyb, packed, up_weight, up_bias, down_weight, down_bias]
        aliases = {}
        if not first:
            aliases = {len(args): 0}
            aliases.update({len(args) + 1 + j: 2 + j for j in range(4)})
            in_specs += [any_spec, *total_specs]
            args += [results, *totals]
        outs = pl.pallas_call(
            functools.partial(expert_kernel, cfg, first, last),
            grid=(hidden // FF_BLOCK,),
            in_specs=in_specs,
            out_specs=[block_spec(mb), full((experts, room, width)), *total_specs]
            + ([early_spec(), late_spec()] * 2 if last else []),
            out_shape=[
                merged,
                moved,
                struct((width, hidden), F32),
                struct((width, hidden), F32),
                struct((1, hidden), F32),
                struct((1, width), F32),
            ]
            + ([struct((width, hidden // 2), BF)] * 4 if last else []),
            scratch_shapes=[
                pltpu.VMEM((slots, width), BF),
                pltpu.VMEM((width, slots), BF),
                pltpu.VMEM((slots, width), BF),
                pltpu.VMEM((width, slots), BF),
                pltpu.VMEM((slots, width), F32),
                pltpu.VMEM((slots, width), F32),
            ],
            input_output_aliases=aliases,
            compiler_params=params(),
            cost_estimate=cost(19),
            name="expert",
        )(*args)
        return outs[0], outs[1], tuple(outs[2:])

    def backward(mb, dback, saved, totals):
        first = mb == 0
        last = mb == MICRO - 1
        cfg = (count, local_len, seq_count, width, experts, room, capacity)
        middle, gate, second, oT, q, k, v, lse, n1T = saved
        whole = [gate, middle, second]
        heads = [oT, packed, q, k, v, lse, n1T]
        args = [meta, lengths, dback, pcol, *whole, cotangent, *heads, images, others]
        in_specs = [
            smem_spec(),
            smem_spec(),
            full(dback.shape),
            table_spec(mb, (tokens, 8)),
            *[full(a.shape) for a in whole],
            token_spec(mb),
            *[full(a.shape) for a in heads],
            token_spec(mb),
            other_spec(mb),
        ]
        aliases = {}
        if not first:
            in_specs += [full(a.shape) for a in totals]
            args += list(totals)
            if not last:
                aliases = {len(args) - 2: 3, len(args) - 1: 4}
        outs = [
            ((tokens, width), F32),
            ((seq_count - 1, tokens, width), BF),
            ((tokens, width), F32),
            ((width, packed_width), BF) if last else ((width, 4 * width), F32),
            ((LANES, width), F32),
        ]
        return pl.pallas_call(
            functools.partial(backward_kernel, cfg, mb, first, last),
            grid=(1,),
            in_specs=in_specs,
            out_specs=[full(s) for s, _ in outs],
            out_shape=[struct(s, t) for s, t in outs],
            scratch_shapes=[
                pltpu.VMEM((tokens, width), BF),
                pltpu.VMEM((width, local_len), F32),
                pltpu.VMEM((full_len, 2 * width), BF),
            ],
            input_output_aliases=aliases,
            compiler_params=params(),
            cost_estimate=cost(17),
            name="backward",
        )(*args)

    def into(kernel, mb, args, specs, previous, micros, name):
        aliases = {}
        if previous is not None:
            aliases = {len(args): 0}
            args = [*args, previous]
            specs = [*specs, any_spec]
        return pl.pallas_call(
            kernel,
            grid=(1,),
            in_specs=specs,
            out_specs=token_spec(mb),
            out_shape=struct(images.shape, BF),
            input_output_aliases=aliases,
            compiler_params=params(),
            cost_estimate=cost(micros),
            name=name,
        )(*args)

    def finish(mb, own, got, dm, previous):
        cfg = (count, local_len, seq_count, width, experts)
        specs = [full(own.shape), full(got.shape), token_spec(mb), full(dm.shape), misc_spec]
        return into(
            functools.partial(input_kernel, cfg),
            mb,
            [own, got, images, dm, packed],
            specs,
            previous,
            3,
            "finish",
        )

    def mix(mb, back, gate, middle, previous):
        cfg = (count, local_len, width, experts, room)
        specs = [
            block_spec(mb),
            table_spec(mb, (tokens, 8)),
            full(gate.shape),
            full(middle.shape),
        ]
        return into(
            functools.partial(mix_kernel, cfg),
            mb,
            [back, pcol, gate, middle],
            specs,
            previous,
            3,
            "mix",
        )

    swap = [(i, (i + 1) % seq_count) for i in range(seq_count)]

    def seq_sum(value):
        if seq_count == 2:
            return value + lax.ppermute(value.astype(BF), "seq", swap).astype(F32)
        return lax.psum(value.astype(BF), "seq").astype(F32)

    dyb = exchange(sent_dy)
    saved = []
    bufs = []
    for mb in range(MICRO):
        outs = forward(mb)
        bufs.append(exchange(outs[0]))
        saved.append(outs[1:])
    totals = None
    results = None
    ready = []
    for mb in range(MICRO):
        results, dback, totals = expert(mb, bufs[mb], results, totals)
        ready.append(dback)
    gup, gdn, gbias, gdbias, *pieces = totals
    arrived = []
    if seq_count == 2:
        arrived = [lax.ppermute(piece, "seq", swap) for piece in pieces]
    dense = None
    grads = None
    owns = []
    for mb in range(MICRO):
        sent = ready[mb]
        if mb == 1:
            sent = after(sent, ready[MICRO - 1])
        if mb >= 2:
            sent = after(sent, owns[mb - 2])
        dback = exchange(sent)
        if arrived and mb >= 1:
            dback, arrived[mb - 1] = lax.optimization_barrier((dback, arrived[mb - 1]))
        if mb == MICRO - 1:
            results = after(results, owns[mb - 1])
        own, oth, dm, *dense = backward(mb, dback, saved[mb], dense)
        owns.append(own)
        got = jnp.stack(
            [
                lax.ppermute(
                    oth[j - 1], "seq", [(i, (i + j) % seq_count) for i in range(seq_count)]
                )
                for j in range(1, seq_count)
            ]
        )
        if arrived and mb == MICRO - 1:
            got, arrived[2] = lax.optimization_barrier((got, arrived[2]))
        grads = finish(mb, own, got, dm, grads)
    shards = lax.psum_scatter(dense[0], "dp", scatter_dimension=0, tiled=True)
    back = exchange(after(results, dback))
    out = None
    for mb in range(MICRO):
        out = mix(mb, back, saved[mb][1], saved[mb][0], out)

    if seq_count == 2:
        wide = lambda: pl.BlockSpec((width, FF_BLOCK), lambda i: (0, i))
        final_up, final_down = pl.pallas_call(
            sum_kernel,
            grid=(hidden // FF_BLOCK,),
            in_specs=[wide(), wide(), *[early_spec(), late_spec()] * 2],
            out_specs=[
                pl.BlockSpec((1, width, FF_BLOCK), lambda i: (0, 0, i)),
                pl.BlockSpec((1, FF_BLOCK, width), lambda i: (0, i, 0)),
            ],
            out_shape=[struct((1, width, hidden), F32), struct((1, hidden, width), F32)],
            compiler_params=params(),
            cost_estimate=cost(8),
            name="sum_experts",
        )(gup, gdn, *arrived)
    else:
        sums = [lax.psum(piece, "seq").astype(F32) for piece in pieces]
        final_up = jnp.concatenate(sums[:2], axis=1)[None]
        final_down = jnp.swapaxes(jnp.concatenate(sums[2:], axis=1), 0, 1)[None]
    biases = seq_sum(jnp.concatenate([gbias, gdbias], axis=1))
    final_up_shift = biases[:, :hidden]
    final_down_shift = biases[:, hidden:]

    shards = seq_sum(shards.astype(F32))
    misc = 4 * width + experts
    return (
        out,
        grads,
        shards[:, misc],
        shards[:, misc + 1],
        shards[:, : 3 * width],
        jnp.stack([shards[:, misc + 2], shards[:, misc + 3]]),
        shards[:, 3 * width : 4 * width],
        shards[:, misc + 4],
        shards[:, misc + 5],
        shards[:, misc + 6],
        shards[:, 4 * width : misc],
        final_up,
        final_up_shift,
        final_down,
        final_down_shift,
    )


def solution(mesh):
    return jax.shard_map(
        on_device,
        mesh=mesh,
        in_specs=(
            P("dp", "seq", None),
            P("dp", "seq", None),
            P("dp"),
            P("dp", None, "seq", None, None),
            P("dp"),
            P("dp"),
            P("dp", None),
            P(None, "dp"),
            P("dp", None),
            P("dp"),
            P("dp"),
            P("dp"),
            P("dp", None),
            P("dp", None, None),
            P("dp", None),
            P("dp", None, None),
            P("dp", None),
        ),
        out_specs=(
            P("dp", "seq", None),
            P("dp", "seq", None),
            P("dp"),
            P("dp"),
            P("dp", None),
            P(None, "dp"),
            P("dp", None),
            P("dp"),
            P("dp"),
            P("dp"),
            P("dp", None),
            P("dp", None, None),
            P("dp", None),
            P("dp", None, None),
            P("dp", None),
        ),
        check_vma=False,
    )
```

```python
import functools

import jax
import jax.numpy as jnp
from jax import lax
from jax.experimental import pallas as pl
from jax.experimental.pallas import tpu as pltpu
from jax.sharding import PartitionSpec as P

HD = 64
TOP = 2
MICRO = 3
BF = jnp.bfloat16
F32 = jnp.float32
EPS = 1e-06
LANES = 128
VEC = 8
FF_BLOCK = 512
VMEM_LIMIT = 60 * 1024 * 1024


def mm(left, right):
    return jnp.dot(left, right, preferred_element_type=F32)


def mm_nt(left, right):
    return lax.dot_general(
        left, right, (((1,), (1,)), ((), ())), preferred_element_type=F32
    )


def iota(shape, dim):
    return lax.broadcasted_iota(jnp.int32, shape, dim)


def norm_parts(values):
    average = jnp.mean(values, axis=-1, keepdims=True)
    centred = values - average
    spread = jnp.mean(centred * centred, axis=-1, keepdims=True)
    scale = lax.rsqrt(spread + EPS)
    return centred * scale, scale


def norm_pull(unit, scale, gain, cotangent):
    inner = cotangent * gain
    mean_inner = jnp.mean(inner, axis=-1, keepdims=True)
    mean_unit = jnp.mean(inner * unit, axis=-1, keepdims=True)
    return scale * (inner - mean_inner - unit * mean_unit)


def misc_rows(w_ref, start):
    return jnp.transpose(w_ref[:, start : start + LANES].astype(F32))


def pack_kernel(experts, qkv_ref, proj_ref, router_ref, vec_ref, out_ref):
    width = proj_ref.shape[1]
    shard = proj_ref.shape[0]
    out_ref[:, : 3 * width] = qkv_ref[...]
    out_ref[:, 3 * width : 4 * width] = proj_ref[...]
    rows = jnp.concatenate([router_ref[...].astype(F32), vec_ref[...].astype(F32)], axis=0)
    columns = jnp.transpose(rows)
    tail = jnp.zeros((shard, LANES - columns.shape[1]), F32)
    out_ref[:, 4 * width :] = jnp.concatenate([columns, tail], axis=1).astype(BF)


def assemble_kernel(sources, shard, meta_ref, *refs):
    out_ref = refs[-1]
    for ref, offsets in zip(refs[:-1], sources):
        for at, offset in enumerate(offsets):
            row = jnp.bitwise_xor(meta_ref[0], offset) * shard
            out_ref[pl.ds(pl.multiple_of(row, shard), shard), :] = ref[at]


def place_kernel(experts, room, routes_ref, dy_ref, send_ref, prow_ref, pcol_ref):
    tokens = routes_ref.shape[4]
    slots = experts * room
    rows = routes_ref[0, 0, 0]
    first_row = rows[0:1]
    second_row = rows[1:2]
    tall = jnp.concatenate([rows.astype(F32), jnp.zeros((LANES - TOP, tokens), F32)], axis=0)
    cols = jnp.transpose(tall)[:, 0:8].astype(jnp.int32)
    hot_first = (iota((experts, tokens), 0) == first_row).astype(F32)
    hot_second = (iota((experts, tokens), 0) == second_row).astype(F32)
    earlier = (iota((tokens, tokens), 0) < iota((tokens, tokens), 1)).astype(BF)
    before = mm((hot_first + hot_second).astype(BF), earlier)
    in_first = jnp.sum(before * hot_first, axis=0, keepdims=True).astype(jnp.int32)
    in_second = jnp.sum((before + hot_first) * hot_second, axis=0, keepdims=True).astype(jnp.int32)
    place_first = first_row * room + in_first
    place_second = second_row * room + in_second
    prow_ref[0, 0:1, :] = place_first
    prow_ref[0, 1:2, :] = place_second
    slot_of = iota((slots, tokens), 0)
    hot = jnp.where((slot_of == place_first) | (slot_of == place_second), 1.0, 0.0).astype(BF)
    flat = dy_ref[...].reshape(tokens, dy_ref.shape[-1])
    rows = mm(hot, flat)
    for e in range(experts):
        send_ref[e] = rows[e * room : (e + 1) * room].astype(BF)
    first_col = cols[:, 0:1]
    second_col = cols[:, 1:2]
    hot_first = (iota((tokens, experts), 1) == first_col).astype(F32)
    hot_second = (iota((tokens, experts), 1) == second_col).astype(F32)
    later = (iota((tokens, tokens), 1) < iota((tokens, tokens), 0)).astype(BF)
    before = mm(later, (hot_first + hot_second).astype(BF))
    in_first = jnp.sum(before * hot_first, axis=1, keepdims=True).astype(jnp.int32)
    in_second = jnp.sum((before + hot_first) * hot_second, axis=1, keepdims=True).astype(jnp.int32)
    lane = iota((tokens, 8), 1)
    table = jnp.zeros((tokens, 8), jnp.int32)
    for at, col in enumerate(
        (
            first_col * room + in_first,
            second_col * room + in_second,
            first_col,
            second_col,
            in_first,
            in_second,
        )
    ):
        table = jnp.where(lane == at, col, table)
    pcol_ref[0] = table


def forward_kernel(
    cfg,
    mb,
    meta_ref,
    len_ref,
    own_ref,
    oth_ref,
    w_ref,
    prow_ref,
    send_ref,
    middle_ref,
    gate_ref,
    second_ref,
    oT_ref,
    q_ref,
    k_ref,
    v_ref,
    lse_ref,
    n1T_ref,
    att_ref,
    logs_ref,
):
    images, local_len, seq_count, width, experts, room = cfg
    full_len = local_len * seq_count
    tokens = images * local_len
    slots = experts * room
    misc_at = 4 * width
    rows = misc_rows(w_ref, misc_at)

    def vec(j):
        return rows[experts + j : experts + j + 1, :]

    here = meta_ref[1]
    lane = iota((1, LANES), 1)
    low_half = (lane < HD).astype(BF)
    high_half = (lane >= HD).astype(BF)
    for b in range(images):
        blocks = [own_ref[b]] + [oth_ref[j, b] for j in range(seq_count - 1)]
        full = jnp.concatenate(blocks, axis=0).astype(F32)
        unit, _ = norm_parts(full)
        normed = (unit * vec(0) + vec(1)).astype(BF)
        n1T_ref[:, b * full_len : (b + 1) * full_len] = jnp.transpose(normed)
        span = slice(b * local_len, (b + 1) * local_len)
        wide = slice(b * full_len, (b + 1) * full_len)
        queries = (mm(normed[:local_len], w_ref[:, :width]) + vec(2)).astype(BF)
        q_ref[span, :] = queries * jnp.asarray(HD**-0.5, BF)
        k_ref[wide, :] = mm(normed, w_ref[:, width : 2 * width]).astype(BF)
        v_ref[wide, :] = (mm(normed, w_ref[:, 2 * width : 3 * width]) + vec(3)).astype(BF)
        kpos = iota((1, full_len), 1)
        shift = jnp.zeros((1, full_len), jnp.int32)
        for j in range(seq_count):
            origin = lax.rem(here + j, seq_count) * local_len - j * local_len
            shift = jnp.where(kpos >= j * local_len, origin, shift)
        valid = (kpos + shift) < len_ref[mb * images + b]
        logs_ref[...] = jnp.zeros_like(logs_ref)

        def heads(blk, carry):
            at = pl.ds(pl.multiple_of(blk * LANES, LANES), LANES)
            q_blk = q_ref[span, at]
            k_blk = k_ref[wide, at]
            v_blk = v_ref[wide, at]
            outs = []
            for side, keep in enumerate((low_half, high_half)):
                scores = mm_nt(q_blk * keep, k_blk)
                scores = jnp.where(valid, scores, -1e30)
                highest = jnp.max(scores, axis=1, keepdims=True)
                powers = jnp.exp(scores - highest)
                total = jnp.sum(powers, axis=1, keepdims=True)
                probs = (powers * (1.0 / total)).astype(BF)
                outs.append(mm(probs, v_blk))
                logs_ref[...] = jnp.where(
                    lane == 2 * blk + side, highest + jnp.log(total), logs_ref[...]
                )
            att_ref[span, at] = jnp.where(lane < HD, outs[0], outs[1]).astype(BF)
            return carry

        lax.fori_loop(0, width // LANES, heads, 0)
        lse_ref[b * 8 : b * 8 + 8, :] = jnp.transpose(logs_ref[...])[0:8, :]
    attended = att_ref[...]
    oT_ref[...] = jnp.transpose(attended)
    branch = mm(attended, w_ref[:, 3 * width : 4 * width]) + vec(4)
    middle = own_ref[...].reshape(tokens, width).astype(F32) + branch
    middle_ref[...] = middle
    unit, _ = norm_parts(middle)
    second = (unit * vec(5) + vec(6)).astype(BF)
    second_ref[...] = second
    gate_ref[...] = gates(mm(second, w_ref[:, misc_at : misc_at + LANES]), experts)
    slot_of = iota((slots, tokens), 0)
    hot = jnp.where(
        (slot_of == prow_ref[0, 0:1, :]) | (slot_of == prow_ref[0, 1:2, :]), 1.0, 0.0
    ).astype(BF)
    sent = mm(hot, second)
    for e in range(experts):
        send_ref[e] = sent[e * room : (e + 1) * room].astype(BF)


def gates(logits, experts):
    real = iota((1, LANES), 1) < experts
    logits = jnp.where(real, logits, -1e30)
    powers = jnp.where(real, jnp.exp(logits - jnp.max(logits, axis=1, keepdims=True)), 0.0)
    return powers / jnp.sum(powers, axis=1, keepdims=True)


def expert_kernel(cfg, first, last, *refs):
    groups, room, capacity, width = cfg
    meta_ref, buf_ref, dyb_ref, wm_ref, up_ref, ub_ref, down_ref, db_ref = refs[:8]
    refs = refs[8:]
    if not first:
        _, gup_in, gdn_in, gb_in, gdb_in = refs[:5]
        refs = refs[6 if last else 5 :]
    r_ref, dbuf_ref, gup_ref, gdn_ref, gb_ref, gdb_ref = refs[:6]
    refs = refs[6:]
    if last:
        lows = refs[:4]
        refs = refs[4:]
    (
        flat_s,
        flatT_s,
        dr_s,
        drT_s,
        racc_s,
        dacc_s,
    ) = refs
    slots = groups * room
    step = pl.program_id(0)
    experts = groups

    @pl.when(step == 0)
    def _():
        flat = buf_ref[...].astype(F32).reshape(slots, width).astype(BF)
        flat_s[...] = flat
        flatT_s[...] = jnp.transpose(flat)
        gate = gates(mm(flat, wm_ref[...]), experts)
        mine = iota((1, LANES), 1) == meta_ref[0]
        mine_gate = jnp.sum(jnp.where(mine, gate, 0.0), axis=1, keepdims=True)
        dr = (dyb_ref[...].astype(F32).reshape(slots, width) * mine_gate).astype(BF)
        dr_s[...] = dr
        drT_s[...] = jnp.transpose(dr)
        shift_sum = jnp.sum(dr.astype(F32), axis=0, keepdims=True)
        gdb_ref[...] = shift_sum if first else gdb_in[...] + shift_sum
        racc_s[...] = jnp.zeros_like(racc_s)
        dacc_s[...] = jnp.zeros_like(dacc_s)

    flat = flat_s[...]
    dr = dr_s[...]
    hidden = mm(flat, up_ref[0]) + ub_ref[...].astype(F32)
    half_erf = 0.5 * lax.erf(hidden * (0.5**0.5)) + 0.5
    active = (hidden * half_erf).astype(BF)
    slope = half_erf + hidden * (jnp.exp(-0.5 * hidden * hidden) * 0.3989422804014327)
    racc_s[...] += mm(active, down_ref[0])
    grad_pre = mm_nt(dr, down_ref[0]) * slope
    low_pre = grad_pre.astype(BF)
    dacc_s[...] += mm_nt(low_pre, up_ref[0])
    gup = mm(flatT_s[...], low_pre)
    gdn = mm(drT_s[...], active)
    gbias = jnp.sum(low_pre.astype(F32), axis=0, keepdims=True)
    if not first:
        gup = gup_in[...] + gup
        gdn = gdn_in[...] + gdn
        gbias = gb_in[...] + gbias
    gup_ref[...] = gup
    gdn_ref[...] = gdn
    gb_ref[...] = gbias
    if last:
        early = step < pl.num_programs(0) // 2

        @pl.when(early)
        def _():
            lows[0][...] = gup.astype(BF)
            lows[2][...] = gdn.astype(BF)

        @pl.when(jnp.logical_not(early))
        def _():
            lows[1][...] = gup.astype(BF)
            lows[3][...] = gdn.astype(BF)

    @pl.when(step == pl.num_programs(0) - 1)
    def _():
        result = (racc_s[...] + db_ref[...].astype(F32)).astype(BF)
        for e in range(groups):
            r_ref[e] = result[e * room : (e + 1) * room]
        dy = dyb_ref[...].astype(F32).reshape(slots, width)
        dgate = jnp.sum(dy * result.astype(F32), axis=1, keepdims=True).reshape(groups, room, 1)
        spread = jnp.where(
            iota((groups, room, LANES), 2) == iota((groups, room, LANES), 1), dgate, 0.0
        )
        as_row = jnp.sum(spread, axis=1, keepdims=True)
        high = as_row.astype(BF).astype(F32)
        tail = jnp.zeros((groups, 1, width - 2 * LANES), F32)
        as_row = jnp.concatenate([high, as_row - high, tail], axis=2)
        back = dacc_s[...].reshape(groups, room, width)
        back = jnp.where(iota((groups, room, 1), 1) == capacity, as_row, back).astype(BF)
        for e in range(groups):
            dbuf_ref[e] = back[e]


def backward_kernel(cfg, mb, first, last, *refs):
    images, local_len, seq_count, width, experts, room, capacity = cfg
    (
        meta_ref,
        len_ref,
        dback_ref,
        pcol_ref,
        gate_ref,
        middle_ref,
        second_ref,
        dy_ref,
        oT_ref,
        w_ref,
        q_ref,
        k_ref,
        v_ref,
        lse_ref,
        n1T_ref,
        own_ref,
        oth_ref,
    ) = refs[:17]
    refs = refs[17:]
    if not first:
        g_in, mrow_in = refs[:2]
        refs = refs[2:]
    down_own, down_oth, dm_ref = refs[:3]
    refs = refs[3:]
    if last:
        low_ref = refs[0]
        refs = refs[1:]
    else:
        g_ref = refs[0]
        refs = refs[1:]
    mrow_ref, do_s, dqT_s, dkv_s = refs

    def add_dense(at, value):
        if not first:
            value = g_in[:, at] + value
        if last:
            low_ref[:, at] = value.astype(BF)
        else:
            g_ref[:, at] = value

    full_len = local_len * seq_count
    tokens = images * local_len
    slots = experts * room
    misc_at = 4 * width
    rows = misc_rows(w_ref, misc_at)
    here = meta_ref[1]

    def vec(j):
        return rows[experts + j : experts + j + 1, :]

    dback = dback_ref[...].astype(F32)
    back_rows = dback.reshape(slots, width).astype(BF)
    slot_of = iota((tokens, slots), 1)
    hot = jnp.where(
        (slot_of == pcol_ref[0, :, 0:1]) | (slot_of == pcol_ref[0, :, 1:2]), 1.0, 0.0
    ).astype(BF)
    from_experts = mm(hot, back_rows)
    spare = jnp.where(iota((experts, room, 1), 1) == capacity, dback[:, :, : 2 * LANES], 0.0)
    spare = jnp.sum(spare, axis=1)
    spare = jnp.concatenate(
        [spare, jnp.zeros((LANES - experts, 2 * LANES), F32)], axis=0
    ).astype(BF)
    lane = iota((tokens, LANES), 1)
    pulled = jnp.zeros((tokens, LANES), F32)
    for k in range(TOP):
        within = jnp.where(lane == pcol_ref[0, :, 4 + k : 5 + k], 1.0, 0.0).astype(BF)
        found = mm_nt(jnp.concatenate([within, within], axis=1), spare)
        pulled = pulled + jnp.where(lane == pcol_ref[0, :, 2 + k : 3 + k], found, 0.0)
    gate = gate_ref[...]
    dlogit = gate * (pulled - jnp.sum(gate * pulled, axis=1, keepdims=True))
    dlogit_low = dlogit.astype(BF)
    mrow_ref[...] = mm(jnp.transpose(dlogit_low.astype(F32)).astype(BF), second_ref[...])
    dn2 = from_experts + mm_nt(dlogit_low, w_ref[:, misc_at : misc_at + LANES])
    unit, scale = norm_parts(middle_ref[...])
    dy = dy_ref[...].reshape(tokens, width).astype(F32)
    dm = dy + norm_pull(unit, scale, vec(5), dn2)
    dm_ref[...] = dm
    da = dm.astype(BF)
    gproj = mm(oT_ref[...], da)
    proj = slice(3 * width, 4 * width)
    add_dense(proj, gproj)
    do_s[...] = mm_nt(da, w_ref[:, proj]).astype(BF)
    half_lane = iota((1, LANES), 1)
    low_half = (half_lane < HD).astype(BF)
    high_half = (half_lane >= HD).astype(BF)
    gqkv = [None, None]
    bias_q = jnp.zeros((1, width), F32)
    bias_v = jnp.zeros((1, width), F32)
    gain_sum = jnp.zeros((1, width), F32)
    shift_sum = jnp.zeros((1, width), F32)
    for b in range(images):
        span = slice(b * local_len, (b + 1) * local_len)
        wide = slice(b * full_len, (b + 1) * full_len)
        kpos = iota((full_len, 1), 0)
        shift = jnp.zeros((full_len, 1), jnp.int32)
        for j in range(seq_count):
            origin = lax.rem(here + j, seq_count) * local_len - j * local_len
            shift = jnp.where(kpos >= j * local_len, origin, shift)
        valid = (kpos + shift) < len_ref[mb * images + b]

        def heads(blk, carry):
            at = pl.ds(pl.multiple_of(blk * LANES, LANES), LANES)
            q_blk = q_ref[span, at]
            k_blk = k_ref[wide, at]
            v_blk = v_ref[wide, at]
            do_blk = do_s[span, at]
            kT_blk = jnp.transpose(k_blk)
            dvs = []
            dks = []
            dqs = []
            for side, keep in enumerate((low_half, high_half)):
                scores = mm_nt(k_blk, q_blk * keep)
                logs = lse_ref[pl.ds(b * 8 + 2 * blk + side, 1), :]
                probs = jnp.where(valid, jnp.exp(scores - logs), 0.0)
                dprobs = mm_nt(v_blk, do_blk * keep)
                inner = jnp.sum(probs * dprobs, axis=0, keepdims=True)
                dscores = (probs * (dprobs - inner)).astype(BF)
                dvs.append(mm(probs.astype(BF), do_blk))
                dks.append(mm(dscores, q_blk))
                dqs.append(mm(kT_blk[side * HD : (side + 1) * HD], dscores))
            dqT_s[pl.ds(pl.multiple_of(blk * LANES, LANES), HD), :] = dqs[0]
            dqT_s[pl.ds(pl.multiple_of(blk * LANES + HD, HD), HD), :] = dqs[1]
            left = half_lane < HD
            dkv_s[:, at] = jnp.where(left, dks[0], dks[1]).astype(BF)
            vat = pl.ds(pl.multiple_of(width + blk * LANES, LANES), LANES)
            dkv_s[:, vat] = jnp.where(left, dvs[0], dvs[1]).astype(BF)
            return carry

        lax.fori_loop(0, width // LANES, heads, 0)
        dq = (jnp.transpose(dqT_s[...]) * HD**-0.5).astype(BF)
        dkv = dkv_s[...]
        part_q = mm(n1T_ref[:, b * full_len : b * full_len + local_len], dq)
        part_kv = mm(n1T_ref[:, wide], dkv)
        gqkv[0] = part_q if b == 0 else gqkv[0] + part_q
        gqkv[1] = part_kv if b == 0 else gqkv[1] + part_kv
        bias_q = bias_q + jnp.sum(dq.astype(F32), axis=0, keepdims=True)
        bias_v = bias_v + jnp.sum(dkv[:, width:].astype(F32), axis=0, keepdims=True)
        down = mm_nt(dkv, w_ref[:, width : 3 * width])
        down_own[span, :] = mm_nt(dq, w_ref[:, :width])
        down_own[span, :] += down[:local_len]
        for j in range(seq_count):
            part = down_own[span, :] if j == 0 else down[j * local_len : (j + 1) * local_len]
            tokens_in = own_ref[b] if j == 0 else oth_ref[j - 1, b]
            first_unit, _ = norm_parts(tokens_in.astype(F32))
            gain_sum = gain_sum + jnp.sum(part * first_unit, axis=0, keepdims=True)
            shift_sum = shift_sum + jnp.sum(part, axis=0, keepdims=True)
            if j > 0:
                down_oth[j - 1, span, :] = part.astype(BF)
    add_dense(slice(0, width), gqkv[0])
    add_dense(slice(width, 3 * width), gqkv[1])
    row = iota((LANES, 1), 0)
    mrow = jnp.where(row < experts, mrow_ref[...], 0.0)
    sums = (
        gain_sum,
        shift_sum,
        bias_q,
        bias_v,
        jnp.sum(da.astype(F32), axis=0, keepdims=True),
        jnp.sum(dn2 * unit, axis=0, keepdims=True),
        jnp.sum(dn2, axis=0, keepdims=True),
    )
    for j, value in enumerate(sums):
        mrow = jnp.where(row == experts + j, value, mrow)
    if not first:
        mrow = mrow_in[...] + mrow
    mrow_ref[...] = mrow
    if last:
        low_ref[:, misc_at : misc_at + LANES] = jnp.transpose(mrow).astype(BF)


def input_kernel(cfg, own_ref, got_ref, x_ref, dm_ref, wm_ref, *refs):
    out_ref = refs[-1]
    images, local_len, seq_count, width, experts = cfg
    tokens = images * local_len
    rows = jnp.transpose(wm_ref[...].astype(F32))
    dn1 = own_ref[...]
    for j in range(seq_count - 1):
        dn1 = dn1 + got_ref[j].astype(F32)
    unit, scale = norm_parts(x_ref[...].reshape(tokens, width).astype(F32))
    grad = dm_ref[...] + norm_pull(unit, scale, rows[experts : experts + 1, :], dn1)
    out_ref[...] = grad.astype(BF).reshape(images, local_len, width)


def mix_kernel(cfg, back_ref, pcol_ref, *refs):
    for mb in range(MICRO):

        @pl.when(pl.program_id(0) == mb)
        def _():
            mix_part(cfg, back_ref, pcol_ref, refs[2 * mb], refs[2 * mb + 1], refs[-1])


def mix_part(cfg, back_ref, pcol_ref, gate_ref, middle_ref, out_ref):
    images, local_len, width, experts, room = cfg
    tokens = images * local_len
    slots = experts * room
    back = back_ref[...].astype(F32).reshape(slots, width).astype(BF)
    slot_of = iota((tokens, slots), 1)
    lane = iota((tokens, LANES), 1)
    gate = gate_ref[...]
    total = middle_ref[...]
    for k in range(TOP):
        hot = jnp.where(slot_of == pcol_ref[0, :, k : k + 1], 1.0, 0.0).astype(BF)
        chosen = jnp.where(lane == pcol_ref[0, :, 2 + k : 3 + k], gate, 0.0)
        total = total + jnp.sum(chosen, axis=1, keepdims=True) * mm(hot, back)
    out_ref[...] = total.astype(BF).reshape(images, local_len, width)


def sum_kernel(gup_ref, gdn_ref, up_early, up_late, dn_early, dn_late, up_ref, dn_ref):
    late = pl.program_id(0) >= pl.num_programs(0) // 2
    got_up = jnp.where(late, up_late[...], up_early[...])
    got_dn = jnp.where(late, dn_late[...], dn_early[...])
    up_ref[0] = gup_ref[...] + got_up.astype(F32)
    dn_ref[0] = jnp.transpose(gdn_ref[...] + got_dn.astype(F32))


def smem_spec():
    return pl.BlockSpec(memory_space=pltpu.SMEM)


def params():
    return pltpu.CompilerParams(vmem_limit_bytes=VMEM_LIMIT)


def cost(micros):
    return pl.CostEstimate(
        flops=int(micros * 1e9), transcendentals=0, bytes_accessed=int(micros * 2e6)
    )


def struct(shape, kind):
    return jax.ShapeDtypeStruct(shape, kind)


def after(value, *others):
    return lax.optimization_barrier((value, *others))[0]


def on_device(
    images,
    cotangent,
    lengths,
    routes,
    attn_norm_gain,
    attn_norm_bias,
    qkv_weight,
    query_value_bias,
    proj_weight,
    proj_bias,
    moe_norm_gain,
    moe_norm_bias,
    router_weight,
    up_weight,
    up_bias,
    down_weight,
    down_bias,
):
    seq_count = lax.axis_size("seq")
    dp_count = lax.axis_size("dp")
    count = images.shape[0] // MICRO
    local_len = images.shape[1]
    width = images.shape[2]
    tokens = count * local_len
    full_len = local_len * seq_count
    experts = router_weight.shape[1]
    hidden = up_weight.shape[2]
    capacity = (5 * tokens * TOP + 4 * experts - 1) // (4 * experts)
    room = (capacity + 1 + 7) // 8 * 8
    slots = experts * room
    assert up_weight.shape[0] == 1 and experts == dp_count
    assert experts + VEC <= LANES and capacity <= LANES
    meta = jnp.stack([lax.axis_index("dp"), lax.axis_index("seq")]).astype(jnp.int32)
    packed_width = 4 * width + LANES

    def full(shape):
        return pl.BlockSpec(shape, lambda i: (0,) * len(shape))

    def token_spec(mb):
        return pl.BlockSpec((count, local_len, width), lambda i: (mb, 0, 0))

    def table_spec(mb, shape):
        return pl.BlockSpec((1, *shape), lambda i: (mb, 0, 0))

    def block_spec(mb):
        return pl.BlockSpec((experts, room, width), lambda i: (0, mb, 0))

    any_spec = pl.BlockSpec(memory_space=pl.ANY)
    other_spec = lambda mb: pl.BlockSpec(
        (seq_count - 1, count, local_len, width), lambda i: (0, max(mb - 1, 0), 0, 0)
    )
    halved = hidden // FF_BLOCK // 2
    early_spec = lambda: pl.BlockSpec(
        (width, FF_BLOCK), lambda i: (0, jnp.minimum(i, halved - 1))
    )
    late_spec = lambda: pl.BlockSpec(
        (width, FF_BLOCK), lambda i: (0, jnp.maximum(i - halved, 0))
    )
    misc_spec = pl.BlockSpec((width, LANES), lambda i: (0, 4 * width // LANES))
    moved = struct((experts, room, width), BF)
    merged = struct((experts, MICRO * room, width), BF)
    tailed = struct((experts, (MICRO - 1) * room, width), BF)

    def seq_shift(array, j):
        return lax.ppermute(array, "seq", [((i + j) % seq_count, i) for i in range(seq_count)])

    others = []
    for part in (images[:count], images[count:]):
        moved_images = jnp.stack([seq_shift(part, j) for j in range(1, seq_count)])
        others.append(moved_images)

    sent_dy, prow, pcol = pl.pallas_call(
        functools.partial(place_kernel, experts, room),
        grid=(MICRO,),
        in_specs=[
            pl.BlockSpec((1, 1, 1, TOP, tokens), lambda i: (0, i, 0, 0, 0)),
            pl.BlockSpec((count, local_len, width), lambda i: (i, 0, 0)),
        ],
        out_specs=[
            pl.BlockSpec((experts, room, width), lambda i: (0, i, 0)),
            pl.BlockSpec((1, TOP, tokens), lambda i: (i, 0, 0)),
            pl.BlockSpec((1, tokens, 8), lambda i: (i, 0, 0)),
        ],
        out_shape=[
            merged,
            struct((MICRO, TOP, tokens), jnp.int32),
            struct((MICRO, tokens, 8), jnp.int32),
        ],
        compiler_params=params(),
        cost_estimate=cost(8),
        name="place",
    )(jnp.swapaxes(routes, 3, 4), cotangent)

    vectors = jnp.concatenate(
        [
            jnp.stack([attn_norm_gain, attn_norm_bias]),
            query_value_bias,
            jnp.stack([proj_bias, moe_norm_gain, moe_norm_bias, jnp.zeros_like(proj_bias)]),
        ],
        axis=0,
    )
    shard = router_weight.shape[0]
    bits = dp_count.bit_length() - 1
    assert dp_count == 1 << bits

    def across(value, offset):
        return lax.ppermute(value, "dp", [(i, i ^ offset) for i in range(dp_count)])

    def gather_rows(own, gate):
        quarter = dp_count // 4
        held = [jnp.stack([own, *[across(own, k * quarter) for k in (1, 2, 3)]])]
        offsets = [[0, quarter, 2 * quarter, 3 * quarter]]
        for bit in reversed(range(bits - 2)):
            if bit == 0:
                held[-1] = after(held[-1], gate)
            held += [across(h, 1 << bit) for h in held]
            offsets += [[k ^ (1 << bit) for k in known] for known in offsets]
        return pl.pallas_call(
            functools.partial(assemble_kernel, offsets, shard),
            grid=(1,),
            in_specs=[smem_spec(), *[full(h.shape) for h in held]],
            out_specs=full((dp_count * shard, packed_width)),
            out_shape=struct((dp_count * shard, packed_width), BF),
            compiler_params=params(),
            cost_estimate=cost(3),
            name="assemble",
        )(meta, *held), held[0]

    def scatter_rows(total, far):
        me = lax.axis_index("dp")
        value = total.reshape(dp_count // 2, 2, shard, packed_width)
        for bit in range(bits - 2):
            mine = lax.bitwise_and(lax.shift_right_logical(me, bit), 1)
            keep = lax.dynamic_index_in_dim(value, mine, 1, keepdims=False)
            give = lax.dynamic_index_in_dim(value, 1 - mine, 1, keepdims=False)
            give = give.astype(BF)
            value = keep.astype(F32) + across(give, 1 << bit).astype(F32)
            if bit < bits - 3:
                value = value.reshape(-1, 2, shard, packed_width)
        value = after(value, *far)
        high = lax.shift_right_logical(me, bits - 2)
        result = lax.dynamic_index_in_dim(value, high, 0, keepdims=False)
        for offset in (1, 2, 3):
            give = lax.dynamic_index_in_dim(
                value, lax.bitwise_xor(high, offset), 0, keepdims=False
            )
            result = result + across(give.astype(BF), offset << (bits - 2)).astype(F32)
        return result, value

    pack_args = (qkv_weight, proj_weight, router_weight.T, vectors)
    packed_shard = pl.pallas_call(
        functools.partial(pack_kernel, experts),
        grid=(1,),
        in_specs=[full(a.shape) for a in pack_args],
        out_specs=full((shard, packed_width)),
        out_shape=struct((shard, packed_width), BF),
        compiler_params=params(),
        cost_estimate=cost(1),
        name="pack",
    )(*pack_args)

    def exchange(array):
        return lax.all_to_all(array, "dp", split_axis=0, concat_axis=0, tiled=True)

    packed, near = gather_rows(packed_shard, others[1])
    dyb = exchange(after(sent_dy, near, others[0]))

    def forward(mb):
        cfg = (count, local_len, seq_count, width, experts, room)
        outs = [
            ((experts, room, width), BF),
            ((tokens, width), F32),
            ((tokens, LANES), F32),
            ((tokens, width), BF),
            ((width, tokens), BF),
            ((tokens, width), BF),
            ((count * full_len, width), BF),
            ((count * full_len, width), BF),
            ((count * 8, local_len), F32),
            ((width, count * full_len), BF),
        ]
        return pl.pallas_call(
            functools.partial(forward_kernel, cfg, mb),
            grid=(1,),
            in_specs=[
                smem_spec(),
                smem_spec(),
                token_spec(mb),
                other_spec(mb),
                full((width, packed_width)),
                table_spec(mb, (TOP, tokens)),
            ],
            out_specs=[full(s) for s, _ in outs],
            out_shape=[struct(s, k) for s, k in outs],
            scratch_shapes=[
                pltpu.VMEM((tokens, width), BF),
                pltpu.VMEM((local_len, LANES), F32),
            ],
            compiler_params=params(),
            cost_estimate=cost(11),
            name="forward",
        )(meta, lengths, images, others[min(mb, 1)], packed, prow)

    def expert(mb, buf, results, tail_back, totals):
        first = mb == 0
        last = mb == MICRO - 1
        cfg = (experts, room, capacity, width)
        wide = lambda: pl.BlockSpec((width, FF_BLOCK), lambda i: (0, i))
        thin = lambda: pl.BlockSpec((1, FF_BLOCK), lambda i: (0, i))
        in_specs = [
            smem_spec(),
            full((experts, room, width)),
            block_spec(mb),
            misc_spec,
            pl.BlockSpec((1, width, FF_BLOCK), lambda i: (0, 0, i)),
            thin(),
            pl.BlockSpec((1, FF_BLOCK, width), lambda i: (0, i, 0)),
            full((1, width)),
        ]
        total_specs = [wide(), wide(), thin(), full((1, width))]
        args = [meta, buf, dyb, packed, up_weight, up_bias, down_weight, down_bias]
        aliases = {}
        if not first:
            aliases = {len(args): 0}
            aliases.update({len(args) + 1 + j: 2 + j for j in range(4)})
            in_specs += [any_spec, *total_specs]
            args += [results, *totals]
        if mb >= 2:
            aliases[len(args)] = 1
            in_specs += [any_spec]
            args += [tail_back]
        outs = pl.pallas_call(
            functools.partial(expert_kernel, cfg, first, last),
            grid=(hidden // FF_BLOCK,),
            in_specs=in_specs,
            out_specs=[block_spec(mb), block_spec(max(mb - 1, 0)), *total_specs]
            + ([early_spec(), late_spec()] * 2 if last else []),
            out_shape=[
                merged,
                moved if first else tailed,
                struct((width, hidden), F32),
                struct((width, hidden), F32),
                struct((1, hidden), F32),
                struct((1, width), F32),
            ]
            + ([struct((width, hidden // 2), BF)] * 4 if last else []),
            scratch_shapes=[
                pltpu.VMEM((slots, width), BF),
                pltpu.VMEM((width, slots), BF),
                pltpu.VMEM((slots, width), BF),
                pltpu.VMEM((width, slots), BF),
                pltpu.VMEM((slots, width), F32),
                pltpu.VMEM((slots, width), F32),
            ],
            input_output_aliases=aliases,
            compiler_params=params(),
            cost_estimate=cost(19),
            name="expert",
        )(*args)
        return outs[0], outs[1], tuple(outs[2:])

    def backward(mb, dback, saved, totals):
        first = mb == 0
        last = mb == MICRO - 1
        cfg = (count, local_len, seq_count, width, experts, room, capacity)
        middle, gate, second, oT, q, k, v, lse, n1T = saved
        whole = [gate, middle, second]
        heads = [oT, packed, q, k, v, lse, n1T]
        args = [meta, lengths, dback, pcol, *whole, cotangent, *heads, images, others[min(mb, 1)]]
        in_specs = [
            smem_spec(),
            smem_spec(),
            block_spec(max(mb - 1, 0)),
            table_spec(mb, (tokens, 8)),
            *[full(a.shape) for a in whole],
            token_spec(mb),
            *[full(a.shape) for a in heads],
            token_spec(mb),
            other_spec(mb),
        ]
        aliases = {}
        if not first:
            in_specs += [full(a.shape) for a in totals]
            args += list(totals)
            if not last:
                aliases = {len(args) - 2: 3, len(args) - 1: 4}
        outs = [
            ((tokens, width), F32),
            ((seq_count - 1, tokens, width), BF),
            ((tokens, width), F32),
            ((width, packed_width), BF) if last else ((width, 4 * width), F32),
            ((LANES, width), F32),
        ]
        return pl.pallas_call(
            functools.partial(backward_kernel, cfg, mb, first, last),
            grid=(1,),
            in_specs=in_specs,
            out_specs=[full(s) for s, _ in outs],
            out_shape=[struct(s, t) for s, t in outs],
            scratch_shapes=[
                pltpu.VMEM((tokens, width), BF),
                pltpu.VMEM((width, local_len), F32),
                pltpu.VMEM((full_len, 2 * width), BF),
            ],
            input_output_aliases=aliases,
            compiler_params=params(),
            cost_estimate=cost(1 if last else 17),
            name="backward",
        )(*args)

    def into(kernel, mb, args, specs, previous, micros, name):
        aliases = {}
        if previous is not None:
            aliases = {len(args): 0}
            args = [*args, previous]
            specs = [*specs, any_spec]
        return pl.pallas_call(
            kernel,
            grid=(1,),
            in_specs=specs,
            out_specs=token_spec(mb),
            out_shape=struct(images.shape, BF),
            input_output_aliases=aliases,
            compiler_params=params(),
            cost_estimate=cost(micros),
            name=name,
        )(*args)

    def finish(mb, own, got, dm, previous):
        cfg = (count, local_len, seq_count, width, experts)
        specs = [full(own.shape), full(got.shape), token_spec(mb), full(dm.shape), misc_spec]
        return into(
            functools.partial(input_kernel, cfg),
            mb,
            [own, got, images, dm, packed],
            specs,
            previous,
            3,
            "finish",
        )

    def mix(back):
        cfg = (count, local_len, width, experts, room)
        tables = sum([[saved[mb][1], saved[mb][0]] for mb in range(MICRO)], [])
        return pl.pallas_call(
            functools.partial(mix_kernel, cfg),
            grid=(MICRO,),
            in_specs=[
                pl.BlockSpec((experts, room, width), lambda i: (0, i, 0)),
                pl.BlockSpec((1, tokens, 8), lambda i: (i, 0, 0)),
                *[full(t.shape) for t in tables],
            ],
            out_specs=pl.BlockSpec((count, local_len, width), lambda i: (i, 0, 0)),
            out_shape=struct(images.shape, BF),
            compiler_params=params(),
            cost_estimate=cost(7),
            name="mix",
        )(back, pcol, *tables)

    swap = [(i, (i + 1) % seq_count) for i in range(seq_count)]

    def seq_sum(value):
        if seq_count == 2:
            return value + lax.ppermute(value.astype(BF), "seq", swap).astype(F32)
        return lax.psum(value.astype(BF), "seq").astype(F32)

    passed = [forward(mb) for mb in range(MICRO)]
    saved = [outs[1:] for outs in passed]
    bufs = []
    for mb in range(MICRO):
        first_gate = (dyb,) if mb == 0 else ()
        bufs.append(exchange(after(passed[mb][0], *first_gate)))
    totals = None
    results = None
    ready = [None, None]
    for mb in range(MICRO):
        results, ready[min(mb, 1)], totals = expert(mb, bufs[mb], results, ready[1], totals)
    gup, gdn, gbias, gdbias, *pieces = totals
    arrived = []
    if seq_count == 2:
        arrived = [lax.ppermute(piece, "seq", swap) for piece in pieces]
    dense = None
    owns = []
    gots = []
    dms = []
    dbacks = [exchange(ready[0]), exchange(ready[1])]
    if arrived:
        dbacks[1], arrived[0] = lax.optimization_barrier((dbacks[1], arrived[0]))
    for mb in range(MICRO):
        dback = dbacks[min(mb, 1)]
        if mb == 2 and arrived:
            dense, arrived[1] = lax.optimization_barrier((dense, arrived[1]))
        own, oth, dm, *dense = backward(mb, dback, saved[mb], dense)
        owns.append(own)
        dms.append(dm)
        gots.append(
            jnp.stack(
                [
                    lax.ppermute(
                        oth[j - 1], "seq", [(i, (i + j) % seq_count) for i in range(seq_count)]
                    )
                    for j in range(1, seq_count)
                ]
            )
        )
    back = exchange(after(results, dbacks[1]))
    first, far = (), ()
    if arrived:
        first, far = (arrived[2],), (arrived[3], gots[0], gots[1])
    shards, late = scatter_rows(after(dense[0], *first), (*far, back))
    owns = [after(own, late) for own in owns]
    grads = None
    for mb in range(MICRO):
        grads = finish(mb, owns[mb], gots[mb], dms[mb], grads)
    out = mix(back)

    if seq_count == 2:
        wide = lambda: pl.BlockSpec((width, FF_BLOCK), lambda i: (0, i))
        final_up, final_down = pl.pallas_call(
            sum_kernel,
            grid=(hidden // FF_BLOCK,),
            in_specs=[wide(), wide(), *[early_spec(), late_spec()] * 2],
            out_specs=[
                pl.BlockSpec((1, width, FF_BLOCK), lambda i: (0, 0, i)),
                pl.BlockSpec((1, FF_BLOCK, width), lambda i: (0, i, 0)),
            ],
            out_shape=[struct((1, width, hidden), F32), struct((1, hidden, width), F32)],
            compiler_params=params(),
            cost_estimate=cost(8),
            name="sum_experts",
        )(gup, gdn, *arrived)
    else:
        sums = [lax.psum(piece, "seq").astype(F32) for piece in pieces]
        final_up = jnp.concatenate(sums[:2], axis=1)[None]
        final_down = jnp.swapaxes(jnp.concatenate(sums[2:], axis=1), 0, 1)[None]
    biases = seq_sum(jnp.concatenate([gbias, gdbias], axis=1))
    final_up_shift = biases[:, :hidden]
    final_down_shift = biases[:, hidden:]

    shards = seq_sum(shards)
    misc = 4 * width + experts
    return (
        out,
        grads,
        shards[:, misc],
        shards[:, misc + 1],
        shards[:, : 3 * width],
        jnp.stack([shards[:, misc + 2], shards[:, misc + 3]]),
        shards[:, 3 * width : 4 * width],
        shards[:, misc + 4],
        shards[:, misc + 5],
        shards[:, misc + 6],
        shards[:, 4 * width : misc],
        final_up,
        final_up_shift,
        final_down,
        final_down_shift,
    )


def solution(mesh):
    return jax.shard_map(
        on_device,
        mesh=mesh,
        in_specs=(
            P("dp", "seq", None),
            P("dp", "seq", None),
            P("dp"),
            P("dp", None, "seq", None, None),
            P("dp"),
            P("dp"),
            P("dp", None),
            P(None, "dp"),
            P("dp", None),
            P("dp"),
            P("dp"),
            P("dp"),
            P("dp", None),
            P("dp", None, None),
            P("dp", None),
            P("dp", None, None),
            P("dp", None),
        ),
        out_specs=(
            P("dp", "seq", None),
            P("dp", "seq", None),
            P("dp"),
            P("dp"),
            P("dp", None),
            P(None, "dp"),
            P("dp", None),
            P("dp"),
            P("dp"),
            P("dp"),
            P("dp", None),
            P("dp", None, None),
            P("dp", None),
            P("dp", None, None),
            P("dp", None),
        ),
        check_vma=False,
    )
```

```python
import functools

import jax
import jax.numpy as jnp
from jax import lax
from jax.experimental import pallas as pl
from jax.experimental.pallas import tpu as pltpu
from jax.sharding import PartitionSpec as P

HD = 64
TOP = 2
MICRO = 3
BF = jnp.bfloat16
F32 = jnp.float32
EPS = 1e-06
LANES = 128
VEC = 8
FF_BLOCK = 512
VMEM_LIMIT = 60 * 1024 * 1024


def mm(left, right):
    return jnp.dot(left, right, preferred_element_type=F32)


def mm_nt(left, right):
    return lax.dot_general(
        left, right, (((1,), (1,)), ((), ())), preferred_element_type=F32
    )


def iota(shape, dim):
    return lax.broadcasted_iota(jnp.int32, shape, dim)


def norm_parts(values):
    average = jnp.mean(values, axis=-1, keepdims=True)
    centred = values - average
    spread = jnp.mean(centred * centred, axis=-1, keepdims=True)
    scale = lax.rsqrt(spread + EPS)
    return centred * scale, scale


def norm_pull(unit, scale, gain, cotangent):
    inner = cotangent * gain
    mean_inner = jnp.mean(inner, axis=-1, keepdims=True)
    mean_unit = jnp.mean(inner * unit, axis=-1, keepdims=True)
    return scale * (inner - mean_inner - unit * mean_unit)


def misc_rows(w_ref, start):
    return jnp.transpose(w_ref[:, start : start + LANES].astype(F32))


def pack_kernel(experts, qkv_ref, proj_ref, router_ref, vec_ref, out_ref):
    width = proj_ref.shape[1]
    shard = proj_ref.shape[0]
    out_ref[:, : 3 * width] = qkv_ref[...]
    out_ref[:, 3 * width : 4 * width] = proj_ref[...]
    rows = jnp.concatenate([router_ref[...].astype(F32), vec_ref[...].astype(F32)], axis=0)
    columns = jnp.transpose(rows)
    tail = jnp.zeros((shard, LANES - columns.shape[1]), F32)
    out_ref[:, 4 * width :] = jnp.concatenate([columns, tail], axis=1).astype(BF)


def assemble_kernel(sources, shard, meta_ref, *refs):
    out_ref = refs[-1]
    for ref, offsets in zip(refs[:-1], sources):
        for at, offset in enumerate(offsets):
            row = jnp.bitwise_xor(meta_ref[0], offset) * shard
            out_ref[pl.ds(pl.multiple_of(row, shard), shard), :] = ref[at]


def window(capacity, mb):
    start = capacity * mb // 8 * 8
    return start, capacity * mb - start


def place_kernel(experts, room, capacity, routes_ref, dy_ref, send_ref, prow_ref, pcol_ref):
    for mb in range(MICRO):

        @pl.when(pl.program_id(0) == mb)
        def _():
            place_part(
                experts, room, window(capacity, mb), routes_ref, dy_ref, send_ref, prow_ref, pcol_ref
            )


def place_part(experts, room, where, routes_ref, dy_ref, send_ref, prow_ref, pcol_ref):
    start, shift = where
    tokens = routes_ref.shape[4]
    slots = experts * room
    rows = routes_ref[0, 0, 0]
    first_row = rows[0:1]
    second_row = rows[1:2]
    tall = jnp.concatenate([rows.astype(F32), jnp.zeros((LANES - TOP, tokens), F32)], axis=0)
    cols = jnp.transpose(tall)[:, 0:8].astype(jnp.int32)
    hot_first = (iota((experts, tokens), 0) == first_row).astype(F32)
    hot_second = (iota((experts, tokens), 0) == second_row).astype(F32)
    earlier = (iota((tokens, tokens), 0) < iota((tokens, tokens), 1)).astype(BF)
    before = mm((hot_first + hot_second).astype(BF), earlier)
    in_first = jnp.sum(before * hot_first, axis=0, keepdims=True).astype(jnp.int32)
    in_second = jnp.sum((before + hot_first) * hot_second, axis=0, keepdims=True).astype(jnp.int32)
    place_first = first_row * room + in_first + shift
    place_second = second_row * room + in_second + shift
    prow_ref[0, 0:1, :] = place_first
    prow_ref[0, 1:2, :] = place_second
    slot_of = iota((slots, tokens), 0)
    hot = jnp.where((slot_of == place_first) | (slot_of == place_second), 1.0, 0.0).astype(BF)
    flat = dy_ref[...].reshape(tokens, dy_ref.shape[-1])
    rows = mm(hot, flat)
    for e in range(experts):
        block = rows[e * room : (e + 1) * room].astype(BF)
        if shift:
            send_ref[e, start : start + 8] = send_ref[e, start : start + 8] + block[:8]
            send_ref[e, start + 8 : start + room] = block[8:]
        else:
            send_ref[e, start : start + room] = block
    first_col = cols[:, 0:1]
    second_col = cols[:, 1:2]
    hot_first = (iota((tokens, experts), 1) == first_col).astype(F32)
    hot_second = (iota((tokens, experts), 1) == second_col).astype(F32)
    later = (iota((tokens, tokens), 1) < iota((tokens, tokens), 0)).astype(BF)
    before = mm(later, (hot_first + hot_second).astype(BF))
    in_first = jnp.sum(before * hot_first, axis=1, keepdims=True).astype(jnp.int32)
    in_second = jnp.sum((before + hot_first) * hot_second, axis=1, keepdims=True).astype(jnp.int32)
    lane = iota((tokens, 8), 1)
    table = jnp.zeros((tokens, 8), jnp.int32)
    for at, col in enumerate(
        (
            first_col * room + in_first + shift,
            second_col * room + in_second + shift,
            first_col,
            second_col,
            in_first + shift,
            in_second + shift,
        )
    ):
        table = jnp.where(lane == at, col, table)
    pcol_ref[0] = table


def forward_kernel(
    cfg,
    mb,
    meta_ref,
    len_ref,
    own_ref,
    oth_ref,
    w_ref,
    prow_ref,
    send_ref,
    middle_ref,
    gate_ref,
    second_ref,
    oT_ref,
    q_ref,
    k_ref,
    v_ref,
    lse_ref,
    n1T_ref,
    att_ref,
    logs_ref,
):
    images, local_len, seq_count, width, experts, room = cfg
    full_len = local_len * seq_count
    tokens = images * local_len
    slots = experts * room
    misc_at = 4 * width
    rows = misc_rows(w_ref, misc_at)

    def vec(j):
        return rows[experts + j : experts + j + 1, :]

    here = meta_ref[1]
    lane = iota((1, LANES), 1)
    low_half = (lane < HD).astype(BF)
    high_half = (lane >= HD).astype(BF)
    for b in range(images):
        blocks = [own_ref[b]] + [oth_ref[j, b] for j in range(seq_count - 1)]
        full = jnp.concatenate(blocks, axis=0).astype(F32)
        unit, _ = norm_parts(full)
        normed = (unit * vec(0) + vec(1)).astype(BF)
        n1T_ref[:, b * full_len : (b + 1) * full_len] = jnp.transpose(normed)
        span = slice(b * local_len, (b + 1) * local_len)
        wide = slice(b * full_len, (b + 1) * full_len)
        queries = (mm(normed[:local_len], w_ref[:, :width]) + vec(2)).astype(BF)
        q_ref[span, :] = queries * jnp.asarray(HD**-0.5, BF)
        k_ref[wide, :] = mm(normed, w_ref[:, width : 2 * width]).astype(BF)
        v_ref[wide, :] = (mm(normed, w_ref[:, 2 * width : 3 * width]) + vec(3)).astype(BF)
        kpos = iota((1, full_len), 1)
        shift = jnp.zeros((1, full_len), jnp.int32)
        for j in range(seq_count):
            origin = lax.rem(here + j, seq_count) * local_len - j * local_len
            shift = jnp.where(kpos >= j * local_len, origin, shift)
        valid = (kpos + shift) < len_ref[mb * images + b]
        logs_ref[...] = jnp.zeros_like(logs_ref)

        def heads(blk, carry):
            at = pl.ds(pl.multiple_of(blk * LANES, LANES), LANES)
            q_blk = q_ref[span, at]
            k_blk = k_ref[wide, at]
            v_blk = v_ref[wide, at]
            outs = []
            for side, keep in enumerate((low_half, high_half)):
                scores = mm_nt(q_blk * keep, k_blk)
                scores = jnp.where(valid, scores, -1e30)
                highest = jnp.max(scores, axis=1, keepdims=True)
                powers = jnp.exp(scores - highest)
                total = jnp.sum(powers, axis=1, keepdims=True)
                probs = (powers * (1.0 / total)).astype(BF)
                outs.append(mm(probs, v_blk))
                logs_ref[...] = jnp.where(
                    lane == 2 * blk + side, highest + jnp.log(total), logs_ref[...]
                )
            att_ref[span, at] = jnp.where(lane < HD, outs[0], outs[1]).astype(BF)
            return carry

        lax.fori_loop(0, width // LANES, heads, 0)
        lse_ref[b * 8 : b * 8 + 8, :] = jnp.transpose(logs_ref[...])[0:8, :]
    attended = att_ref[...]
    oT_ref[...] = jnp.transpose(attended)
    branch = mm(attended, w_ref[:, 3 * width : 4 * width]) + vec(4)
    middle = own_ref[...].reshape(tokens, width).astype(F32) + branch
    middle_ref[...] = middle
    unit, _ = norm_parts(middle)
    second = (unit * vec(5) + vec(6)).astype(BF)
    second_ref[...] = second
    gate_ref[...] = gates(mm(second, w_ref[:, misc_at : misc_at + LANES]), experts)
    slot_of = iota((slots, tokens), 0)
    hot = jnp.where(
        (slot_of == prow_ref[0, 0:1, :]) | (slot_of == prow_ref[0, 1:2, :]), 1.0, 0.0
    ).astype(BF)
    sent = mm(hot, second)
    for e in range(experts):
        send_ref[e] = sent[e * room : (e + 1) * room].astype(BF)


def gates(logits, experts):
    real = iota((1, LANES), 1) < experts
    logits = jnp.where(real, logits, -1e30)
    powers = jnp.where(real, jnp.exp(logits - jnp.max(logits, axis=1, keepdims=True)), 0.0)
    return powers / jnp.sum(powers, axis=1, keepdims=True)


def expert_kernel(cfg, first, last, *refs):
    groups, room, capacity, shift, width = cfg
    meta_ref, buf_ref, dyb_ref, wm_ref, up_ref, ub_ref, down_ref, db_ref = refs[:8]
    refs = refs[8:]
    if not first:
        r_in, gup_in, gdn_in, gb_in, gdb_in = refs[:5]
        refs = refs[6 if last else 5 :]
    r_ref, dbuf_ref, gup_ref, gdn_ref, gb_ref, gdb_ref = refs[:6]
    refs = refs[6:]
    if last:
        lows = refs[:4]
        refs = refs[4:]
    (
        flat_s,
        flatT_s,
        dr_s,
        drT_s,
        racc_s,
        dacc_s,
    ) = refs
    slots = groups * room
    step = pl.program_id(0)
    experts = groups

    @pl.when(step == 0)
    def _():
        flat = buf_ref[...].astype(F32).reshape(slots, width).astype(BF)
        flat_s[...] = flat
        flatT_s[...] = jnp.transpose(flat)
        gate = gates(mm(flat, wm_ref[...]), experts)
        mine = iota((1, LANES), 1) == meta_ref[0]
        mine_gate = jnp.sum(jnp.where(mine, gate, 0.0), axis=1, keepdims=True)
        at = iota((groups, room, 1), 1)
        own = (at >= shift) & (at < shift + capacity)
        dy = jnp.where(own, dyb_ref[...].astype(F32), 0.0)
        dr = (dy.reshape(slots, width) * mine_gate).astype(BF)
        dr_s[...] = dr
        drT_s[...] = jnp.transpose(dr)
        shift_sum = jnp.sum(dr.astype(F32), axis=0, keepdims=True)
        gdb_ref[...] = shift_sum if first else gdb_in[...] + shift_sum
        racc_s[...] = jnp.zeros_like(racc_s)
        dacc_s[...] = jnp.zeros_like(dacc_s)

    flat = flat_s[...]
    dr = dr_s[...]
    hidden = mm(flat, up_ref[0]) + ub_ref[...].astype(F32)
    half_erf = 0.5 * lax.erf(hidden * (0.5**0.5)) + 0.5
    active = (hidden * half_erf).astype(BF)
    slope = half_erf + hidden * (jnp.exp(-0.5 * hidden * hidden) * 0.3989422804014327)
    racc_s[...] += mm(active, down_ref[0])
    grad_pre = mm_nt(dr, down_ref[0]) * slope
    low_pre = grad_pre.astype(BF)
    dacc_s[...] += mm_nt(low_pre, up_ref[0])
    gup = mm(flatT_s[...], low_pre)
    gdn = mm(drT_s[...], active)
    gbias = jnp.sum(low_pre.astype(F32), axis=0, keepdims=True)
    if not first:
        gup = gup_in[...] + gup
        gdn = gdn_in[...] + gdn
        gbias = gb_in[...] + gbias
    gup_ref[...] = gup
    gdn_ref[...] = gdn
    gb_ref[...] = gbias
    if last:
        early = step < pl.num_programs(0) // 2

        @pl.when(early)
        def _():
            lows[0][...] = gup.astype(BF)
            lows[2][...] = gdn.astype(BF)

        @pl.when(jnp.logical_not(early))
        def _():
            lows[1][...] = gup.astype(BF)
            lows[3][...] = gdn.astype(BF)

    @pl.when(step == pl.num_programs(0) - 1)
    def _():
        result = (racc_s[...] + db_ref[...].astype(F32)).astype(BF)
        for e in range(groups):
            block = result[e * room : (e + 1) * room]
            if shift:
                older = iota((8, 1), 0) < shift
                head = jnp.where(older, r_in[e, :8].astype(F32), block[:8].astype(F32))
                r_ref[e, :8] = head.astype(BF)
                r_ref[e, 8:] = block[8:]
            else:
                r_ref[e] = block
        dy = dyb_ref[...].astype(F32).reshape(slots, width)
        dgate = jnp.sum(dy * result.astype(F32), axis=1, keepdims=True).reshape(groups, room, 1)
        spread = jnp.where(
            iota((groups, room, LANES), 2) == iota((groups, room, LANES), 1), dgate, 0.0
        )
        as_row = jnp.sum(spread, axis=1, keepdims=True)
        high = as_row.astype(BF).astype(F32)
        tail = jnp.zeros((groups, 1, width - 2 * LANES), F32)
        as_row = jnp.concatenate([high, as_row - high, tail], axis=2)
        back = dacc_s[...].reshape(groups, room, width)
        back = jnp.where(iota((groups, room, 1), 1) == room - 1, as_row, back).astype(BF)
        for e in range(groups):
            dbuf_ref[e] = back[e]


def backward_kernel(cfg, mb, first, last, *refs):
    images, local_len, seq_count, width, experts, room, capacity = cfg
    (
        meta_ref,
        len_ref,
        dback_ref,
        pcol_ref,
        gate_ref,
        middle_ref,
        second_ref,
        dy_ref,
        oT_ref,
        w_ref,
        q_ref,
        k_ref,
        v_ref,
        lse_ref,
        n1T_ref,
        own_ref,
        oth_ref,
    ) = refs[:17]
    refs = refs[17:]
    if not first:
        g_in, mrow_in = refs[:2]
        refs = refs[2:]
    down_own, down_oth, dm_ref = refs[:3]
    refs = refs[3:]
    if last:
        low_ref = refs[0]
        refs = refs[1:]
    else:
        g_ref = refs[0]
        refs = refs[1:]
    mrow_ref, do_s, dqT_s, dkv_s = refs

    def add_dense(at, value):
        if not first:
            value = g_in[:, at] + value
        if last:
            low_ref[:, at] = value.astype(BF)
        else:
            g_ref[:, at] = value

    full_len = local_len * seq_count
    tokens = images * local_len
    slots = experts * room
    misc_at = 4 * width
    rows = misc_rows(w_ref, misc_at)
    here = meta_ref[1]

    def vec(j):
        return rows[experts + j : experts + j + 1, :]

    dback = dback_ref[...].astype(F32)
    back_rows = dback.reshape(slots, width).astype(BF)
    slot_of = iota((tokens, slots), 1)
    hot = jnp.where(
        (slot_of == pcol_ref[0, :, 0:1]) | (slot_of == pcol_ref[0, :, 1:2]), 1.0, 0.0
    ).astype(BF)
    from_experts = mm(hot, back_rows)
    spare = jnp.where(iota((experts, room, 1), 1) == room - 1, dback[:, :, : 2 * LANES], 0.0)
    spare = jnp.sum(spare, axis=1)
    spare = jnp.concatenate(
        [spare, jnp.zeros((LANES - experts, 2 * LANES), F32)], axis=0
    ).astype(BF)
    lane = iota((tokens, LANES), 1)
    pulled = jnp.zeros((tokens, LANES), F32)
    for k in range(TOP):
        within = jnp.where(lane == pcol_ref[0, :, 4 + k : 5 + k], 1.0, 0.0).astype(BF)
        found = mm_nt(jnp.concatenate([within, within], axis=1), spare)
        pulled = pulled + jnp.where(lane == pcol_ref[0, :, 2 + k : 3 + k], found, 0.0)
    gate = gate_ref[...]
    dlogit = gate * (pulled - jnp.sum(gate * pulled, axis=1, keepdims=True))
    dlogit_low = dlogit.astype(BF)
    mrow_ref[...] = mm(jnp.transpose(dlogit_low.astype(F32)).astype(BF), second_ref[...])
    dn2 = from_experts + mm_nt(dlogit_low, w_ref[:, misc_at : misc_at + LANES])
    unit, scale = norm_parts(middle_ref[...])
    dy = dy_ref[...].reshape(tokens, width).astype(F32)
    dm = dy + norm_pull(unit, scale, vec(5), dn2)
    dm_ref[...] = dm
    da = dm.astype(BF)
    gproj = mm(oT_ref[...], da)
    proj = slice(3 * width, 4 * width)
    add_dense(proj, gproj)
    do_s[...] = mm_nt(da, w_ref[:, proj]).astype(BF)
    half_lane = iota((1, LANES), 1)
    low_half = (half_lane < HD).astype(BF)
    high_half = (half_lane >= HD).astype(BF)
    gqkv = [None, None]
    bias_q = jnp.zeros((1, width), F32)
    bias_v = jnp.zeros((1, width), F32)
    gain_sum = jnp.zeros((1, width), F32)
    shift_sum = jnp.zeros((1, width), F32)
    for b in range(images):
        span = slice(b * local_len, (b + 1) * local_len)
        wide = slice(b * full_len, (b + 1) * full_len)
        kpos = iota((full_len, 1), 0)
        shift = jnp.zeros((full_len, 1), jnp.int32)
        for j in range(seq_count):
            origin = lax.rem(here + j, seq_count) * local_len - j * local_len
            shift = jnp.where(kpos >= j * local_len, origin, shift)
        valid = (kpos + shift) < len_ref[mb * images + b]

        def heads(blk, carry):
            at = pl.ds(pl.multiple_of(blk * LANES, LANES), LANES)
            q_blk = q_ref[span, at]
            k_blk = k_ref[wide, at]
            v_blk = v_ref[wide, at]
            do_blk = do_s[span, at]
            kT_blk = jnp.transpose(k_blk)
            dvs = []
            dks = []
            dqs = []
            for side, keep in enumerate((low_half, high_half)):
                scores = mm_nt(k_blk, q_blk * keep)
                logs = lse_ref[pl.ds(b * 8 + 2 * blk + side, 1), :]
                probs = jnp.where(valid, jnp.exp(scores - logs), 0.0)
                dprobs = mm_nt(v_blk, do_blk * keep)
                inner = jnp.sum(probs * dprobs, axis=0, keepdims=True)
                dscores = (probs * (dprobs - inner)).astype(BF)
                dvs.append(mm(probs.astype(BF), do_blk))
                dks.append(mm(dscores, q_blk))
                dqs.append(mm(kT_blk[side * HD : (side + 1) * HD], dscores))
            dqT_s[pl.ds(pl.multiple_of(blk * LANES, LANES), HD), :] = dqs[0]
            dqT_s[pl.ds(pl.multiple_of(blk * LANES + HD, HD), HD), :] = dqs[1]
            left = half_lane < HD
            dkv_s[:, at] = jnp.where(left, dks[0], dks[1]).astype(BF)
            vat = pl.ds(pl.multiple_of(width + blk * LANES, LANES), LANES)
            dkv_s[:, vat] = jnp.where(left, dvs[0], dvs[1]).astype(BF)
            return carry

        lax.fori_loop(0, width // LANES, heads, 0)
        dq = (jnp.transpose(dqT_s[...]) * HD**-0.5).astype(BF)
        dkv = dkv_s[...]
        part_q = mm(n1T_ref[:, b * full_len : b * full_len + local_len], dq)
        part_kv = mm(n1T_ref[:, wide], dkv)
        gqkv[0] = part_q if b == 0 else gqkv[0] + part_q
        gqkv[1] = part_kv if b == 0 else gqkv[1] + part_kv
        bias_q = bias_q + jnp.sum(dq.astype(F32), axis=0, keepdims=True)
        bias_v = bias_v + jnp.sum(dkv[:, width:].astype(F32), axis=0, keepdims=True)
        down = mm_nt(dkv, w_ref[:, width : 3 * width])
        down_own[span, :] = mm_nt(dq, w_ref[:, :width])
        down_own[span, :] += down[:local_len]
        for j in range(seq_count):
            part = down_own[span, :] if j == 0 else down[j * local_len : (j + 1) * local_len]
            tokens_in = own_ref[b] if j == 0 else oth_ref[j - 1, b]
            first_unit, _ = norm_parts(tokens_in.astype(F32))
            gain_sum = gain_sum + jnp.sum(part * first_unit, axis=0, keepdims=True)
            shift_sum = shift_sum + jnp.sum(part, axis=0, keepdims=True)
            if j > 0:
                down_oth[j - 1, span, :] = part.astype(BF)
    add_dense(slice(0, width), gqkv[0])
    add_dense(slice(width, 3 * width), gqkv[1])
    row = iota((LANES, 1), 0)
    mrow = jnp.where(row < experts, mrow_ref[...], 0.0)
    sums = (
        gain_sum,
        shift_sum,
        bias_q,
        bias_v,
        jnp.sum(da.astype(F32), axis=0, keepdims=True),
        jnp.sum(dn2 * unit, axis=0, keepdims=True),
        jnp.sum(dn2, axis=0, keepdims=True),
    )
    for j, value in enumerate(sums):
        mrow = jnp.where(row == experts + j, value, mrow)
    if not first:
        mrow = mrow_in[...] + mrow
    mrow_ref[...] = mrow
    if last:
        low_ref[:, misc_at : misc_at + LANES] = jnp.transpose(mrow).astype(BF)


def input_kernel(cfg, own_ref, got_ref, x_ref, dm_ref, wm_ref, *refs):
    out_ref = refs[-1]
    images, local_len, seq_count, width, experts = cfg
    tokens = images * local_len
    rows = jnp.transpose(wm_ref[...].astype(F32))
    dn1 = own_ref[...]
    for j in range(seq_count - 1):
        dn1 = dn1 + got_ref[j].astype(F32)
    unit, scale = norm_parts(x_ref[...].reshape(tokens, width).astype(F32))
    grad = dm_ref[...] + norm_pull(unit, scale, rows[experts : experts + 1, :], dn1)
    out_ref[...] = grad.astype(BF).reshape(images, local_len, width)


def mix_kernel(cfg, back_ref, pcol_ref, *refs):
    for mb in range(MICRO):

        @pl.when(pl.program_id(0) == mb)
        def _():
            mix_part(cfg, back_ref, pcol_ref, refs[2 * mb], refs[2 * mb + 1], refs[-1])


def mix_part(cfg, back_ref, pcol_ref, gate_ref, middle_ref, out_ref):
    images, local_len, width, experts, room = cfg
    tokens = images * local_len
    slots = experts * room
    back = back_ref[...].astype(F32).reshape(slots, width).astype(BF)
    slot_of = iota((tokens, slots), 1)
    lane = iota((tokens, LANES), 1)
    gate = gate_ref[...]
    total = middle_ref[...]
    for k in range(TOP):
        hot = jnp.where(slot_of == pcol_ref[0, :, k : k + 1], 1.0, 0.0).astype(BF)
        chosen = jnp.where(lane == pcol_ref[0, :, 2 + k : 3 + k], gate, 0.0)
        total = total + jnp.sum(chosen, axis=1, keepdims=True) * mm(hot, back)
    out_ref[...] = total.astype(BF).reshape(images, local_len, width)


def sum_kernel(gup_ref, gdn_ref, up_early, up_late, dn_early, dn_late, up_ref, dn_ref):
    late = pl.program_id(0) >= pl.num_programs(0) // 2
    got_up = jnp.where(late, up_late[...], up_early[...])
    got_dn = jnp.where(late, dn_late[...], dn_early[...])
    up_ref[0] = gup_ref[...] + got_up.astype(F32)
    dn_ref[0] = jnp.transpose(gdn_ref[...] + got_dn.astype(F32))


def smem_spec():
    return pl.BlockSpec(memory_space=pltpu.SMEM)


def params():
    return pltpu.CompilerParams(vmem_limit_bytes=VMEM_LIMIT)


def cost(micros):
    return pl.CostEstimate(
        flops=int(micros * 1e9), transcendentals=0, bytes_accessed=int(micros * 2e6)
    )


def struct(shape, kind):
    return jax.ShapeDtypeStruct(shape, kind)


def after(value, *others):
    return lax.optimization_barrier((value, *others))[0]


def on_device(
    images,
    cotangent,
    lengths,
    routes,
    attn_norm_gain,
    attn_norm_bias,
    qkv_weight,
    query_value_bias,
    proj_weight,
    proj_bias,
    moe_norm_gain,
    moe_norm_bias,
    router_weight,
    up_weight,
    up_bias,
    down_weight,
    down_bias,
):
    seq_count = lax.axis_size("seq")
    dp_count = lax.axis_size("dp")
    count = images.shape[0] // MICRO
    local_len = images.shape[1]
    width = images.shape[2]
    tokens = count * local_len
    full_len = local_len * seq_count
    experts = router_weight.shape[1]
    hidden = up_weight.shape[2]
    capacity = (5 * tokens * TOP + 4 * experts - 1) // (4 * experts)
    room = (capacity + window(capacity, MICRO - 1)[1] + 8) // 8 * 8
    assert all(window(capacity, mb)[1] + capacity < room for mb in range(MICRO))
    assert window(capacity, 1)[0] + room <= window(capacity, 2)[0] + 8
    slots = experts * room
    assert up_weight.shape[0] == 1 and experts == dp_count
    assert experts + VEC <= LANES and capacity <= LANES
    meta = jnp.stack([lax.axis_index("dp"), lax.axis_index("seq")]).astype(jnp.int32)
    packed_width = 4 * width + LANES

    def full(shape):
        return pl.BlockSpec(shape, lambda i: (0,) * len(shape))

    def token_spec(mb):
        return pl.BlockSpec((count, local_len, width), lambda i: (mb, 0, 0))

    def table_spec(mb, shape):
        return pl.BlockSpec((1, *shape), lambda i: (mb, 0, 0))

    def block_spec(mb):
        return pl.BlockSpec((experts, room, width), lambda i: (0, mb, 0))

    def window_spec(mb=None):
        def at(i):
            return (0, (capacity * (i if mb is None else mb)) // 8 * 8, 0)

        return pl.BlockSpec((pl.Element(experts), pl.Element(room), pl.Element(width)), at)

    any_spec = pl.BlockSpec(memory_space=pl.ANY)
    other_spec = lambda mb: pl.BlockSpec(
        (seq_count - 1, count, local_len, width), lambda i: (0, max(mb - 1, 0), 0, 0)
    )
    halved = hidden // FF_BLOCK // 2
    early_spec = lambda: pl.BlockSpec(
        (width, FF_BLOCK), lambda i: (0, jnp.minimum(i, halved - 1))
    )
    late_spec = lambda: pl.BlockSpec(
        (width, FF_BLOCK), lambda i: (0, jnp.maximum(i - halved, 0))
    )
    misc_spec = pl.BlockSpec((width, LANES), lambda i: (0, 4 * width // LANES))
    moved = struct((experts, room, width), BF)
    merged = struct((experts, window(capacity, MICRO - 1)[0] + room, width), BF)
    tailed = struct((experts, (MICRO - 1) * room, width), BF)

    def seq_shift(array, j):
        return lax.ppermute(array, "seq", [((i + j) % seq_count, i) for i in range(seq_count)])

    others = []
    for part in (images[:count], images[count:]):
        moved_images = jnp.stack([seq_shift(part, j) for j in range(1, seq_count)])
        others.append(moved_images)

    sent_dy, prow, pcol = pl.pallas_call(
        functools.partial(place_kernel, experts, room, capacity),
        grid=(MICRO,),
        in_specs=[
            pl.BlockSpec((1, 1, 1, TOP, tokens), lambda i: (0, i, 0, 0, 0)),
            pl.BlockSpec((count, local_len, width), lambda i: (i, 0, 0)),
        ],
        out_specs=[
            pl.BlockSpec(merged.shape, lambda i: (0, 0, 0)),
            pl.BlockSpec((1, TOP, tokens), lambda i: (i, 0, 0)),
            pl.BlockSpec((1, tokens, 8), lambda i: (i, 0, 0)),
        ],
        out_shape=[
            merged,
            struct((MICRO, TOP, tokens), jnp.int32),
            struct((MICRO, tokens, 8), jnp.int32),
        ],
        compiler_params=params(),
        cost_estimate=cost(8),
        name="place",
    )(jnp.swapaxes(routes, 3, 4), cotangent)

    vectors = jnp.concatenate(
        [
            jnp.stack([attn_norm_gain, attn_norm_bias]),
            query_value_bias,
            jnp.stack([proj_bias, moe_norm_gain, moe_norm_bias, jnp.zeros_like(proj_bias)]),
        ],
        axis=0,
    )
    shard = router_weight.shape[0]
    bits = dp_count.bit_length() - 1
    assert dp_count == 1 << bits

    def across(value, offset):
        return lax.ppermute(value, "dp", [(i, i ^ offset) for i in range(dp_count)])

    def gather_rows(own, gate):
        quarter = dp_count // 4
        pieces = [own, *[across(own, k * quarter) for k in (1, 2, 3)]]
        held = [jnp.stack(pieces)]
        offsets = [[0, quarter, 2 * quarter, 3 * quarter]]
        for bit in reversed(range(bits - 2)):
            if bit == 0:
                held[-1] = after(held[-1], gate)
            held += [across(h, 1 << bit) for h in held]
            offsets += [[k ^ (1 << bit) for k in known] for known in offsets]
        return pl.pallas_call(
            functools.partial(assemble_kernel, offsets, shard),
            grid=(1,),
            in_specs=[smem_spec(), *[full(h.shape) for h in held]],
            out_specs=full((dp_count * shard, packed_width)),
            out_shape=struct((dp_count * shard, packed_width), BF),
            compiler_params=params(),
            cost_estimate=cost(3),
            name="assemble",
        )(meta, *held), pieces[1:]

    def scatter_rows(total, far):
        me = lax.axis_index("dp")
        value = total.reshape(dp_count // 2, 2, shard, packed_width)
        for bit in range(bits - 2):
            mine = lax.bitwise_and(lax.shift_right_logical(me, bit), 1)
            keep = lax.dynamic_index_in_dim(value, mine, 1, keepdims=False)
            give = lax.dynamic_index_in_dim(value, 1 - mine, 1, keepdims=False)
            give = give.astype(BF)
            value = keep.astype(F32) + across(give, 1 << bit).astype(F32)
            if bit == 0:
                mid = value
            if bit < bits - 3:
                value = value.reshape(-1, 2, shard, packed_width)
        value = after(value, *far)
        high = lax.shift_right_logical(me, bits - 2)
        result = lax.dynamic_index_in_dim(value, high, 0, keepdims=False)
        for offset in (1, 2, 3):
            give = lax.dynamic_index_in_dim(
                value, lax.bitwise_xor(high, offset), 0, keepdims=False
            )
            result = result + across(give.astype(BF), offset << (bits - 2)).astype(F32)
        return result, mid, value

    pack_args = (qkv_weight, proj_weight, router_weight.T, vectors)
    packed_shard = pl.pallas_call(
        functools.partial(pack_kernel, experts),
        grid=(1,),
        in_specs=[full(a.shape) for a in pack_args],
        out_specs=full((shard, packed_width)),
        out_shape=struct((shard, packed_width), BF),
        compiler_params=params(),
        cost_estimate=cost(1),
        name="pack",
    )(*pack_args)

    def exchange(array):
        return lax.all_to_all(array, "dp", split_axis=0, concat_axis=0, tiled=True)

    packed, near = gather_rows(packed_shard, others[1])
    dyb = exchange(after(sent_dy, *near, others[0]))

    def forward(mb):
        cfg = (count, local_len, seq_count, width, experts, room)
        outs = [
            ((experts, room, width), BF),
            ((tokens, width), F32),
            ((tokens, LANES), F32),
            ((tokens, width), BF),
            ((width, tokens), BF),
            ((tokens, width), BF),
            ((count * full_len, width), BF),
            ((count * full_len, width), BF),
            ((count * 8, local_len), F32),
            ((width, count * full_len), BF),
        ]
        return pl.pallas_call(
            functools.partial(forward_kernel, cfg, mb),
            grid=(1,),
            in_specs=[
                smem_spec(),
                smem_spec(),
                token_spec(mb),
                other_spec(mb),
                full((width, packed_width)),
                table_spec(mb, (TOP, tokens)),
            ],
            out_specs=[full(s) for s, _ in outs],
            out_shape=[struct(s, k) for s, k in outs],
            scratch_shapes=[
                pltpu.VMEM((tokens, width), BF),
                pltpu.VMEM((local_len, LANES), F32),
            ],
            compiler_params=params(),
            cost_estimate=cost(11),
            name="forward",
        )(meta, lengths, images, others[min(mb, 1)], packed, prow)

    def expert(mb, buf, results, tail_back, totals):
        first = mb == 0
        last = mb == MICRO - 1
        cfg = (experts, room, capacity, window(capacity, mb)[1], width)
        wide = lambda: pl.BlockSpec((width, FF_BLOCK), lambda i: (0, i))
        thin = lambda: pl.BlockSpec((1, FF_BLOCK), lambda i: (0, i))
        in_specs = [
            smem_spec(),
            full((experts, room, width)),
            window_spec(mb),
            misc_spec,
            pl.BlockSpec((1, width, FF_BLOCK), lambda i: (0, 0, i)),
            thin(),
            pl.BlockSpec((1, FF_BLOCK, width), lambda i: (0, i, 0)),
            full((1, width)),
        ]
        total_specs = [wide(), wide(), thin(), full((1, width))]
        args = [meta, buf, dyb, packed, up_weight, up_bias, down_weight, down_bias]
        aliases = {}
        if not first:
            aliases = {len(args): 0}
            aliases.update({len(args) + 1 + j: 2 + j for j in range(4)})
            in_specs += [window_spec(mb), *total_specs]
            args += [results, *totals]
        if mb >= 2:
            aliases[len(args)] = 1
            in_specs += [any_spec]
            args += [tail_back]
        outs = pl.pallas_call(
            functools.partial(expert_kernel, cfg, first, last),
            grid=(hidden // FF_BLOCK,),
            in_specs=in_specs,
            out_specs=[window_spec(mb), block_spec(max(mb - 1, 0)), *total_specs]
            + ([early_spec(), late_spec()] * 2 if last else []),
            out_shape=[
                merged,
                moved if first else tailed,
                struct((width, hidden), F32),
                struct((width, hidden), F32),
                struct((1, hidden), F32),
                struct((1, width), F32),
            ]
            + ([struct((width, hidden // 2), BF)] * 4 if last else []),
            scratch_shapes=[
                pltpu.VMEM((slots, width), BF),
                pltpu.VMEM((width, slots), BF),
                pltpu.VMEM((slots, width), BF),
                pltpu.VMEM((width, slots), BF),
                pltpu.VMEM((slots, width), F32),
                pltpu.VMEM((slots, width), F32),
            ],
            input_output_aliases=aliases,
            compiler_params=params(),
            cost_estimate=cost(19),
            name="expert",
        )(*args)
        return outs[0], outs[1], tuple(outs[2:])

    def backward(mb, dback, saved, totals):
        first = mb == 0
        last = mb == MICRO - 1
        cfg = (count, local_len, seq_count, width, experts, room, capacity)
        middle, gate, second, oT, q, k, v, lse, n1T = saved
        whole = [gate, middle, second]
        heads = [oT, packed, q, k, v, lse, n1T]
        args = [meta, lengths, dback, pcol, *whole, cotangent, *heads, images, others[min(mb, 1)]]
        in_specs = [
            smem_spec(),
            smem_spec(),
            block_spec(max(mb - 1, 0)),
            table_spec(mb, (tokens, 8)),
            *[full(a.shape) for a in whole],
            token_spec(mb),
            *[full(a.shape) for a in heads],
            token_spec(mb),
            other_spec(mb),
        ]
        aliases = {}
        if not first:
            in_specs += [full(a.shape) for a in totals]
            args += list(totals)
            if not last:
                aliases = {len(args) - 2: 3, len(args) - 1: 4}
        outs = [
            ((tokens, width), F32),
            ((seq_count - 1, tokens, width), BF),
            ((tokens, width), F32),
            ((width, packed_width), BF) if last else ((width, 4 * width), F32),
            ((LANES, width), F32),
        ]
        return pl.pallas_call(
            functools.partial(backward_kernel, cfg, mb, first, last),
            grid=(1,),
            in_specs=in_specs,
            out_specs=[full(s) for s, _ in outs],
            out_shape=[struct(s, t) for s, t in outs],
            scratch_shapes=[
                pltpu.VMEM((tokens, width), BF),
                pltpu.VMEM((width, local_len), F32),
                pltpu.VMEM((full_len, 2 * width), BF),
            ],
            input_output_aliases=aliases,
            compiler_params=params(),
            cost_estimate=cost(1 if last else 17),
            name="backward",
        )(*args)

    def into(kernel, mb, args, specs, previous, micros, name):
        aliases = {}
        if previous is not None:
            aliases = {len(args): 0}
            args = [*args, previous]
            specs = [*specs, any_spec]
        return pl.pallas_call(
            kernel,
            grid=(1,),
            in_specs=specs,
            out_specs=token_spec(mb),
            out_shape=struct(images.shape, BF),
            input_output_aliases=aliases,
            compiler_params=params(),
            cost_estimate=cost(micros),
            name=name,
        )(*args)

    def finish(mb, own, got, dm, previous):
        cfg = (count, local_len, seq_count, width, experts)
        specs = [full(own.shape), full(got.shape), token_spec(mb), full(dm.shape), misc_spec]
        return into(
            functools.partial(input_kernel, cfg),
            mb,
            [own, got, images, dm, packed],
            specs,
            previous,
            3,
            "finish",
        )

    def mix(back):
        cfg = (count, local_len, width, experts, room)
        tables = sum([[saved[mb][1], saved[mb][0]] for mb in range(MICRO)], [])
        return pl.pallas_call(
            functools.partial(mix_kernel, cfg),
            grid=(MICRO,),
            in_specs=[
                window_spec(),
                pl.BlockSpec((1, tokens, 8), lambda i: (i, 0, 0)),
                *[full(t.shape) for t in tables],
            ],
            out_specs=pl.BlockSpec((count, local_len, width), lambda i: (i, 0, 0)),
            out_shape=struct(images.shape, BF),
            compiler_params=params(),
            cost_estimate=cost(7),
            name="mix",
        )(back, pcol, *tables)

    swap = [(i, (i + 1) % seq_count) for i in range(seq_count)]

    def seq_sum(value):
        if seq_count == 2:
            return value + lax.ppermute(value.astype(BF), "seq", swap).astype(F32)
        return lax.psum(value.astype(BF), "seq").astype(F32)

    passed = [forward(mb) for mb in range(MICRO)]
    saved = [outs[1:] for outs in passed]
    bufs = []
    for mb in range(MICRO):
        first_gate = (dyb,) if mb == 0 else ()
        bufs.append(exchange(after(passed[mb][0], *first_gate)))
    totals = None
    results = None
    ready = [None, None]
    for mb in range(MICRO):
        results, ready[min(mb, 1)], totals = expert(mb, bufs[mb], results, ready[1], totals)
    gup, gdn, gbias, gdbias, *pieces = totals
    arrived = []
    if seq_count == 2:
        arrived = [lax.ppermute(piece, "seq", swap) for piece in pieces]
    dense = None
    owns = []
    gots = []
    dms = []
    dbacks = [exchange(ready[0]), exchange(ready[1])]
    if arrived:
        dbacks[1], arrived[0] = lax.optimization_barrier((dbacks[1], arrived[0]))
    for mb in range(MICRO):
        dback = dbacks[min(mb, 1)]
        if mb == 2 and arrived:
            dense, arrived[1] = lax.optimization_barrier((dense, arrived[1]))
        own, oth, dm, *dense = backward(mb, dback, saved[mb], dense)
        owns.append(own)
        dms.append(dm)
        gots.append(
            jnp.stack(
                [
                    lax.ppermute(
                        oth[j - 1], "seq", [(i, (i + j) % seq_count) for i in range(seq_count)]
                    )
                    for j in range(1, seq_count)
                ]
            )
        )
    back = exchange(after(results, dbacks[1]))
    first, far = (), ()
    if arrived:
        first, far = (arrived[2], arrived[3]), (gots[0], gots[1])
    shards, mid, late = scatter_rows(after(dense[0], *first), (*far, back))
    owns = [after(own, late if mb == MICRO - 1 else mid) for mb, own in enumerate(owns)]
    grads = None
    for mb in range(MICRO):
        grads = finish(mb, owns[mb], gots[mb], dms[mb], grads)
    out = mix(back)

    if seq_count == 2:
        wide = lambda: pl.BlockSpec((width, FF_BLOCK), lambda i: (0, i))
        final_up, final_down = pl.pallas_call(
            sum_kernel,
            grid=(hidden // FF_BLOCK,),
            in_specs=[wide(), wide(), *[early_spec(), late_spec()] * 2],
            out_specs=[
                pl.BlockSpec((1, width, FF_BLOCK), lambda i: (0, 0, i)),
                pl.BlockSpec((1, FF_BLOCK, width), lambda i: (0, i, 0)),
            ],
            out_shape=[struct((1, width, hidden), F32), struct((1, hidden, width), F32)],
            compiler_params=params(),
            cost_estimate=cost(8),
            name="sum_experts",
        )(after(gup, mid), gdn, *arrived)
    else:
        sums = [lax.psum(piece, "seq").astype(F32) for piece in pieces]
        final_up = jnp.concatenate(sums[:2], axis=1)[None]
        final_down = jnp.swapaxes(jnp.concatenate(sums[2:], axis=1), 0, 1)[None]
    biases = seq_sum(jnp.concatenate([gbias, gdbias], axis=1))
    final_up_shift = biases[:, :hidden]
    final_down_shift = biases[:, hidden:]

    shards = seq_sum(shards)
    misc = 4 * width + experts
    return (
        out,
        grads,
        shards[:, misc],
        shards[:, misc + 1],
        shards[:, : 3 * width],
        jnp.stack([shards[:, misc + 2], shards[:, misc + 3]]),
        shards[:, 3 * width : 4 * width],
        shards[:, misc + 4],
        shards[:, misc + 5],
        shards[:, misc + 6],
        shards[:, 4 * width : misc],
        final_up,
        final_up_shift,
        final_down,
        final_down_shift,
    )


def solution(mesh):
    return jax.shard_map(
        on_device,
        mesh=mesh,
        in_specs=(
            P("dp", "seq", None),
            P("dp", "seq", None),
            P("dp"),
            P("dp", None, "seq", None, None),
            P("dp"),
            P("dp"),
            P("dp", None),
            P(None, "dp"),
            P("dp", None),
            P("dp"),
            P("dp"),
            P("dp"),
            P("dp", None),
            P("dp", None, None),
            P("dp", None),
            P("dp", None, None),
            P("dp", None),
        ),
        out_specs=(
            P("dp", "seq", None),
            P("dp", "seq", None),
            P("dp"),
            P("dp"),
            P("dp", None),
            P(None, "dp"),
            P("dp", None),
            P("dp"),
            P("dp"),
            P("dp"),
            P("dp", None),
            P("dp", None, None),
            P("dp", None),
            P("dp", None, None),
            P("dp", None),
        ),
        check_vma=False,
    )
```

```python
import functools

import jax
import jax.numpy as jnp
from jax import lax
from jax.experimental import pallas as pl
from jax.experimental.pallas import tpu as pltpu
from jax.sharding import PartitionSpec as P

HD = 64
TOP = 2
MICRO = 3
BF = jnp.bfloat16
F32 = jnp.float32
EPS = 1e-06
LANES = 128
VEC = 8
FF_BLOCK = 512
UP_PIECES = ((0, 2), (2, 4))
DOWN_PIECES = ((0, 2), (2, 3), (3, 4))
PIECES = UP_PIECES + DOWN_PIECES
VMEM_LIMIT = 60 * 1024 * 1024


def mm(left, right):
    return jnp.dot(left, right, preferred_element_type=F32)


def mm_nt(left, right):
    return lax.dot_general(
        left, right, (((1,), (1,)), ((), ())), preferred_element_type=F32
    )


def iota(shape, dim):
    return lax.broadcasted_iota(jnp.int32, shape, dim)


def norm_parts(values):
    average = jnp.mean(values, axis=-1, keepdims=True)
    centred = values - average
    spread = jnp.mean(centred * centred, axis=-1, keepdims=True)
    scale = lax.rsqrt(spread + EPS)
    return centred * scale, scale


def norm_pull(unit, scale, gain, cotangent):
    inner = cotangent * gain
    mean_inner = jnp.mean(inner, axis=-1, keepdims=True)
    mean_unit = jnp.mean(inner * unit, axis=-1, keepdims=True)
    return scale * (inner - mean_inner - unit * mean_unit)


def misc_rows(w_ref, start):
    return jnp.transpose(w_ref[:, start : start + LANES].astype(F32))


def pack_kernel(experts, qkv_ref, proj_ref, router_ref, vec_ref, out_ref):
    width = proj_ref.shape[1]
    shard = proj_ref.shape[0]
    out_ref[:, : 3 * width] = qkv_ref[...]
    out_ref[:, 3 * width : 4 * width] = proj_ref[...]
    rows = jnp.concatenate([router_ref[...].astype(F32), vec_ref[...].astype(F32)], axis=0)
    columns = jnp.transpose(rows)
    tail = jnp.zeros((shard, LANES - columns.shape[1]), F32)
    out_ref[:, 4 * width :] = jnp.concatenate([columns, tail], axis=1).astype(BF)


def assemble_kernel(sources, shard, meta_ref, *refs):
    out_ref = refs[-1]
    for ref, offsets in zip(refs[:-1], sources):
        for at, offset in enumerate(offsets):
            row = jnp.bitwise_xor(meta_ref[0], offset) * shard
            out_ref[pl.ds(pl.multiple_of(row, shard), shard), :] = ref[at]


def window(capacity, mb):
    start = capacity * mb // 8 * 8
    return start, capacity * mb - start


def place_kernel(experts, room, capacity, routes_ref, dy_ref, send_ref, prow_ref, pcol_ref):
    for mb in range(MICRO):

        @pl.when(pl.program_id(0) == mb)
        def _():
            place_part(
                experts, room, window(capacity, mb), routes_ref, dy_ref, send_ref, prow_ref, pcol_ref
            )


def place_part(experts, room, where, routes_ref, dy_ref, send_ref, prow_ref, pcol_ref):
    start, shift = where
    tokens = routes_ref.shape[4]
    slots = experts * room
    rows = routes_ref[0, 0, 0]
    first_row = rows[0:1]
    second_row = rows[1:2]
    tall = jnp.concatenate([rows.astype(F32), jnp.zeros((LANES - TOP, tokens), F32)], axis=0)
    cols = jnp.transpose(tall)[:, 0:8].astype(jnp.int32)
    hot_first = (iota((experts, tokens), 0) == first_row).astype(F32)
    hot_second = (iota((experts, tokens), 0) == second_row).astype(F32)
    earlier = (iota((tokens, tokens), 0) < iota((tokens, tokens), 1)).astype(BF)
    before = mm((hot_first + hot_second).astype(BF), earlier)
    in_first = jnp.sum(before * hot_first, axis=0, keepdims=True).astype(jnp.int32)
    in_second = jnp.sum((before + hot_first) * hot_second, axis=0, keepdims=True).astype(jnp.int32)
    place_first = first_row * room + in_first + shift
    place_second = second_row * room + in_second + shift
    prow_ref[0, 0:1, :] = place_first
    prow_ref[0, 1:2, :] = place_second
    slot_of = iota((slots, tokens), 0)
    hot = jnp.where((slot_of == place_first) | (slot_of == place_second), 1.0, 0.0).astype(BF)
    flat = dy_ref[...].reshape(tokens, dy_ref.shape[-1])
    rows = mm(hot, flat)
    for e in range(experts):
        block = rows[e * room : (e + 1) * room].astype(BF)
        if shift:
            send_ref[e, start : start + 8] = send_ref[e, start : start + 8] + block[:8]
            send_ref[e, start + 8 : start + room] = block[8:]
        else:
            send_ref[e, start : start + room] = block
    first_col = cols[:, 0:1]
    second_col = cols[:, 1:2]
    hot_first = (iota((tokens, experts), 1) == first_col).astype(F32)
    hot_second = (iota((tokens, experts), 1) == second_col).astype(F32)
    later = (iota((tokens, tokens), 1) < iota((tokens, tokens), 0)).astype(BF)
    before = mm(later, (hot_first + hot_second).astype(BF))
    in_first = jnp.sum(before * hot_first, axis=1, keepdims=True).astype(jnp.int32)
    in_second = jnp.sum((before + hot_first) * hot_second, axis=1, keepdims=True).astype(jnp.int32)
    lane = iota((tokens, 8), 1)
    table = jnp.zeros((tokens, 8), jnp.int32)
    for at, col in enumerate(
        (
            first_col * room + in_first + shift,
            second_col * room + in_second + shift,
            first_col,
            second_col,
            in_first + shift,
            in_second + shift,
        )
    ):
        table = jnp.where(lane == at, col, table)
    pcol_ref[0] = table


def forward_kernel(
    cfg,
    mb,
    meta_ref,
    len_ref,
    own_ref,
    oth_ref,
    w_ref,
    prow_ref,
    send_ref,
    middle_ref,
    gate_ref,
    second_ref,
    oT_ref,
    q_ref,
    k_ref,
    v_ref,
    lse_ref,
    n1T_ref,
    att_ref,
    logs_ref,
):
    images, local_len, seq_count, width, experts, room = cfg
    full_len = local_len * seq_count
    tokens = images * local_len
    slots = experts * room
    misc_at = 4 * width
    rows = misc_rows(w_ref, misc_at)

    def vec(j):
        return rows[experts + j : experts + j + 1, :]

    here = meta_ref[1]
    lane = iota((1, LANES), 1)
    low_half = (lane < HD).astype(BF)
    high_half = (lane >= HD).astype(BF)
    for b in range(images):
        blocks = [own_ref[b]] + [oth_ref[j, b] for j in range(seq_count - 1)]
        full = jnp.concatenate(blocks, axis=0).astype(F32)
        unit, _ = norm_parts(full)
        normed = (unit * vec(0) + vec(1)).astype(BF)
        n1T_ref[:, b * full_len : (b + 1) * full_len] = jnp.transpose(normed)
        span = slice(b * local_len, (b + 1) * local_len)
        wide = slice(b * full_len, (b + 1) * full_len)
        queries = (mm(normed[:local_len], w_ref[:, :width]) + vec(2)).astype(BF)
        q_ref[span, :] = queries * jnp.asarray(HD**-0.5, BF)
        k_ref[wide, :] = mm(normed, w_ref[:, width : 2 * width]).astype(BF)
        v_ref[wide, :] = (mm(normed, w_ref[:, 2 * width : 3 * width]) + vec(3)).astype(BF)
        kpos = iota((1, full_len), 1)
        shift = jnp.zeros((1, full_len), jnp.int32)
        for j in range(seq_count):
            origin = lax.rem(here + j, seq_count) * local_len - j * local_len
            shift = jnp.where(kpos >= j * local_len, origin, shift)
        valid = (kpos + shift) < len_ref[mb * images + b]
        logs_ref[...] = jnp.zeros_like(logs_ref)

        def heads(blk, carry):
            at = pl.ds(pl.multiple_of(blk * LANES, LANES), LANES)
            q_blk = q_ref[span, at]
            k_blk = k_ref[wide, at]
            v_blk = v_ref[wide, at]
            outs = []
            for side, keep in enumerate((low_half, high_half)):
                scores = mm_nt(q_blk * keep, k_blk)
                scores = jnp.where(valid, scores, -1e30)
                highest = jnp.max(scores, axis=1, keepdims=True)
                powers = jnp.exp(scores - highest)
                total = jnp.sum(powers, axis=1, keepdims=True)
                probs = (powers * (1.0 / total)).astype(BF)
                outs.append(mm(probs, v_blk))
                logs_ref[...] = jnp.where(
                    lane == 2 * blk + side, highest + jnp.log(total), logs_ref[...]
                )
            att_ref[span, at] = jnp.where(lane < HD, outs[0], outs[1]).astype(BF)
            return carry

        lax.fori_loop(0, width // LANES, heads, 0)
        lse_ref[b * 8 : b * 8 + 8, :] = jnp.transpose(logs_ref[...])[0:8, :]
    attended = att_ref[...]
    oT_ref[...] = jnp.transpose(attended)
    branch = mm(attended, w_ref[:, 3 * width : 4 * width]) + vec(4)
    middle = own_ref[...].reshape(tokens, width).astype(F32) + branch
    middle_ref[...] = middle
    unit, _ = norm_parts(middle)
    second = (unit * vec(5) + vec(6)).astype(BF)
    second_ref[...] = second
    gate_ref[...] = gates(mm(second, w_ref[:, misc_at : misc_at + LANES]), experts)
    slot_of = iota((slots, tokens), 0)
    hot = jnp.where(
        (slot_of == prow_ref[0, 0:1, :]) | (slot_of == prow_ref[0, 1:2, :]), 1.0, 0.0
    ).astype(BF)
    sent = mm(hot, second)
    for e in range(experts):
        send_ref[e] = sent[e * room : (e + 1) * room].astype(BF)


def gates(logits, experts):
    real = iota((1, LANES), 1) < experts
    logits = jnp.where(real, logits, -1e30)
    powers = jnp.where(real, jnp.exp(logits - jnp.max(logits, axis=1, keepdims=True)), 0.0)
    return powers / jnp.sum(powers, axis=1, keepdims=True)


def expert_kernel(cfg, first, last, *refs):
    groups, room, capacity, shift, width = cfg
    meta_ref, buf_ref, dyb_ref, wm_ref, up_ref, ub_ref, down_ref, db_ref = refs[:8]
    refs = refs[8:]
    if not first:
        r_in, gup_in, gdn_in, gb_in, gdb_in = refs[:5]
        refs = refs[6 if last else 5 :]
    r_ref, dbuf_ref, gup_ref, gdn_ref, gb_ref, gdb_ref = refs[:6]
    refs = refs[6:]
    if last:
        lows = refs[: len(PIECES)]
        refs = refs[len(PIECES) :]
    (
        flat_s,
        flatT_s,
        dr_s,
        drT_s,
        racc_s,
        dacc_s,
    ) = refs
    slots = groups * room
    step = pl.program_id(0)
    experts = groups

    @pl.when(step == 0)
    def _():
        flat = buf_ref[...].astype(F32).reshape(slots, width).astype(BF)
        flat_s[...] = flat
        flatT_s[...] = jnp.transpose(flat)
        gate = gates(mm(flat, wm_ref[...]), experts)
        mine = iota((1, LANES), 1) == meta_ref[0]
        mine_gate = jnp.sum(jnp.where(mine, gate, 0.0), axis=1, keepdims=True)
        at = iota((groups, room, 1), 1)
        own = (at >= shift) & (at < shift + capacity)
        dy = jnp.where(own, dyb_ref[...].astype(F32), 0.0)
        dr = (dy.reshape(slots, width) * mine_gate).astype(BF)
        dr_s[...] = dr
        drT_s[...] = jnp.transpose(dr)
        shift_sum = jnp.sum(dr.astype(F32), axis=0, keepdims=True)
        gdb_ref[...] = shift_sum if first else gdb_in[...] + shift_sum
        racc_s[...] = jnp.zeros_like(racc_s)
        dacc_s[...] = jnp.zeros_like(dacc_s)

    flat = flat_s[...]
    dr = dr_s[...]
    hidden = mm(flat, up_ref[0]) + ub_ref[...].astype(F32)
    half_erf = 0.5 * lax.erf(hidden * (0.5**0.5)) + 0.5
    active = (hidden * half_erf).astype(BF)
    slope = half_erf + hidden * (jnp.exp(-0.5 * hidden * hidden) * 0.3989422804014327)
    racc_s[...] += mm(active, down_ref[0])
    grad_pre = mm_nt(dr, down_ref[0]) * slope
    low_pre = grad_pre.astype(BF)
    dacc_s[...] += mm_nt(low_pre, up_ref[0])
    gup = mm(flatT_s[...], low_pre)
    gdn = mm(drT_s[...], active)
    gbias = jnp.sum(low_pre.astype(F32), axis=0, keepdims=True)
    if not first:
        gup = gup_in[...] + gup
        gdn = gdn_in[...] + gdn
        gbias = gb_in[...] + gbias
    gup_ref[...] = gup
    gdn_ref[...] = gdn
    gb_ref[...] = gbias
    if last:
        for at, (low, (begin, end)) in enumerate(zip(lows, PIECES)):
            value = gup if at < len(UP_PIECES) else gdn

            @pl.when((step >= begin) & (step < end))
            def _(low=low, value=value):
                low[...] = value.astype(BF)

    @pl.when(step == pl.num_programs(0) - 1)
    def _():
        result = (racc_s[...] + db_ref[...].astype(F32)).astype(BF)
        for e in range(groups):
            block = result[e * room : (e + 1) * room]
            if shift:
                older = iota((8, 1), 0) < shift
                head = jnp.where(older, r_in[e, :8].astype(F32), block[:8].astype(F32))
                r_ref[e, :8] = head.astype(BF)
                r_ref[e, 8:] = block[8:]
            else:
                r_ref[e] = block
        dy = dyb_ref[...].astype(F32).reshape(slots, width)
        dgate = jnp.sum(dy * result.astype(F32), axis=1, keepdims=True).reshape(groups, room, 1)
        spread = jnp.where(
            iota((groups, room, LANES), 2) == iota((groups, room, LANES), 1), dgate, 0.0
        )
        as_row = jnp.sum(spread, axis=1, keepdims=True)
        high = as_row.astype(BF).astype(F32)
        tail = jnp.zeros((groups, 1, width - 2 * LANES), F32)
        as_row = jnp.concatenate([high, as_row - high, tail], axis=2)
        back = dacc_s[...].reshape(groups, room, width)
        back = jnp.where(iota((groups, room, 1), 1) == room - 1, as_row, back).astype(BF)
        for e in range(groups):
            dbuf_ref[e] = back[e]


def backward_kernel(cfg, mb, first, last, *refs):
    images, local_len, seq_count, width, experts, room, capacity = cfg
    (
        meta_ref,
        len_ref,
        dback_ref,
        pcol_ref,
        gate_ref,
        middle_ref,
        second_ref,
        dy_ref,
        oT_ref,
        w_ref,
        q_ref,
        k_ref,
        v_ref,
        lse_ref,
        n1T_ref,
        own_ref,
        oth_ref,
    ) = refs[:17]
    refs = refs[17:]
    if not first:
        g_in, mrow_in = refs[:2]
        refs = refs[2:]
    down_own, down_oth, dm_ref = refs[:3]
    refs = refs[3:]
    if last:
        low_ref = refs[0]
        refs = refs[1:]
    else:
        g_ref = refs[0]
        refs = refs[1:]
    mrow_ref, do_s, dqT_s, dkv_s = refs

    def add_dense(at, value):
        if not first:
            value = g_in[:, at] + value
        if last:
            low_ref[:, at] = value.astype(BF)
        else:
            g_ref[:, at] = value

    full_len = local_len * seq_count
    tokens = images * local_len
    slots = experts * room
    misc_at = 4 * width
    rows = misc_rows(w_ref, misc_at)
    here = meta_ref[1]

    def vec(j):
        return rows[experts + j : experts + j + 1, :]

    dback = dback_ref[...].astype(F32)
    back_rows = dback.reshape(slots, width).astype(BF)
    slot_of = iota((tokens, slots), 1)
    hot = jnp.where(
        (slot_of == pcol_ref[0, :, 0:1]) | (slot_of == pcol_ref[0, :, 1:2]), 1.0, 0.0
    ).astype(BF)
    from_experts = mm(hot, back_rows)
    spare = jnp.where(iota((experts, room, 1), 1) == room - 1, dback[:, :, : 2 * LANES], 0.0)
    spare = jnp.sum(spare, axis=1)
    spare = jnp.concatenate(
        [spare, jnp.zeros((LANES - experts, 2 * LANES), F32)], axis=0
    ).astype(BF)
    lane = iota((tokens, LANES), 1)
    pulled = jnp.zeros((tokens, LANES), F32)
    for k in range(TOP):
        within = jnp.where(lane == pcol_ref[0, :, 4 + k : 5 + k], 1.0, 0.0).astype(BF)
        found = mm_nt(jnp.concatenate([within, within], axis=1), spare)
        pulled = pulled + jnp.where(lane == pcol_ref[0, :, 2 + k : 3 + k], found, 0.0)
    gate = gate_ref[...]
    dlogit = gate * (pulled - jnp.sum(gate * pulled, axis=1, keepdims=True))
    dlogit_low = dlogit.astype(BF)
    mrow_ref[...] = mm(jnp.transpose(dlogit_low.astype(F32)).astype(BF), second_ref[...])
    dn2 = from_experts + mm_nt(dlogit_low, w_ref[:, misc_at : misc_at + LANES])
    unit, scale = norm_parts(middle_ref[...])
    dy = dy_ref[...].reshape(tokens, width).astype(F32)
    dm = dy + norm_pull(unit, scale, vec(5), dn2)
    dm_ref[...] = dm
    da = dm.astype(BF)
    gproj = mm(oT_ref[...], da)
    proj = slice(3 * width, 4 * width)
    add_dense(proj, gproj)
    do_s[...] = mm_nt(da, w_ref[:, proj]).astype(BF)
    half_lane = iota((1, LANES), 1)
    low_half = (half_lane < HD).astype(BF)
    high_half = (half_lane >= HD).astype(BF)
    gqkv = [None, None]
    bias_q = jnp.zeros((1, width), F32)
    bias_v = jnp.zeros((1, width), F32)
    gain_sum = jnp.zeros((1, width), F32)
    shift_sum = jnp.zeros((1, width), F32)
    for b in range(images):
        span = slice(b * local_len, (b + 1) * local_len)
        wide = slice(b * full_len, (b + 1) * full_len)
        kpos = iota((full_len, 1), 0)
        shift = jnp.zeros((full_len, 1), jnp.int32)
        for j in range(seq_count):
            origin = lax.rem(here + j, seq_count) * local_len - j * local_len
            shift = jnp.where(kpos >= j * local_len, origin, shift)
        valid = (kpos + shift) < len_ref[mb * images + b]

        def heads(blk, carry):
            at = pl.ds(pl.multiple_of(blk * LANES, LANES), LANES)
            q_blk = q_ref[span, at]
            k_blk = k_ref[wide, at]
            v_blk = v_ref[wide, at]
            do_blk = do_s[span, at]
            kT_blk = jnp.transpose(k_blk)
            dvs = []
            dks = []
            dqs = []
            for side, keep in enumerate((low_half, high_half)):
                scores = mm_nt(k_blk, q_blk * keep)
                logs = lse_ref[pl.ds(b * 8 + 2 * blk + side, 1), :]
                probs = jnp.where(valid, jnp.exp(scores - logs), 0.0)
                dprobs = mm_nt(v_blk, do_blk * keep)
                inner = jnp.sum(probs * dprobs, axis=0, keepdims=True)
                dscores = (probs * (dprobs - inner)).astype(BF)
                dvs.append(mm(probs.astype(BF), do_blk))
                dks.append(mm(dscores, q_blk))
                dqs.append(mm(kT_blk[side * HD : (side + 1) * HD], dscores))
            dqT_s[pl.ds(pl.multiple_of(blk * LANES, LANES), HD), :] = dqs[0]
            dqT_s[pl.ds(pl.multiple_of(blk * LANES + HD, HD), HD), :] = dqs[1]
            left = half_lane < HD
            dkv_s[:, at] = jnp.where(left, dks[0], dks[1]).astype(BF)
            vat = pl.ds(pl.multiple_of(width + blk * LANES, LANES), LANES)
            dkv_s[:, vat] = jnp.where(left, dvs[0], dvs[1]).astype(BF)
            return carry

        lax.fori_loop(0, width // LANES, heads, 0)
        dq = (jnp.transpose(dqT_s[...]) * HD**-0.5).astype(BF)
        dkv = dkv_s[...]
        part_q = mm(n1T_ref[:, b * full_len : b * full_len + local_len], dq)
        part_kv = mm(n1T_ref[:, wide], dkv)
        gqkv[0] = part_q if b == 0 else gqkv[0] + part_q
        gqkv[1] = part_kv if b == 0 else gqkv[1] + part_kv
        bias_q = bias_q + jnp.sum(dq.astype(F32), axis=0, keepdims=True)
        bias_v = bias_v + jnp.sum(dkv[:, width:].astype(F32), axis=0, keepdims=True)
        down = mm_nt(dkv, w_ref[:, width : 3 * width])
        down_own[span, :] = mm_nt(dq, w_ref[:, :width])
        down_own[span, :] += down[:local_len]
        for j in range(seq_count):
            part = down_own[span, :] if j == 0 else down[j * local_len : (j + 1) * local_len]
            tokens_in = own_ref[b] if j == 0 else oth_ref[j - 1, b]
            first_unit, _ = norm_parts(tokens_in.astype(F32))
            gain_sum = gain_sum + jnp.sum(part * first_unit, axis=0, keepdims=True)
            shift_sum = shift_sum + jnp.sum(part, axis=0, keepdims=True)
            if j > 0:
                down_oth[j - 1, span, :] = part.astype(BF)
    add_dense(slice(0, width), gqkv[0])
    add_dense(slice(width, 3 * width), gqkv[1])
    row = iota((LANES, 1), 0)
    mrow = jnp.where(row < experts, mrow_ref[...], 0.0)
    sums = (
        gain_sum,
        shift_sum,
        bias_q,
        bias_v,
        jnp.sum(da.astype(F32), axis=0, keepdims=True),
        jnp.sum(dn2 * unit, axis=0, keepdims=True),
        jnp.sum(dn2, axis=0, keepdims=True),
    )
    for j, value in enumerate(sums):
        mrow = jnp.where(row == experts + j, value, mrow)
    if not first:
        mrow = mrow_in[...] + mrow
    mrow_ref[...] = mrow
    if last:
        low_ref[:, misc_at : misc_at + LANES] = jnp.transpose(mrow).astype(BF)


def input_kernel(cfg, own_ref, got_ref, x_ref, dm_ref, wm_ref, *refs):
    out_ref = refs[-1]
    images, local_len, seq_count, width, experts = cfg
    tokens = images * local_len
    rows = jnp.transpose(wm_ref[...].astype(F32))
    dn1 = own_ref[...]
    for j in range(seq_count - 1):
        dn1 = dn1 + got_ref[j].astype(F32)
    unit, scale = norm_parts(x_ref[...].reshape(tokens, width).astype(F32))
    grad = dm_ref[...] + norm_pull(unit, scale, rows[experts : experts + 1, :], dn1)
    out_ref[...] = grad.astype(BF).reshape(images, local_len, width)


def mix_kernel(cfg, back_ref, pcol_ref, *refs):
    for mb in range(MICRO):

        @pl.when(pl.program_id(0) == mb)
        def _():
            mix_part(cfg, back_ref, pcol_ref, refs[2 * mb], refs[2 * mb + 1], refs[-1])


def mix_part(cfg, back_ref, pcol_ref, gate_ref, middle_ref, out_ref):
    images, local_len, width, experts, room = cfg
    tokens = images * local_len
    slots = experts * room
    back = back_ref[...].astype(F32).reshape(slots, width).astype(BF)
    slot_of = iota((tokens, slots), 1)
    lane = iota((tokens, LANES), 1)
    gate = gate_ref[...]
    total = middle_ref[...]
    for k in range(TOP):
        hot = jnp.where(slot_of == pcol_ref[0, :, k : k + 1], 1.0, 0.0).astype(BF)
        chosen = jnp.where(lane == pcol_ref[0, :, 2 + k : 3 + k], gate, 0.0)
        total = total + jnp.sum(chosen, axis=1, keepdims=True) * mm(hot, back)
    out_ref[...] = total.astype(BF).reshape(images, local_len, width)


def sum_kernel(gup_ref, gdn_ref, *refs):
    up_ref, dn_ref = refs[-2:]
    step = pl.program_id(0)
    ups = refs[: len(UP_PIECES)]
    downs = refs[len(UP_PIECES) : -2]
    got_up = ups[0][...]
    for ref, (begin, _) in zip(ups[1:], UP_PIECES[1:]):
        got_up = jnp.where(step >= begin, ref[...], got_up)
    got_dn = downs[0][...]
    for ref, (begin, _) in zip(downs[1:], DOWN_PIECES[1:]):
        got_dn = jnp.where(step >= begin, ref[...], got_dn)
    up_ref[0] = gup_ref[...] + got_up.astype(F32)
    dn_ref[0] = jnp.transpose(gdn_ref[...] + got_dn.astype(F32))


def smem_spec():
    return pl.BlockSpec(memory_space=pltpu.SMEM)


def params():
    return pltpu.CompilerParams(vmem_limit_bytes=VMEM_LIMIT)


def cost(micros):
    return pl.CostEstimate(
        flops=int(micros * 1e9), transcendentals=0, bytes_accessed=int(micros * 2e6)
    )


def struct(shape, kind):
    return jax.ShapeDtypeStruct(shape, kind)


def after(value, *others):
    return lax.optimization_barrier((value, *others))[0]


def on_device(
    images,
    cotangent,
    lengths,
    routes,
    attn_norm_gain,
    attn_norm_bias,
    qkv_weight,
    query_value_bias,
    proj_weight,
    proj_bias,
    moe_norm_gain,
    moe_norm_bias,
    router_weight,
    up_weight,
    up_bias,
    down_weight,
    down_bias,
):
    seq_count = lax.axis_size("seq")
    dp_count = lax.axis_size("dp")
    count = images.shape[0] // MICRO
    local_len = images.shape[1]
    width = images.shape[2]
    tokens = count * local_len
    full_len = local_len * seq_count
    experts = router_weight.shape[1]
    hidden = up_weight.shape[2]
    capacity = (5 * tokens * TOP + 4 * experts - 1) // (4 * experts)
    room = (capacity + window(capacity, MICRO - 1)[1] + 8) // 8 * 8
    assert all(window(capacity, mb)[1] + capacity < room for mb in range(MICRO))
    assert window(capacity, 1)[0] + room <= window(capacity, 2)[0] + 8
    slots = experts * room
    assert up_weight.shape[0] == 1 and experts == dp_count
    assert experts + VEC <= LANES and capacity <= LANES
    meta = jnp.stack([lax.axis_index("dp"), lax.axis_index("seq")]).astype(jnp.int32)
    packed_width = 4 * width + LANES

    def full(shape):
        return pl.BlockSpec(shape, lambda i: (0,) * len(shape))

    def token_spec(mb):
        return pl.BlockSpec((count, local_len, width), lambda i: (mb, 0, 0))

    def table_spec(mb, shape):
        return pl.BlockSpec((1, *shape), lambda i: (mb, 0, 0))

    def block_spec(mb):
        return pl.BlockSpec((experts, room, width), lambda i: (0, mb, 0))

    def window_spec(mb=None):
        def at(i):
            return (0, (capacity * (i if mb is None else mb)) // 8 * 8, 0)

        return pl.BlockSpec((pl.Element(experts), pl.Element(room), pl.Element(width)), at)

    any_spec = pl.BlockSpec(memory_space=pl.ANY)
    other_spec = lambda mb: pl.BlockSpec(
        (seq_count - 1, count, local_len, width), lambda i: (0, max(mb - 1, 0), 0, 0)
    )
    assert hidden // FF_BLOCK == UP_PIECES[-1][1] == DOWN_PIECES[-1][1]

    def piece_spec(begin, end):
        return pl.BlockSpec(
            (width, FF_BLOCK), lambda i: (0, jnp.clip(i - begin, 0, end - begin - 1))
        )

    misc_spec = pl.BlockSpec((width, LANES), lambda i: (0, 4 * width // LANES))
    moved = struct((experts, room, width), BF)
    merged = struct((experts, window(capacity, MICRO - 1)[0] + room, width), BF)
    tailed = struct((experts, (MICRO - 1) * room, width), BF)

    def seq_shift(array, j):
        return lax.ppermute(array, "seq", [((i + j) % seq_count, i) for i in range(seq_count)])

    others = []
    for part in (images[:count], images[count:]):
        moved_images = jnp.stack([seq_shift(part, j) for j in range(1, seq_count)])
        others.append(moved_images)

    sent_dy, prow, pcol = pl.pallas_call(
        functools.partial(place_kernel, experts, room, capacity),
        grid=(MICRO,),
        in_specs=[
            pl.BlockSpec((1, 1, 1, TOP, tokens), lambda i: (0, i, 0, 0, 0)),
            pl.BlockSpec((count, local_len, width), lambda i: (i, 0, 0)),
        ],
        out_specs=[
            pl.BlockSpec(merged.shape, lambda i: (0, 0, 0)),
            pl.BlockSpec((1, TOP, tokens), lambda i: (i, 0, 0)),
            pl.BlockSpec((1, tokens, 8), lambda i: (i, 0, 0)),
        ],
        out_shape=[
            merged,
            struct((MICRO, TOP, tokens), jnp.int32),
            struct((MICRO, tokens, 8), jnp.int32),
        ],
        compiler_params=params(),
        cost_estimate=cost(8),
        name="place",
    )(jnp.swapaxes(routes, 3, 4), cotangent)

    vectors = jnp.concatenate(
        [
            jnp.stack([attn_norm_gain, attn_norm_bias]),
            query_value_bias,
            jnp.stack([proj_bias, moe_norm_gain, moe_norm_bias, jnp.zeros_like(proj_bias)]),
        ],
        axis=0,
    )
    shard = router_weight.shape[0]
    bits = dp_count.bit_length() - 1
    assert dp_count == 1 << bits

    def across(value, offset):
        return lax.ppermute(value, "dp", [(i, i ^ offset) for i in range(dp_count)])

    def gather_rows(own, gate):
        quarter = dp_count // 4
        pieces = [own, *[across(own, k * quarter) for k in (1, 2, 3)]]
        held = [jnp.stack(pieces)]
        offsets = [[0, quarter, 2 * quarter, 3 * quarter]]
        for bit in reversed(range(bits - 2)):
            if bit == 0:
                held[-1] = after(held[-1], gate)
            held += [across(h, 1 << bit) for h in held]
            offsets += [[k ^ (1 << bit) for k in known] for known in offsets]
        return pl.pallas_call(
            functools.partial(assemble_kernel, offsets, shard),
            grid=(1,),
            in_specs=[smem_spec(), *[full(h.shape) for h in held]],
            out_specs=full((dp_count * shard, packed_width)),
            out_shape=struct((dp_count * shard, packed_width), BF),
            compiler_params=params(),
            cost_estimate=cost(3),
            name="assemble",
        )(meta, *held), pieces[1:]

    def halve(value, bit):
        mine = lax.bitwise_and(lax.shift_right_logical(lax.axis_index("dp"), bit), 1)
        value = value.reshape(-1, 2, shard, packed_width)
        keep = lax.dynamic_index_in_dim(value, mine, 1, keepdims=False)
        give = lax.dynamic_index_in_dim(value, 1 - mine, 1, keepdims=False).astype(BF)
        return keep.astype(F32) + across(give, 1 << bit).astype(F32)

    def scatter_far(value):
        high = lax.shift_right_logical(lax.axis_index("dp"), bits - 2)
        result = lax.dynamic_index_in_dim(value, high, 0, keepdims=False)
        for offset in (1, 2, 3):
            give = lax.dynamic_index_in_dim(
                value, lax.bitwise_xor(high, offset), 0, keepdims=False
            )
            result = result + across(give.astype(BF), offset << (bits - 2)).astype(F32)
        return result

    pack_args = (qkv_weight, proj_weight, router_weight.T, vectors)
    packed_shard = pl.pallas_call(
        functools.partial(pack_kernel, experts),
        grid=(1,),
        in_specs=[full(a.shape) for a in pack_args],
        out_specs=full((shard, packed_width)),
        out_shape=struct((shard, packed_width), BF),
        compiler_params=params(),
        cost_estimate=cost(1),
        name="pack",
    )(*pack_args)

    def exchange(array):
        return lax.all_to_all(array, "dp", split_axis=0, concat_axis=0, tiled=True)

    packed, near = gather_rows(packed_shard, others[1])
    dyb = exchange(after(sent_dy, *near, others[0]))

    def forward(mb):
        cfg = (count, local_len, seq_count, width, experts, room)
        outs = [
            ((experts, room, width), BF),
            ((tokens, width), F32),
            ((tokens, LANES), F32),
            ((tokens, width), BF),
            ((width, tokens), BF),
            ((tokens, width), BF),
            ((count * full_len, width), BF),
            ((count * full_len, width), BF),
            ((count * 8, local_len), F32),
            ((width, count * full_len), BF),
        ]
        return pl.pallas_call(
            functools.partial(forward_kernel, cfg, mb),
            grid=(1,),
            in_specs=[
                smem_spec(),
                smem_spec(),
                token_spec(mb),
                other_spec(mb),
                full((width, packed_width)),
                table_spec(mb, (TOP, tokens)),
            ],
            out_specs=[full(s) for s, _ in outs],
            out_shape=[struct(s, k) for s, k in outs],
            scratch_shapes=[
                pltpu.VMEM((tokens, width), BF),
                pltpu.VMEM((local_len, LANES), F32),
            ],
            compiler_params=params(),
            cost_estimate=cost(11),
            name="forward",
        )(meta, lengths, images, others[min(mb, 1)], packed, prow)

    def expert(mb, buf, results, tail_back, totals):
        first = mb == 0
        last = mb == MICRO - 1
        cfg = (experts, room, capacity, window(capacity, mb)[1], width)
        wide = lambda: pl.BlockSpec((width, FF_BLOCK), lambda i: (0, i))
        thin = lambda: pl.BlockSpec((1, FF_BLOCK), lambda i: (0, i))
        in_specs = [
            smem_spec(),
            full((experts, room, width)),
            window_spec(mb),
            misc_spec,
            pl.BlockSpec((1, width, FF_BLOCK), lambda i: (0, 0, i)),
            thin(),
            pl.BlockSpec((1, FF_BLOCK, width), lambda i: (0, i, 0)),
            full((1, width)),
        ]
        total_specs = [wide(), wide(), thin(), full((1, width))]
        args = [meta, buf, dyb, packed, up_weight, up_bias, down_weight, down_bias]
        aliases = {}
        if not first:
            aliases = {len(args): 0}
            aliases.update({len(args) + 1 + j: 2 + j for j in range(4)})
            in_specs += [window_spec(mb), *total_specs]
            args += [results, *totals]
        if mb >= 2:
            aliases[len(args)] = 1
            in_specs += [any_spec]
            args += [tail_back]
        outs = pl.pallas_call(
            functools.partial(expert_kernel, cfg, first, last),
            grid=(hidden // FF_BLOCK,),
            in_specs=in_specs,
            out_specs=[window_spec(mb), block_spec(max(mb - 1, 0)), *total_specs]
            + ([piece_spec(*p) for p in PIECES] if last else []),
            out_shape=[
                merged,
                moved if first else tailed,
                struct((width, hidden), F32),
                struct((width, hidden), F32),
                struct((1, hidden), F32),
                struct((1, width), F32),
            ]
            + (
                [struct((width, (end - begin) * FF_BLOCK), BF) for begin, end in PIECES]
                if last
                else []
            ),
            scratch_shapes=[
                pltpu.VMEM((slots, width), BF),
                pltpu.VMEM((width, slots), BF),
                pltpu.VMEM((slots, width), BF),
                pltpu.VMEM((width, slots), BF),
                pltpu.VMEM((slots, width), F32),
                pltpu.VMEM((slots, width), F32),
            ],
            input_output_aliases=aliases,
            compiler_params=params(),
            cost_estimate=cost(19),
            name="expert",
        )(*args)
        return outs[0], outs[1], tuple(outs[2:])

    def backward(mb, dback, saved, totals):
        first = mb == 0
        last = mb == MICRO - 1
        cfg = (count, local_len, seq_count, width, experts, room, capacity)
        middle, gate, second, oT, q, k, v, lse, n1T = saved
        whole = [gate, middle, second]
        heads = [oT, packed, q, k, v, lse, n1T]
        args = [meta, lengths, dback, pcol, *whole, cotangent, *heads, images, others[min(mb, 1)]]
        in_specs = [
            smem_spec(),
            smem_spec(),
            block_spec(max(mb - 1, 0)),
            table_spec(mb, (tokens, 8)),
            *[full(a.shape) for a in whole],
            token_spec(mb),
            *[full(a.shape) for a in heads],
            token_spec(mb),
            other_spec(mb),
        ]
        aliases = {}
        if not first:
            in_specs += [full(a.shape) for a in totals]
            args += list(totals)
            if not last:
                aliases = {len(args) - 2: 3, len(args) - 1: 4}
        outs = [
            ((tokens, width), F32),
            ((seq_count - 1, tokens, width), BF),
            ((tokens, width), F32),
            ((width, packed_width), BF) if last else ((width, 4 * width), F32),
            ((LANES, width), F32),
        ]
        return pl.pallas_call(
            functools.partial(backward_kernel, cfg, mb, first, last),
            grid=(1,),
            in_specs=in_specs,
            out_specs=[full(s) for s, _ in outs],
            out_shape=[struct(s, t) for s, t in outs],
            scratch_shapes=[
                pltpu.VMEM((tokens, width), BF),
                pltpu.VMEM((width, local_len), F32),
                pltpu.VMEM((full_len, 2 * width), BF),
            ],
            input_output_aliases=aliases,
            compiler_params=params(),
            cost_estimate=cost(0.1 if last else 17),
            name="backward",
        )(*args)

    def into(kernel, mb, args, specs, previous, micros, name):
        aliases = {}
        if previous is not None:
            aliases = {len(args): 0}
            args = [*args, previous]
            specs = [*specs, any_spec]
        return pl.pallas_call(
            kernel,
            grid=(1,),
            in_specs=specs,
            out_specs=token_spec(mb),
            out_shape=struct(images.shape, BF),
            input_output_aliases=aliases,
            compiler_params=params(),
            cost_estimate=cost(micros),
            name=name,
        )(*args)

    def finish(mb, own, got, dm, previous):
        cfg = (count, local_len, seq_count, width, experts)
        specs = [full(own.shape), full(got.shape), token_spec(mb), full(dm.shape), misc_spec]
        return into(
            functools.partial(input_kernel, cfg),
            mb,
            [own, got, images, dm, packed],
            specs,
            previous,
            0.1,
            "finish",
        )

    def mix(back):
        cfg = (count, local_len, width, experts, room)
        tables = sum([[saved[mb][1], saved[mb][0]] for mb in range(MICRO)], [])
        return pl.pallas_call(
            functools.partial(mix_kernel, cfg),
            grid=(MICRO,),
            in_specs=[
                window_spec(),
                pl.BlockSpec((1, tokens, 8), lambda i: (i, 0, 0)),
                *[full(t.shape) for t in tables],
            ],
            out_specs=pl.BlockSpec((count, local_len, width), lambda i: (i, 0, 0)),
            out_shape=struct(images.shape, BF),
            compiler_params=params(),
            cost_estimate=cost(0.1),
            name="mix",
        )(back, pcol, *tables)

    swap = [(i, (i + 1) % seq_count) for i in range(seq_count)]

    def seq_sum(value):
        if seq_count == 2:
            return value + lax.ppermute(value.astype(BF), "seq", swap).astype(F32)
        return lax.psum(value.astype(BF), "seq").astype(F32)

    passed = [forward(mb) for mb in range(MICRO)]
    saved = [outs[1:] for outs in passed]
    bufs = []
    for mb in range(MICRO):
        first_gate = (dyb,) if mb == 0 else ()
        bufs.append(exchange(after(passed[mb][0], *first_gate)))
    totals = None
    results = None
    ready = [None, None]
    for mb in range(MICRO):
        results, ready[min(mb, 1)], totals = expert(mb, bufs[mb], results, ready[1], totals)
    gup, gdn, gbias, gdbias, *pieces = totals
    arrived = []
    if seq_count == 2:
        arrived = [lax.ppermute(piece, "seq", swap) for piece in pieces]
    dense = None
    owns = []
    gots = []
    dms = []
    dbacks = [exchange(ready[0]), exchange(ready[1])]
    if arrived:
        dbacks[1], arrived[0] = lax.optimization_barrier((dbacks[1], arrived[0]))
    for mb in range(MICRO):
        dback = dbacks[min(mb, 1)]
        if mb == 2 and arrived:
            dense, arrived[1] = lax.optimization_barrier((dense, arrived[1]))
        own, oth, dm, *dense = backward(mb, dback, saved[mb], dense)
        owns.append(own)
        dms.append(dm)
        gots.append(
            jnp.stack(
                [
                    lax.ppermute(
                        oth[j - 1], "seq", [(i, (i + j) % seq_count) for i in range(seq_count)]
                    )
                    for j in range(1, seq_count)
                ]
            )
        )
    back = exchange(after(results, dbacks[1]))
    part = halve(after(dense[0], *arrived[2:4]), 0)
    mid = part
    owns = [after(own, mid) for own in owns]
    grads = None
    for mb in range(MICRO - 1):
        grads = finish(mb, owns[mb], gots[mb], dms[mb], grads)

    if seq_count == 2:
        wide = lambda: pl.BlockSpec((width, FF_BLOCK), lambda i: (0, i))
        final_up, final_down = pl.pallas_call(
            sum_kernel,
            grid=(hidden // FF_BLOCK,),
            in_specs=[wide(), wide(), *[piece_spec(*p) for p in PIECES]],
            out_specs=[
                pl.BlockSpec((1, width, FF_BLOCK), lambda i: (0, 0, i)),
                pl.BlockSpec((1, FF_BLOCK, width), lambda i: (0, i, 0)),
            ],
            out_shape=[struct((1, width, hidden), F32), struct((1, hidden, width), F32)],
            compiler_params=params(),
            cost_estimate=cost(0.1),
            name="sum_experts",
        )(after(gup, mid), gdn, *arrived)
    else:
        sums = [lax.psum(piece, "seq").astype(F32) for piece in pieces]
        ups, downs = sums[: len(UP_PIECES)], sums[len(UP_PIECES) :]
        final_up = jnp.concatenate(ups, axis=1)[None]
        final_down = jnp.swapaxes(jnp.concatenate(downs, axis=1), 0, 1)[None]
    biases = seq_sum(jnp.concatenate([gbias, gdbias], axis=1))
    for bit in range(1, bits - 2):
        part = halve(part, bit)
    part, grads, final_up, biases, back = lax.optimization_barrier(
        (part, grads, final_up, biases, back)
    )
    shards = scatter_far(part)
    last_own = after(owns[-1], part)
    grads = finish(MICRO - 1, last_own, gots[-1], dms[-1], grads)
    out = mix(back)
    final_up_shift = biases[:, :hidden]
    final_down_shift = biases[:, hidden:]

    shards = seq_sum(shards)
    misc = 4 * width + experts
    return (
        out,
        grads,
        shards[:, misc],
        shards[:, misc + 1],
        shards[:, : 3 * width],
        jnp.stack([shards[:, misc + 2], shards[:, misc + 3]]),
        shards[:, 3 * width : 4 * width],
        shards[:, misc + 4],
        shards[:, misc + 5],
        shards[:, misc + 6],
        shards[:, 4 * width : misc],
        final_up,
        final_up_shift,
        final_down,
        final_down_shift,
    )


def solution(mesh):
    return jax.shard_map(
        on_device,
        mesh=mesh,
        in_specs=(
            P("dp", "seq", None),
            P("dp", "seq", None),
            P("dp"),
            P("dp", None, "seq", None, None),
            P("dp"),
            P("dp"),
            P("dp", None),
            P(None, "dp"),
            P("dp", None),
            P("dp"),
            P("dp"),
            P("dp"),
            P("dp", None),
            P("dp", None, None),
            P("dp", None),
            P("dp", None, None),
            P("dp", None),
        ),
        out_specs=(
            P("dp", "seq", None),
            P("dp", "seq", None),
            P("dp"),
            P("dp"),
            P("dp", None),
            P(None, "dp"),
            P("dp", None),
            P("dp"),
            P("dp"),
            P("dp"),
            P("dp", None),
            P("dp", None, None),
            P("dp", None),
            P("dp", None, None),
            P("dp", None),
        ),
        check_vma=False,
    )
```

```python
import functools

import jax
import jax.numpy as jnp
from jax import lax
from jax.experimental import pallas as pl
from jax.experimental.pallas import tpu as pltpu
from jax.sharding import PartitionSpec as P

HD = 64
TOP = 2
MICRO = 3
BF = jnp.bfloat16
F32 = jnp.float32
EPS = 1e-06
LANES = 128
VEC = 8
FF_BLOCK = 512
UP_PIECES = ((0, 2), (2, 4))
DOWN_PIECES = ((0, 2), (2, 3), (3, 4))
PIECES = UP_PIECES + DOWN_PIECES
VMEM_LIMIT = 60 * 1024 * 1024


def mm(left, right):
    return jnp.dot(left, right, preferred_element_type=F32)


def mm_nt(left, right):
    return lax.dot_general(
        left, right, (((1,), (1,)), ((), ())), preferred_element_type=F32
    )


def iota(shape, dim):
    return lax.broadcasted_iota(jnp.int32, shape, dim)


def norm_parts(values):
    average = jnp.mean(values, axis=-1, keepdims=True)
    centred = values - average
    spread = jnp.mean(centred * centred, axis=-1, keepdims=True)
    scale = lax.rsqrt(spread + EPS)
    return centred * scale, scale


def norm_pull(unit, scale, gain, cotangent):
    inner = cotangent * gain
    mean_inner = jnp.mean(inner, axis=-1, keepdims=True)
    mean_unit = jnp.mean(inner * unit, axis=-1, keepdims=True)
    return scale * (inner - mean_inner - unit * mean_unit)


def misc_rows(w_ref, start):
    return jnp.transpose(w_ref[:, start : start + LANES].astype(F32))


def pack_kernel(experts, qkv_ref, proj_ref, router_ref, vec_ref, out_ref):
    width = proj_ref.shape[1]
    shard = proj_ref.shape[0]
    out_ref[:, : 3 * width] = qkv_ref[...]
    out_ref[:, 3 * width : 4 * width] = proj_ref[...]
    rows = jnp.concatenate([router_ref[...].astype(F32), vec_ref[...].astype(F32)], axis=0)
    columns = jnp.transpose(rows)
    tail = jnp.zeros((shard, LANES - columns.shape[1]), F32)
    out_ref[:, 4 * width :] = jnp.concatenate([columns, tail], axis=1).astype(BF)


def assemble_kernel(sources, shard, meta_ref, *refs):
    out_ref = refs[-1]
    for ref, offsets in zip(refs[:-1], sources):
        for at, offset in enumerate(offsets):
            row = jnp.bitwise_xor(meta_ref[0], offset) * shard
            out_ref[pl.ds(pl.multiple_of(row, shard), shard), :] = ref[at]


def window(capacity, mb):
    start = capacity * mb // 8 * 8
    return start, capacity * mb - start


def place_kernel(experts, room, capacity, routes_ref, dy_ref, send_ref, prow_ref, pcol_ref):
    for mb in range(MICRO):

        @pl.when(pl.program_id(0) == mb)
        def _():
            place_part(
                experts, room, window(capacity, mb), routes_ref, dy_ref, send_ref, prow_ref, pcol_ref
            )


def place_part(experts, room, where, routes_ref, dy_ref, send_ref, prow_ref, pcol_ref):
    start, shift = where
    tokens = routes_ref.shape[4]
    slots = experts * room
    rows = routes_ref[0, 0, 0]
    first_row = rows[0:1]
    second_row = rows[1:2]
    tall = jnp.concatenate([rows.astype(F32), jnp.zeros((LANES - TOP, tokens), F32)], axis=0)
    cols = jnp.transpose(tall)[:, 0:8].astype(jnp.int32)
    hot_first = (iota((experts, tokens), 0) == first_row).astype(F32)
    hot_second = (iota((experts, tokens), 0) == second_row).astype(F32)
    earlier = (iota((tokens, tokens), 0) < iota((tokens, tokens), 1)).astype(BF)
    before = mm((hot_first + hot_second).astype(BF), earlier)
    in_first = jnp.sum(before * hot_first, axis=0, keepdims=True).astype(jnp.int32)
    in_second = jnp.sum((before + hot_first) * hot_second, axis=0, keepdims=True).astype(jnp.int32)
    place_first = first_row * room + in_first + shift
    place_second = second_row * room + in_second + shift
    prow_ref[0, 0:1, :] = place_first
    prow_ref[0, 1:2, :] = place_second
    slot_of = iota((slots, tokens), 0)
    hot = jnp.where((slot_of == place_first) | (slot_of == place_second), 1.0, 0.0).astype(BF)
    flat = dy_ref[...].reshape(tokens, dy_ref.shape[-1])
    rows = mm(hot, flat)
    for e in range(experts):
        block = rows[e * room : (e + 1) * room].astype(BF)
        if shift:
            send_ref[e, start : start + 8] = send_ref[e, start : start + 8] + block[:8]
            send_ref[e, start + 8 : start + room] = block[8:]
        else:
            send_ref[e, start : start + room] = block
    first_col = cols[:, 0:1]
    second_col = cols[:, 1:2]
    hot_first = (iota((tokens, experts), 1) == first_col).astype(F32)
    hot_second = (iota((tokens, experts), 1) == second_col).astype(F32)
    later = (iota((tokens, tokens), 1) < iota((tokens, tokens), 0)).astype(BF)
    before = mm(later, (hot_first + hot_second).astype(BF))
    in_first = jnp.sum(before * hot_first, axis=1, keepdims=True).astype(jnp.int32)
    in_second = jnp.sum((before + hot_first) * hot_second, axis=1, keepdims=True).astype(jnp.int32)
    lane = iota((tokens, 8), 1)
    table = jnp.zeros((tokens, 8), jnp.int32)
    for at, col in enumerate(
        (
            first_col * room + in_first + shift,
            second_col * room + in_second + shift,
            first_col,
            second_col,
            in_first + shift,
            in_second + shift,
        )
    ):
        table = jnp.where(lane == at, col, table)
    pcol_ref[0] = table


def forward_kernel(
    cfg,
    mb,
    meta_ref,
    len_ref,
    own_ref,
    oth_ref,
    w_ref,
    prow_ref,
    send_ref,
    middle_ref,
    gate_ref,
    second_ref,
    oT_ref,
    q_ref,
    k_ref,
    v_ref,
    lse_ref,
    n1T_ref,
    att_ref,
    logs_ref,
):
    images, local_len, seq_count, width, experts, room = cfg
    full_len = local_len * seq_count
    tokens = images * local_len
    slots = experts * room
    misc_at = 4 * width
    rows = misc_rows(w_ref, misc_at)

    def vec(j):
        return rows[experts + j : experts + j + 1, :]

    here = meta_ref[1]
    lane = iota((1, LANES), 1)
    low_half = (lane < HD).astype(BF)
    high_half = (lane >= HD).astype(BF)
    for b in range(images):
        blocks = [own_ref[b]] + [oth_ref[j, b] for j in range(seq_count - 1)]
        full = jnp.concatenate(blocks, axis=0).astype(F32)
        unit, _ = norm_parts(full)
        normed = (unit * vec(0) + vec(1)).astype(BF)
        n1T_ref[:, b * full_len : (b + 1) * full_len] = jnp.transpose(normed)
        span = slice(b * local_len, (b + 1) * local_len)
        wide = slice(b * full_len, (b + 1) * full_len)
        queries = (mm(normed[:local_len], w_ref[:, :width]) + vec(2)).astype(BF)
        q_ref[span, :] = queries * jnp.asarray(HD**-0.5, BF)
        k_ref[wide, :] = mm(normed, w_ref[:, width : 2 * width]).astype(BF)
        v_ref[wide, :] = (mm(normed, w_ref[:, 2 * width : 3 * width]) + vec(3)).astype(BF)
        kpos = iota((1, full_len), 1)
        shift = jnp.zeros((1, full_len), jnp.int32)
        for j in range(seq_count):
            origin = lax.rem(here + j, seq_count) * local_len - j * local_len
            shift = jnp.where(kpos >= j * local_len, origin, shift)
        valid = (kpos + shift) < len_ref[mb * images + b]
        logs_ref[...] = jnp.zeros_like(logs_ref)

        def heads(blk, carry):
            at = pl.ds(pl.multiple_of(blk * LANES, LANES), LANES)
            q_blk = q_ref[span, at]
            k_blk = k_ref[wide, at]
            v_blk = v_ref[wide, at]
            outs = []
            for side, keep in enumerate((low_half, high_half)):
                scores = mm_nt(q_blk * keep, k_blk)
                scores = jnp.where(valid, scores, -1e30)
                highest = jnp.max(scores, axis=1, keepdims=True)
                powers = jnp.exp(scores - highest)
                total = jnp.sum(powers, axis=1, keepdims=True)
                probs = (powers * (1.0 / total)).astype(BF)
                outs.append(mm(probs, v_blk))
                logs_ref[...] = jnp.where(
                    lane == 2 * blk + side, highest + jnp.log(total), logs_ref[...]
                )
            att_ref[span, at] = jnp.where(lane < HD, outs[0], outs[1]).astype(BF)
            return carry

        lax.fori_loop(0, width // LANES, heads, 0)
        lse_ref[b * 8 : b * 8 + 8, :] = jnp.transpose(logs_ref[...])[0:8, :]
    attended = att_ref[...]
    oT_ref[...] = jnp.transpose(attended)
    branch = mm(attended, w_ref[:, 3 * width : 4 * width]) + vec(4)
    middle = own_ref[...].reshape(tokens, width).astype(F32) + branch
    middle_ref[...] = middle
    unit, _ = norm_parts(middle)
    second = (unit * vec(5) + vec(6)).astype(BF)
    second_ref[...] = second
    gate_ref[...] = gates(mm(second, w_ref[:, misc_at : misc_at + LANES]), experts)
    slot_of = iota((slots, tokens), 0)
    hot = jnp.where(
        (slot_of == prow_ref[0, 0:1, :]) | (slot_of == prow_ref[0, 1:2, :]), 1.0, 0.0
    ).astype(BF)
    sent = mm(hot, second)
    for e in range(experts):
        send_ref[e] = sent[e * room : (e + 1) * room].astype(BF)


def gates(logits, experts):
    real = iota((1, LANES), 1) < experts
    logits = jnp.where(real, logits, -1e30)
    powers = jnp.where(real, jnp.exp(logits - jnp.max(logits, axis=1, keepdims=True)), 0.0)
    return powers / jnp.sum(powers, axis=1, keepdims=True)


def expert_kernel(cfg, first, last, *refs):
    groups, room, capacity, shift, width = cfg
    meta_ref, buf_ref, dyb_ref, wm_ref, up_ref, ub_ref, down_ref, db_ref = refs[:8]
    refs = refs[8:]
    if not first:
        r_in, gup_in, gdn_in, gb_in, gdb_in = refs[:5]
        refs = refs[6 if last else 5 :]
    r_ref, dbuf_ref, gup_ref, gdn_ref, gb_ref, gdb_ref = refs[:6]
    refs = refs[6:]
    if last:
        lows = refs[: len(PIECES)]
        refs = refs[len(PIECES) :]
    (
        flat_s,
        flatT_s,
        dr_s,
        drT_s,
        racc_s,
        dacc_s,
    ) = refs
    slots = groups * room
    step = pl.program_id(0)
    experts = groups

    @pl.when(step == 0)
    def _():
        flat = buf_ref[...].astype(F32).reshape(slots, width).astype(BF)
        flat_s[...] = flat
        flatT_s[...] = jnp.transpose(flat)
        gate = gates(mm(flat, wm_ref[...]), experts)
        mine = iota((1, LANES), 1) == meta_ref[0]
        mine_gate = jnp.sum(jnp.where(mine, gate, 0.0), axis=1, keepdims=True)
        at = iota((groups, room, 1), 1)
        own = (at >= shift) & (at < shift + capacity)
        dy = jnp.where(own, dyb_ref[...].astype(F32), 0.0)
        dr = (dy.reshape(slots, width) * mine_gate).astype(BF)
        dr_s[...] = dr
        drT_s[...] = jnp.transpose(dr)
        shift_sum = jnp.sum(dr.astype(F32), axis=0, keepdims=True)
        gdb_ref[...] = shift_sum if first else gdb_in[...] + shift_sum
        racc_s[...] = jnp.zeros_like(racc_s)
        dacc_s[...] = jnp.zeros_like(dacc_s)

    flat = flat_s[...]
    dr = dr_s[...]
    hidden = mm(flat, up_ref[0]) + ub_ref[...].astype(F32)
    half_erf = 0.5 * lax.erf(hidden * (0.5**0.5)) + 0.5
    active = (hidden * half_erf).astype(BF)
    slope = half_erf + hidden * (jnp.exp(-0.5 * hidden * hidden) * 0.3989422804014327)
    racc_s[...] += mm(active, down_ref[0])
    grad_pre = mm_nt(dr, down_ref[0]) * slope
    low_pre = grad_pre.astype(BF)
    dacc_s[...] += mm_nt(low_pre, up_ref[0])
    gup = mm(flatT_s[...], low_pre)
    gdn = mm(drT_s[...], active)
    gbias = jnp.sum(low_pre.astype(F32), axis=0, keepdims=True)
    if not first:
        gup = gup_in[...] + gup
        gdn = gdn_in[...] + gdn
        gbias = gb_in[...] + gbias
    gup_ref[...] = gup
    gdn_ref[...] = gdn
    gb_ref[...] = gbias
    if last:
        for at, (low, (begin, end)) in enumerate(zip(lows, PIECES)):
            value = gup if at < len(UP_PIECES) else gdn

            @pl.when((step >= begin) & (step < end))
            def _(low=low, value=value):
                low[...] = value.astype(BF)

    @pl.when(step == pl.num_programs(0) - 1)
    def _():
        result = (racc_s[...] + db_ref[...].astype(F32)).astype(BF)
        for e in range(groups):
            block = result[e * room : (e + 1) * room]
            if shift:
                older = iota((8, 1), 0) < shift
                head = jnp.where(older, r_in[e, :8].astype(F32), block[:8].astype(F32))
                r_ref[e, :8] = head.astype(BF)
                r_ref[e, 8:] = block[8:]
            else:
                r_ref[e] = block
        dy = dyb_ref[...].astype(F32).reshape(slots, width)
        dgate = jnp.sum(dy * result.astype(F32), axis=1, keepdims=True).reshape(groups, room, 1)
        spread = jnp.where(
            iota((groups, room, LANES), 2) == iota((groups, room, LANES), 1), dgate, 0.0
        )
        as_row = jnp.sum(spread, axis=1, keepdims=True)
        high = as_row.astype(BF).astype(F32)
        tail = jnp.zeros((groups, 1, width - 2 * LANES), F32)
        as_row = jnp.concatenate([high, as_row - high, tail], axis=2)
        back = dacc_s[...].reshape(groups, room, width)
        back = jnp.where(iota((groups, room, 1), 1) == room - 1, as_row, back).astype(BF)
        for e in range(groups):
            dbuf_ref[e] = back[e]


def backward_kernel(cfg, mb, first, last, *refs):
    images, local_len, seq_count, width, experts, room, capacity = cfg
    (
        meta_ref,
        len_ref,
        dback_ref,
        pcol_ref,
        gate_ref,
        middle_ref,
        second_ref,
        dy_ref,
        oT_ref,
        w_ref,
        q_ref,
        k_ref,
        v_ref,
        lse_ref,
        n1T_ref,
        own_ref,
        oth_ref,
    ) = refs[:17]
    refs = refs[17:]
    if not first:
        g_in, mrow_in = refs[:2]
        refs = refs[2:]
    down_own, down_oth, dm_ref = refs[:3]
    refs = refs[3:]
    if last:
        low_ref = refs[0]
        refs = refs[1:]
    else:
        g_ref = refs[0]
        refs = refs[1:]
    mrow_ref, do_s, dqT_s, dkv_s = refs

    def add_dense(at, value):
        if not first:
            value = g_in[:, at] + value
        if last:
            low_ref[:, at] = value.astype(BF)
        else:
            g_ref[:, at] = value

    full_len = local_len * seq_count
    tokens = images * local_len
    slots = experts * room
    misc_at = 4 * width
    rows = misc_rows(w_ref, misc_at)
    here = meta_ref[1]

    def vec(j):
        return rows[experts + j : experts + j + 1, :]

    dback = dback_ref[...].astype(F32)
    back_rows = dback.reshape(slots, width).astype(BF)
    slot_of = iota((tokens, slots), 1)
    hot = jnp.where(
        (slot_of == pcol_ref[0, :, 0:1]) | (slot_of == pcol_ref[0, :, 1:2]), 1.0, 0.0
    ).astype(BF)
    from_experts = mm(hot, back_rows)
    spare = jnp.where(iota((experts, room, 1), 1) == room - 1, dback[:, :, : 2 * LANES], 0.0)
    spare = jnp.sum(spare, axis=1)
    spare = jnp.concatenate(
        [spare, jnp.zeros((LANES - experts, 2 * LANES), F32)], axis=0
    ).astype(BF)
    lane = iota((tokens, LANES), 1)
    pulled = jnp.zeros((tokens, LANES), F32)
    for k in range(TOP):
        within = jnp.where(lane == pcol_ref[0, :, 4 + k : 5 + k], 1.0, 0.0).astype(BF)
        found = mm_nt(jnp.concatenate([within, within], axis=1), spare)
        pulled = pulled + jnp.where(lane == pcol_ref[0, :, 2 + k : 3 + k], found, 0.0)
    gate = gate_ref[...]
    dlogit = gate * (pulled - jnp.sum(gate * pulled, axis=1, keepdims=True))
    dlogit_low = dlogit.astype(BF)
    mrow_ref[...] = mm(jnp.transpose(dlogit_low.astype(F32)).astype(BF), second_ref[...])
    dn2 = from_experts + mm_nt(dlogit_low, w_ref[:, misc_at : misc_at + LANES])
    unit, scale = norm_parts(middle_ref[...])
    dy = dy_ref[...].reshape(tokens, width).astype(F32)
    dm = dy + norm_pull(unit, scale, vec(5), dn2)
    dm_ref[...] = dm
    da = dm.astype(BF)
    gproj = mm(oT_ref[...], da)
    proj = slice(3 * width, 4 * width)
    add_dense(proj, gproj)
    do_s[...] = mm_nt(da, w_ref[:, proj]).astype(BF)
    half_lane = iota((1, LANES), 1)
    low_half = (half_lane < HD).astype(BF)
    high_half = (half_lane >= HD).astype(BF)
    gqkv = [None, None]
    bias_q = jnp.zeros((1, width), F32)
    bias_v = jnp.zeros((1, width), F32)
    gain_sum = jnp.zeros((1, width), F32)
    shift_sum = jnp.zeros((1, width), F32)
    for b in range(images):
        span = slice(b * local_len, (b + 1) * local_len)
        wide = slice(b * full_len, (b + 1) * full_len)
        kpos = iota((full_len, 1), 0)
        shift = jnp.zeros((full_len, 1), jnp.int32)
        for j in range(seq_count):
            origin = lax.rem(here + j, seq_count) * local_len - j * local_len
            shift = jnp.where(kpos >= j * local_len, origin, shift)
        valid = (kpos + shift) < len_ref[mb * images + b]

        def heads(blk, carry):
            at = pl.ds(pl.multiple_of(blk * LANES, LANES), LANES)
            q_blk = q_ref[span, at]
            k_blk = k_ref[wide, at]
            v_blk = v_ref[wide, at]
            do_blk = do_s[span, at]
            kT_blk = jnp.transpose(k_blk)
            dvs = []
            dks = []
            dqs = []
            for side, keep in enumerate((low_half, high_half)):
                scores = mm_nt(k_blk, q_blk * keep)
                logs = lse_ref[pl.ds(b * 8 + 2 * blk + side, 1), :]
                probs = jnp.where(valid, jnp.exp(scores - logs), 0.0)
                dprobs = mm_nt(v_blk, do_blk * keep)
                inner = jnp.sum(probs * dprobs, axis=0, keepdims=True)
                dscores = (probs * (dprobs - inner)).astype(BF)
                dvs.append(mm(probs.astype(BF), do_blk))
                dks.append(mm(dscores, q_blk))
                dqs.append(mm(kT_blk[side * HD : (side + 1) * HD], dscores))
            dqT_s[pl.ds(pl.multiple_of(blk * LANES, LANES), HD), :] = dqs[0]
            dqT_s[pl.ds(pl.multiple_of(blk * LANES + HD, HD), HD), :] = dqs[1]
            left = half_lane < HD
            dkv_s[:, at] = jnp.where(left, dks[0], dks[1]).astype(BF)
            vat = pl.ds(pl.multiple_of(width + blk * LANES, LANES), LANES)
            dkv_s[:, vat] = jnp.where(left, dvs[0], dvs[1]).astype(BF)
            return carry

        lax.fori_loop(0, width // LANES, heads, 0)
        dq = (jnp.transpose(dqT_s[...]) * HD**-0.5).astype(BF)
        dkv = dkv_s[...]
        part_q = mm(n1T_ref[:, b * full_len : b * full_len + local_len], dq)
        part_kv = mm(n1T_ref[:, wide], dkv)
        gqkv[0] = part_q if b == 0 else gqkv[0] + part_q
        gqkv[1] = part_kv if b == 0 else gqkv[1] + part_kv
        bias_q = bias_q + jnp.sum(dq.astype(F32), axis=0, keepdims=True)
        bias_v = bias_v + jnp.sum(dkv[:, width:].astype(F32), axis=0, keepdims=True)
        down = mm_nt(dkv, w_ref[:, width : 3 * width])
        down_own[span, :] = mm_nt(dq, w_ref[:, :width])
        down_own[span, :] += down[:local_len]
        for j in range(seq_count):
            part = down_own[span, :] if j == 0 else down[j * local_len : (j + 1) * local_len]
            tokens_in = own_ref[b] if j == 0 else oth_ref[j - 1, b]
            first_unit, _ = norm_parts(tokens_in.astype(F32))
            gain_sum = gain_sum + jnp.sum(part * first_unit, axis=0, keepdims=True)
            shift_sum = shift_sum + jnp.sum(part, axis=0, keepdims=True)
            if j > 0:
                down_oth[j - 1, span, :] = part.astype(BF)
    add_dense(slice(0, width), gqkv[0])
    add_dense(slice(width, 3 * width), gqkv[1])
    row = iota((LANES, 1), 0)
    mrow = jnp.where(row < experts, mrow_ref[...], 0.0)
    sums = (
        gain_sum,
        shift_sum,
        bias_q,
        bias_v,
        jnp.sum(da.astype(F32), axis=0, keepdims=True),
        jnp.sum(dn2 * unit, axis=0, keepdims=True),
        jnp.sum(dn2, axis=0, keepdims=True),
    )
    for j, value in enumerate(sums):
        mrow = jnp.where(row == experts + j, value, mrow)
    if not first:
        mrow = mrow_in[...] + mrow
    mrow_ref[...] = mrow
    if last:
        low_ref[:, misc_at : misc_at + LANES] = jnp.transpose(mrow).astype(BF)


def input_kernel(cfg, own_ref, got_ref, x_ref, dm_ref, wm_ref, *refs):
    out_ref = refs[-1]
    images, local_len, seq_count, width, experts = cfg
    tokens = images * local_len
    rows = jnp.transpose(wm_ref[...].astype(F32))
    dn1 = own_ref[...]
    for j in range(seq_count - 1):
        dn1 = dn1 + got_ref[j].astype(F32)
    unit, scale = norm_parts(x_ref[...].reshape(tokens, width).astype(F32))
    grad = dm_ref[...] + norm_pull(unit, scale, rows[experts : experts + 1, :], dn1)
    out_ref[...] = grad.astype(BF).reshape(images, local_len, width)


def mix_kernel(cfg, back_ref, pcol_ref, *refs):
    for mb in range(MICRO):

        @pl.when(pl.program_id(0) == mb)
        def _():
            mix_part(cfg, back_ref, pcol_ref, refs[2 * mb], refs[2 * mb + 1], refs[-1])


def mix_part(cfg, back_ref, pcol_ref, gate_ref, middle_ref, out_ref):
    images, local_len, width, experts, room = cfg
    tokens = images * local_len
    slots = experts * room
    back = back_ref[...].astype(F32).reshape(slots, width).astype(BF)
    slot_of = iota((tokens, slots), 1)
    lane = iota((tokens, LANES), 1)
    gate = gate_ref[...]
    total = middle_ref[...]
    for k in range(TOP):
        hot = jnp.where(slot_of == pcol_ref[0, :, k : k + 1], 1.0, 0.0).astype(BF)
        chosen = jnp.where(lane == pcol_ref[0, :, 2 + k : 3 + k], gate, 0.0)
        total = total + jnp.sum(chosen, axis=1, keepdims=True) * mm(hot, back)
    out_ref[...] = total.astype(BF).reshape(images, local_len, width)


def sum_kernel(gup_ref, gdn_ref, *refs):
    up_ref, dn_ref = refs[-2:]
    step = pl.program_id(0)
    ups = refs[: len(UP_PIECES)]
    downs = refs[len(UP_PIECES) : -2]
    got_up = ups[0][...]
    for ref, (begin, _) in zip(ups[1:], UP_PIECES[1:]):
        got_up = jnp.where(step >= begin, ref[...], got_up)
    got_dn = downs[0][...]
    for ref, (begin, _) in zip(downs[1:], DOWN_PIECES[1:]):
        got_dn = jnp.where(step >= begin, ref[...], got_dn)
    up_ref[0] = gup_ref[...] + got_up.astype(F32)
    dn_ref[0] = jnp.transpose(gdn_ref[...] + got_dn.astype(F32))


def smem_spec():
    return pl.BlockSpec(memory_space=pltpu.SMEM)


def params():
    return pltpu.CompilerParams(vmem_limit_bytes=VMEM_LIMIT)


def cost(micros):
    return pl.CostEstimate(
        flops=int(micros * 1e9), transcendentals=0, bytes_accessed=int(micros * 2e6)
    )


def struct(shape, kind):
    return jax.ShapeDtypeStruct(shape, kind)


def after(value, *others):
    return lax.optimization_barrier((value, *others))[0]


def on_device(
    images,
    cotangent,
    lengths,
    routes,
    attn_norm_gain,
    attn_norm_bias,
    qkv_weight,
    query_value_bias,
    proj_weight,
    proj_bias,
    moe_norm_gain,
    moe_norm_bias,
    router_weight,
    up_weight,
    up_bias,
    down_weight,
    down_bias,
):
    seq_count = lax.axis_size("seq")
    dp_count = lax.axis_size("dp")
    count = images.shape[0] // MICRO
    local_len = images.shape[1]
    width = images.shape[2]
    tokens = count * local_len
    full_len = local_len * seq_count
    experts = router_weight.shape[1]
    hidden = up_weight.shape[2]
    capacity = (5 * tokens * TOP + 4 * experts - 1) // (4 * experts)
    room = (capacity + window(capacity, MICRO - 1)[1] + 8) // 8 * 8
    assert all(window(capacity, mb)[1] + capacity < room for mb in range(MICRO))
    assert window(capacity, 1)[0] + room <= window(capacity, 2)[0] + 8
    slots = experts * room
    assert up_weight.shape[0] == 1 and experts == dp_count
    assert experts + VEC <= LANES and capacity <= LANES
    meta = jnp.stack([lax.axis_index("dp"), lax.axis_index("seq")]).astype(jnp.int32)
    packed_width = 4 * width + LANES

    def full(shape):
        return pl.BlockSpec(shape, lambda i: (0,) * len(shape))

    def token_spec(mb):
        return pl.BlockSpec((count, local_len, width), lambda i: (mb, 0, 0))

    def table_spec(mb, shape):
        return pl.BlockSpec((1, *shape), lambda i: (mb, 0, 0))

    def block_spec(mb):
        return pl.BlockSpec((experts, room, width), lambda i: (0, mb, 0))

    def window_spec(mb=None):
        def at(i):
            return (0, (capacity * (i if mb is None else mb)) // 8 * 8, 0)

        return pl.BlockSpec((pl.Element(experts), pl.Element(room), pl.Element(width)), at)

    any_spec = pl.BlockSpec(memory_space=pl.ANY)
    other_spec = lambda mb: pl.BlockSpec(
        (seq_count - 1, count, local_len, width), lambda i: (0, max(mb - 1, 0), 0, 0)
    )
    assert hidden // FF_BLOCK == UP_PIECES[-1][1] == DOWN_PIECES[-1][1]

    def piece_spec(begin, end):
        return pl.BlockSpec(
            (width, FF_BLOCK), lambda i: (0, jnp.clip(i - begin, 0, end - begin - 1))
        )

    misc_spec = pl.BlockSpec((width, LANES), lambda i: (0, 4 * width // LANES))
    moved = struct((experts, room, width), BF)
    merged = struct((experts, window(capacity, MICRO - 1)[0] + room, width), BF)
    tailed = struct((experts, (MICRO - 1) * room, width), BF)

    def seq_shift(array, j):
        return lax.ppermute(array, "seq", [((i + j) % seq_count, i) for i in range(seq_count)])

    others = []
    for part in (images[:count], images[count:]):
        moved_images = jnp.stack([seq_shift(part, j) for j in range(1, seq_count)])
        others.append(moved_images)

    sent_dy, prow, pcol = pl.pallas_call(
        functools.partial(place_kernel, experts, room, capacity),
        grid=(MICRO,),
        in_specs=[
            pl.BlockSpec((1, 1, 1, TOP, tokens), lambda i: (0, i, 0, 0, 0)),
            pl.BlockSpec((count, local_len, width), lambda i: (i, 0, 0)),
        ],
        out_specs=[
            pl.BlockSpec(merged.shape, lambda i: (0, 0, 0)),
            pl.BlockSpec((1, TOP, tokens), lambda i: (i, 0, 0)),
            pl.BlockSpec((1, tokens, 8), lambda i: (i, 0, 0)),
        ],
        out_shape=[
            merged,
            struct((MICRO, TOP, tokens), jnp.int32),
            struct((MICRO, tokens, 8), jnp.int32),
        ],
        compiler_params=params(),
        cost_estimate=cost(8),
        name="place",
    )(jnp.swapaxes(routes, 3, 4), cotangent)

    vectors = jnp.concatenate(
        [
            jnp.stack([attn_norm_gain, attn_norm_bias]),
            query_value_bias,
            jnp.stack([proj_bias, moe_norm_gain, moe_norm_bias, jnp.zeros_like(proj_bias)]),
        ],
        axis=0,
    )
    shard = router_weight.shape[0]
    bits = dp_count.bit_length() - 1
    assert dp_count == 1 << bits

    def across(value, offset):
        return lax.ppermute(value, "dp", [(i, i ^ offset) for i in range(dp_count)])

    def gather_rows(own, gate):
        quarter = dp_count // 4
        pieces = [own, *[across(own, k * quarter) for k in (1, 2, 3)]]
        held = [jnp.stack(pieces)]
        offsets = [[0, quarter, 2 * quarter, 3 * quarter]]
        for bit in reversed(range(bits - 2)):
            if bit == 0:
                held[-1] = after(held[-1], gate)
            held += [across(h, 1 << bit) for h in held]
            offsets += [[k ^ (1 << bit) for k in known] for known in offsets]
        return pl.pallas_call(
            functools.partial(assemble_kernel, offsets, shard),
            grid=(1,),
            in_specs=[smem_spec(), *[full(h.shape) for h in held]],
            out_specs=full((dp_count * shard, packed_width)),
            out_shape=struct((dp_count * shard, packed_width), BF),
            compiler_params=params(),
            cost_estimate=cost(3),
            name="assemble",
        )(meta, *held), pieces[1:]

    def halve(value, bit):
        mine = lax.bitwise_and(lax.shift_right_logical(lax.axis_index("dp"), bit), 1)
        value = value.reshape(-1, 2, shard, packed_width)
        keep = lax.dynamic_index_in_dim(value, mine, 1, keepdims=False)
        give = lax.dynamic_index_in_dim(value, 1 - mine, 1, keepdims=False).astype(BF)
        return keep.astype(F32) + across(give, 1 << bit).astype(F32)

    def scatter_far(value):
        high = lax.shift_right_logical(lax.axis_index("dp"), bits - 2)
        result = lax.dynamic_index_in_dim(value, high, 0, keepdims=False)
        for offset in (1, 2, 3):
            give = lax.dynamic_index_in_dim(
                value, lax.bitwise_xor(high, offset), 0, keepdims=False
            )
            result = result + across(give.astype(BF), offset << (bits - 2)).astype(F32)
        return result

    pack_args = (qkv_weight, proj_weight, router_weight.T, vectors)
    packed_shard = pl.pallas_call(
        functools.partial(pack_kernel, experts),
        grid=(1,),
        in_specs=[full(a.shape) for a in pack_args],
        out_specs=full((shard, packed_width)),
        out_shape=struct((shard, packed_width), BF),
        compiler_params=params(),
        cost_estimate=cost(1),
        name="pack",
    )(*pack_args)

    def exchange(array):
        return lax.all_to_all(array, "dp", split_axis=0, concat_axis=0, tiled=True)

    packed, near = gather_rows(packed_shard, others[1])
    dyb = exchange(after(sent_dy, *near, others[0]))

    def forward(mb):
        cfg = (count, local_len, seq_count, width, experts, room)
        outs = [
            ((experts, room, width), BF),
            ((tokens, width), F32),
            ((tokens, LANES), F32),
            ((tokens, width), BF),
            ((width, tokens), BF),
            ((tokens, width), BF),
            ((count * full_len, width), BF),
            ((count * full_len, width), BF),
            ((count * 8, local_len), F32),
            ((width, count * full_len), BF),
        ]
        return pl.pallas_call(
            functools.partial(forward_kernel, cfg, mb),
            grid=(1,),
            in_specs=[
                smem_spec(),
                smem_spec(),
                token_spec(mb),
                other_spec(mb),
                full((width, packed_width)),
                table_spec(mb, (TOP, tokens)),
            ],
            out_specs=[full(s) for s, _ in outs],
            out_shape=[struct(s, k) for s, k in outs],
            scratch_shapes=[
                pltpu.VMEM((tokens, width), BF),
                pltpu.VMEM((local_len, LANES), F32),
            ],
            compiler_params=params(),
            cost_estimate=cost(11),
            name="forward",
        )(meta, lengths, images, others[min(mb, 1)], packed, prow)

    def expert(mb, buf, results, tail_back, totals):
        first = mb == 0
        last = mb == MICRO - 1
        cfg = (experts, room, capacity, window(capacity, mb)[1], width)
        wide = lambda: pl.BlockSpec((width, FF_BLOCK), lambda i: (0, i))
        thin = lambda: pl.BlockSpec((1, FF_BLOCK), lambda i: (0, i))
        in_specs = [
            smem_spec(),
            full((experts, room, width)),
            window_spec(mb),
            misc_spec,
            pl.BlockSpec((1, width, FF_BLOCK), lambda i: (0, 0, i)),
            thin(),
            pl.BlockSpec((1, FF_BLOCK, width), lambda i: (0, i, 0)),
            full((1, width)),
        ]
        total_specs = [wide(), wide(), thin(), full((1, width))]
        args = [meta, buf, dyb, packed, up_weight, up_bias, down_weight, down_bias]
        aliases = {}
        if not first:
            aliases = {len(args): 0}
            aliases.update({len(args) + 1 + j: 2 + j for j in range(4)})
            in_specs += [window_spec(mb), *total_specs]
            args += [results, *totals]
        if mb >= 2:
            aliases[len(args)] = 1
            in_specs += [any_spec]
            args += [tail_back]
        outs = pl.pallas_call(
            functools.partial(expert_kernel, cfg, first, last),
            grid=(hidden // FF_BLOCK,),
            in_specs=in_specs,
            out_specs=[window_spec(mb), block_spec(max(mb - 1, 0)), *total_specs]
            + ([piece_spec(*p) for p in PIECES] if last else []),
            out_shape=[
                merged,
                moved if first else tailed,
                struct((width, hidden), F32),
                struct((width, hidden), F32),
                struct((1, hidden), F32),
                struct((1, width), F32),
            ]
            + (
                [struct((width, (end - begin) * FF_BLOCK), BF) for begin, end in PIECES]
                if last
                else []
            ),
            scratch_shapes=[
                pltpu.VMEM((slots, width), BF),
                pltpu.VMEM((width, slots), BF),
                pltpu.VMEM((slots, width), BF),
                pltpu.VMEM((width, slots), BF),
                pltpu.VMEM((slots, width), F32),
                pltpu.VMEM((slots, width), F32),
            ],
            input_output_aliases=aliases,
            compiler_params=params(),
            cost_estimate=cost(19),
            name="expert",
        )(*args)
        return outs[0], outs[1], tuple(outs[2:])

    def backward(mb, dback, saved, totals):
        first = mb == 0
        last = mb == MICRO - 1
        cfg = (count, local_len, seq_count, width, experts, room, capacity)
        middle, gate, second, oT, q, k, v, lse, n1T = saved
        whole = [gate, middle, second]
        heads = [oT, packed, q, k, v, lse, n1T]
        args = [meta, lengths, dback, pcol, *whole, cotangent, *heads, images, others[min(mb, 1)]]
        in_specs = [
            smem_spec(),
            smem_spec(),
            block_spec(max(mb - 1, 0)),
            table_spec(mb, (tokens, 8)),
            *[full(a.shape) for a in whole],
            token_spec(mb),
            *[full(a.shape) for a in heads],
            token_spec(mb),
            other_spec(mb),
        ]
        aliases = {}
        if not first:
            in_specs += [full(a.shape) for a in totals]
            args += list(totals)
            if not last:
                aliases = {len(args) - 2: 3, len(args) - 1: 4}
        outs = [
            ((tokens, width), F32),
            ((seq_count - 1, tokens, width), BF),
            ((tokens, width), F32),
            ((width, packed_width), BF) if last else ((width, 4 * width), F32),
            ((LANES, width), F32),
        ]
        return pl.pallas_call(
            functools.partial(backward_kernel, cfg, mb, first, last),
            grid=(1,),
            in_specs=in_specs,
            out_specs=[full(s) for s, _ in outs],
            out_shape=[struct(s, t) for s, t in outs],
            scratch_shapes=[
                pltpu.VMEM((tokens, width), BF),
                pltpu.VMEM((width, local_len), F32),
                pltpu.VMEM((full_len, 2 * width), BF),
            ],
            input_output_aliases=aliases,
            compiler_params=params(),
            cost_estimate=cost(0.1 if last else 17),
            name="backward",
        )(*args)

    def into(kernel, mb, args, specs, previous, micros, name):
        aliases = {}
        if previous is not None:
            aliases = {len(args): 0}
            args = [*args, previous]
            specs = [*specs, any_spec]
        return pl.pallas_call(
            kernel,
            grid=(1,),
            in_specs=specs,
            out_specs=token_spec(mb),
            out_shape=struct(images.shape, BF),
            input_output_aliases=aliases,
            compiler_params=params(),
            cost_estimate=cost(micros),
            name=name,
        )(*args)

    def finish(mb, own, got, dm, previous):
        cfg = (count, local_len, seq_count, width, experts)
        specs = [full(own.shape), full(got.shape), token_spec(mb), full(dm.shape), misc_spec]
        return into(
            functools.partial(input_kernel, cfg),
            mb,
            [own, got, images, dm, packed],
            specs,
            previous,
            0.1,
            "finish",
        )

    def mix(back):
        cfg = (count, local_len, width, experts, room)
        tables = sum([[saved[mb][1], saved[mb][0]] for mb in range(MICRO)], [])
        return pl.pallas_call(
            functools.partial(mix_kernel, cfg),
            grid=(MICRO,),
            in_specs=[
                window_spec(),
                pl.BlockSpec((1, tokens, 8), lambda i: (i, 0, 0)),
                *[full(t.shape) for t in tables],
            ],
            out_specs=pl.BlockSpec((count, local_len, width), lambda i: (i, 0, 0)),
            out_shape=struct(images.shape, BF),
            compiler_params=params(),
            cost_estimate=cost(0.1),
            name="mix",
        )(back, pcol, *tables)

    swap = [(i, (i + 1) % seq_count) for i in range(seq_count)]

    def seq_sum(value):
        if seq_count == 2:
            return value + lax.ppermute(value.astype(BF), "seq", swap).astype(F32)
        return lax.psum(value.astype(BF), "seq").astype(F32)

    passed = [forward(mb) for mb in range(MICRO)]
    saved = [outs[1:] for outs in passed]
    bufs = []
    for mb in range(MICRO):
        first_gate = (dyb,) if mb == 0 else ()
        bufs.append(exchange(after(passed[mb][0], *first_gate)))
    totals = None
    results = None
    ready = [None, None]
    for mb in range(MICRO):
        results, ready[min(mb, 1)], totals = expert(mb, bufs[mb], results, ready[1], totals)
    gup, gdn, gbias, gdbias, *pieces = totals
    arrived = []
    if seq_count == 2:
        arrived = [lax.ppermute(piece, "seq", swap) for piece in pieces]
    dense = None
    owns = []
    gots = []
    dms = []
    dbacks = [exchange(ready[0]), exchange(ready[1])]
    if arrived:
        dbacks[1], arrived[0] = lax.optimization_barrier((dbacks[1], arrived[0]))
    for mb in range(MICRO):
        dback = dbacks[min(mb, 1)]
        if mb == 2 and arrived:
            dense, arrived[1] = lax.optimization_barrier((dense, arrived[1]))
        own, oth, dm, *dense = backward(mb, dback, saved[mb], dense)
        owns.append(own)
        dms.append(dm)
        gots.append(
            jnp.stack(
                [
                    lax.ppermute(
                        oth[j - 1], "seq", [(i, (i + j) % seq_count) for i in range(seq_count)]
                    )
                    for j in range(1, seq_count)
                ]
            )
        )
    back = exchange(after(results, dbacks[1]))
    part = halve(after(dense[0], *arrived[2:4], gots[0]), 0)
    mid = part

    if seq_count == 2:
        wide = lambda: pl.BlockSpec((width, FF_BLOCK), lambda i: (0, i))
        final_up, final_down = pl.pallas_call(
            sum_kernel,
            grid=(hidden // FF_BLOCK,),
            in_specs=[wide(), wide(), *[piece_spec(*p) for p in PIECES]],
            out_specs=[
                pl.BlockSpec((1, width, FF_BLOCK), lambda i: (0, 0, i)),
                pl.BlockSpec((1, FF_BLOCK, width), lambda i: (0, i, 0)),
            ],
            out_shape=[struct((1, width, hidden), F32), struct((1, hidden, width), F32)],
            compiler_params=params(),
            cost_estimate=cost(0.1),
            name="sum_experts",
        )(after(gup, mid), gdn, *arrived)
    else:
        sums = [lax.psum(piece, "seq").astype(F32) for piece in pieces]
        ups, downs = sums[: len(UP_PIECES)], sums[len(UP_PIECES) :]
        final_up = jnp.concatenate(ups, axis=1)[None]
        final_down = jnp.swapaxes(jnp.concatenate(downs, axis=1), 0, 1)[None]
    biases = seq_sum(jnp.concatenate([gbias, gdbias], axis=1))
    for bit in range(1, bits - 2):
        part = halve(part, bit)
    part, final_up, biases, back = lax.optimization_barrier((part, final_up, biases, back))
    shards = scatter_far(part)
    out = mix(back)
    grads = None
    for mb in range(MICRO):
        if mb == MICRO - 1:
            shards, out, grads = lax.optimization_barrier((shards, out, grads))
        grads = finish(mb, after(owns[mb], part), gots[mb], dms[mb], grads)
    final_up_shift = biases[:, :hidden]
    final_down_shift = biases[:, hidden:]

    shards = seq_sum(shards)
    misc = 4 * width + experts
    return (
        out,
        grads,
        shards[:, misc],
        shards[:, misc + 1],
        shards[:, : 3 * width],
        jnp.stack([shards[:, misc + 2], shards[:, misc + 3]]),
        shards[:, 3 * width : 4 * width],
        shards[:, misc + 4],
        shards[:, misc + 5],
        shards[:, misc + 6],
        shards[:, 4 * width : misc],
        final_up,
        final_up_shift,
        final_down,
        final_down_shift,
    )


def solution(mesh):
    return jax.shard_map(
        on_device,
        mesh=mesh,
        in_specs=(
            P("dp", "seq", None),
            P("dp", "seq", None),
            P("dp"),
            P("dp", None, "seq", None, None),
            P("dp"),
            P("dp"),
            P("dp", None),
            P(None, "dp"),
            P("dp", None),
            P("dp"),
            P("dp"),
            P("dp"),
            P("dp", None),
            P("dp", None, None),
            P("dp", None),
            P("dp", None, None),
            P("dp", None),
        ),
        out_specs=(
            P("dp", "seq", None),
            P("dp", "seq", None),
            P("dp"),
            P("dp"),
            P("dp", None),
            P(None, "dp"),
            P("dp", None),
            P("dp"),
            P("dp"),
            P("dp"),
            P("dp", None),
            P("dp", None, None),
            P("dp", None),
            P("dp", None, None),
            P("dp", None),
        ),
        check_vma=False,
    )
```

```python
import functools

import jax
import jax.numpy as jnp
from jax import lax
from jax.experimental import pallas as pl
from jax.experimental.pallas import tpu as pltpu
from jax.sharding import PartitionSpec as P

HD = 64
TOP = 2
MICRO = 3
BF = jnp.bfloat16
F32 = jnp.float32
EPS = 1e-06
LANES = 128
VEC = 8
FF_BLOCK = 512
UP_PIECES = ((0, 2), (2, 4))
DOWN_PIECES = ((0, 2), (2, 3), (3, 4))
PIECES = UP_PIECES + DOWN_PIECES
VMEM_LIMIT = 60 * 1024 * 1024


def mm(left, right):
    return jnp.dot(left, right, preferred_element_type=F32)


def mm_nt(left, right):
    return lax.dot_general(
        left, right, (((1,), (1,)), ((), ())), preferred_element_type=F32
    )


def iota(shape, dim):
    return lax.broadcasted_iota(jnp.int32, shape, dim)


def norm_parts(values):
    average = jnp.mean(values, axis=-1, keepdims=True)
    centred = values - average
    spread = jnp.mean(centred * centred, axis=-1, keepdims=True)
    scale = lax.rsqrt(spread + EPS)
    return centred * scale, scale


def norm_pull(unit, scale, gain, cotangent):
    inner = cotangent * gain
    mean_inner = jnp.mean(inner, axis=-1, keepdims=True)
    mean_unit = jnp.mean(inner * unit, axis=-1, keepdims=True)
    return scale * (inner - mean_inner - unit * mean_unit)


def misc_rows(w_ref, start):
    return jnp.transpose(w_ref[:, start : start + LANES].astype(F32))


def pack_kernel(experts, qkv_ref, proj_ref, router_ref, vec_ref, out_ref):
    width = proj_ref.shape[1]
    shard = proj_ref.shape[0]
    out_ref[:, : 3 * width] = qkv_ref[...]
    out_ref[:, 3 * width : 4 * width] = proj_ref[...]
    rows = jnp.concatenate([router_ref[...].astype(F32), vec_ref[...].astype(F32)], axis=0)
    columns = jnp.transpose(rows)
    tail = jnp.zeros((shard, LANES - columns.shape[1]), F32)
    out_ref[:, 4 * width :] = jnp.concatenate([columns, tail], axis=1).astype(BF)


def assemble_kernel(sources, shard, meta_ref, *refs):
    out_ref = refs[-1]
    for ref, offsets in zip(refs[:-1], sources):
        for at, offset in enumerate(offsets):
            row = jnp.bitwise_xor(meta_ref[0], offset) * shard
            out_ref[pl.ds(pl.multiple_of(row, shard), shard), :] = ref[at]


def window(capacity, mb):
    start = capacity * mb // 8 * 8
    return start, capacity * mb - start


def place_kernel(experts, room, capacity, routes_ref, dy_ref, send_ref, prow_ref, pcol_ref):
    for mb in range(MICRO):

        @pl.when(pl.program_id(0) == mb)
        def _():
            place_part(
                experts, room, window(capacity, mb), routes_ref, dy_ref, send_ref, prow_ref, pcol_ref
            )


def place_part(experts, room, where, routes_ref, dy_ref, send_ref, prow_ref, pcol_ref):
    start, shift = where
    tokens = routes_ref.shape[4]
    slots = experts * room
    rows = routes_ref[0, 0, 0]
    first_row = rows[0:1]
    second_row = rows[1:2]
    tall = jnp.concatenate([rows.astype(F32), jnp.zeros((LANES - TOP, tokens), F32)], axis=0)
    cols = jnp.transpose(tall)[:, 0:8].astype(jnp.int32)
    hot_first = (iota((experts, tokens), 0) == first_row).astype(F32)
    hot_second = (iota((experts, tokens), 0) == second_row).astype(F32)
    earlier = (iota((tokens, tokens), 0) < iota((tokens, tokens), 1)).astype(BF)
    before = mm((hot_first + hot_second).astype(BF), earlier)
    in_first = jnp.sum(before * hot_first, axis=0, keepdims=True).astype(jnp.int32)
    in_second = jnp.sum((before + hot_first) * hot_second, axis=0, keepdims=True).astype(jnp.int32)
    place_first = first_row * room + in_first + shift
    place_second = second_row * room + in_second + shift
    prow_ref[0, 0:1, :] = place_first
    prow_ref[0, 1:2, :] = place_second
    slot_of = iota((slots, tokens), 0)
    hot = jnp.where((slot_of == place_first) | (slot_of == place_second), 1.0, 0.0).astype(BF)
    flat = dy_ref[...].reshape(tokens, dy_ref.shape[-1])
    rows = mm(hot, flat)
    for e in range(experts):
        block = rows[e * room : (e + 1) * room].astype(BF)
        if shift:
            send_ref[e, start : start + 8] = send_ref[e, start : start + 8] + block[:8]
            send_ref[e, start + 8 : start + room] = block[8:]
        else:
            send_ref[e, start : start + room] = block
    first_col = cols[:, 0:1]
    second_col = cols[:, 1:2]
    hot_first = (iota((tokens, experts), 1) == first_col).astype(F32)
    hot_second = (iota((tokens, experts), 1) == second_col).astype(F32)
    later = (iota((tokens, tokens), 1) < iota((tokens, tokens), 0)).astype(BF)
    before = mm(later, (hot_first + hot_second).astype(BF))
    in_first = jnp.sum(before * hot_first, axis=1, keepdims=True).astype(jnp.int32)
    in_second = jnp.sum((before + hot_first) * hot_second, axis=1, keepdims=True).astype(jnp.int32)
    lane = iota((tokens, 8), 1)
    table = jnp.zeros((tokens, 8), jnp.int32)
    for at, col in enumerate(
        (
            first_col * room + in_first + shift,
            second_col * room + in_second + shift,
            first_col,
            second_col,
            in_first + shift,
            in_second + shift,
        )
    ):
        table = jnp.where(lane == at, col, table)
    pcol_ref[0] = table


def forward_kernel(
    cfg,
    mb,
    meta_ref,
    len_ref,
    own_ref,
    oth_ref,
    w_ref,
    prow_ref,
    send_ref,
    middle_ref,
    gate_ref,
    second_ref,
    oT_ref,
    q_ref,
    k_ref,
    v_ref,
    lse_ref,
    n1T_ref,
    att_ref,
    logs_ref,
):
    images, local_len, seq_count, width, experts, room = cfg
    full_len = local_len * seq_count
    tokens = images * local_len
    slots = experts * room
    misc_at = 4 * width
    rows = misc_rows(w_ref, misc_at)

    def vec(j):
        return rows[experts + j : experts + j + 1, :]

    here = meta_ref[1]
    lane = iota((1, LANES), 1)
    low_half = (lane < HD).astype(BF)
    high_half = (lane >= HD).astype(BF)
    for b in range(images):
        blocks = [own_ref[b]] + [oth_ref[j, b] for j in range(seq_count - 1)]
        full = jnp.concatenate(blocks, axis=0).astype(F32)
        unit, _ = norm_parts(full)
        normed = (unit * vec(0) + vec(1)).astype(BF)
        n1T_ref[:, b * full_len : (b + 1) * full_len] = jnp.transpose(normed)
        span = slice(b * local_len, (b + 1) * local_len)
        wide = slice(b * full_len, (b + 1) * full_len)
        queries = (mm(normed[:local_len], w_ref[:, :width]) + vec(2)).astype(BF)
        q_ref[span, :] = queries * jnp.asarray(HD**-0.5, BF)
        k_ref[wide, :] = mm(normed, w_ref[:, width : 2 * width]).astype(BF)
        v_ref[wide, :] = (mm(normed, w_ref[:, 2 * width : 3 * width]) + vec(3)).astype(BF)
        kpos = iota((1, full_len), 1)
        shift = jnp.zeros((1, full_len), jnp.int32)
        for j in range(seq_count):
            origin = lax.rem(here + j, seq_count) * local_len - j * local_len
            shift = jnp.where(kpos >= j * local_len, origin, shift)
        valid = (kpos + shift) < len_ref[mb * images + b]
        logs_ref[...] = jnp.zeros_like(logs_ref)

        def heads(blk, carry):
            at = pl.ds(pl.multiple_of(blk * LANES, LANES), LANES)
            q_blk = q_ref[span, at]
            k_blk = k_ref[wide, at]
            v_blk = v_ref[wide, at]
            outs = []
            for side, keep in enumerate((low_half, high_half)):
                scores = mm_nt(q_blk * keep, k_blk)
                scores = jnp.where(valid, scores, -1e30)
                highest = jnp.max(scores, axis=1, keepdims=True)
                powers = jnp.exp(scores - highest)
                total = jnp.sum(powers, axis=1, keepdims=True)
                probs = (powers * (1.0 / total)).astype(BF)
                outs.append(mm(probs, v_blk))
                logs_ref[...] = jnp.where(
                    lane == 2 * blk + side, highest + jnp.log(total), logs_ref[...]
                )
            att_ref[span, at] = jnp.where(lane < HD, outs[0], outs[1]).astype(BF)
            return carry

        lax.fori_loop(0, width // LANES, heads, 0)
        lse_ref[b * 8 : b * 8 + 8, :] = jnp.transpose(logs_ref[...])[0:8, :]
    attended = att_ref[...]
    oT_ref[...] = jnp.transpose(attended)
    branch = mm(attended, w_ref[:, 3 * width : 4 * width]) + vec(4)
    middle = own_ref[...].reshape(tokens, width).astype(F32) + branch
    middle_ref[...] = middle
    unit, _ = norm_parts(middle)
    second = (unit * vec(5) + vec(6)).astype(BF)
    second_ref[...] = second
    gate_ref[...] = gates(mm(second, w_ref[:, misc_at : misc_at + LANES]), experts)
    slot_of = iota((slots, tokens), 0)
    hot = jnp.where(
        (slot_of == prow_ref[0, 0:1, :]) | (slot_of == prow_ref[0, 1:2, :]), 1.0, 0.0
    ).astype(BF)
    sent = mm(hot, second)
    for e in range(experts):
        send_ref[e] = sent[e * room : (e + 1) * room].astype(BF)


def gates(logits, experts):
    real = iota((1, LANES), 1) < experts
    logits = jnp.where(real, logits, -1e30)
    powers = jnp.where(real, jnp.exp(logits - jnp.max(logits, axis=1, keepdims=True)), 0.0)
    return powers / jnp.sum(powers, axis=1, keepdims=True)


def expert_kernel(cfg, first, last, *refs):
    groups, room, capacity, shift, width = cfg
    meta_ref, buf_ref, dyb_ref, wm_ref, up_ref, ub_ref, down_ref, db_ref = refs[:8]
    refs = refs[8:]
    if not first:
        r_in, gup_in, gdn_in, gb_in, gdb_in = refs[:5]
        refs = refs[6 if last else 5 :]
    r_ref, dbuf_ref, gup_ref, gdn_ref, gb_ref, gdb_ref = refs[:6]
    refs = refs[6:]
    if last:
        lows = refs[: len(PIECES)]
        refs = refs[len(PIECES) :]
    (
        flat_s,
        flatT_s,
        dr_s,
        drT_s,
        racc_s,
        dacc_s,
    ) = refs
    slots = groups * room
    step = pl.program_id(0)
    experts = groups

    @pl.when(step == 0)
    def _():
        flat = buf_ref[...].astype(F32).reshape(slots, width).astype(BF)
        flat_s[...] = flat
        flatT_s[...] = jnp.transpose(flat)
        gate = gates(mm(flat, wm_ref[...]), experts)
        mine = iota((1, LANES), 1) == meta_ref[0]
        mine_gate = jnp.sum(jnp.where(mine, gate, 0.0), axis=1, keepdims=True)
        at = iota((groups, room, 1), 1)
        own = (at >= shift) & (at < shift + capacity)
        dy = jnp.where(own, dyb_ref[...].astype(F32), 0.0)
        dr = (dy.reshape(slots, width) * mine_gate).astype(BF)
        dr_s[...] = dr
        drT_s[...] = jnp.transpose(dr)
        shift_sum = jnp.sum(dr.astype(F32), axis=0, keepdims=True)
        gdb_ref[...] = shift_sum if first else gdb_in[...] + shift_sum
        racc_s[...] = jnp.zeros_like(racc_s)
        dacc_s[...] = jnp.zeros_like(dacc_s)

    flat = flat_s[...]
    dr = dr_s[...]
    hidden = mm(flat, up_ref[0]) + ub_ref[...].astype(F32)
    half_erf = 0.5 * lax.erf(hidden * (0.5**0.5)) + 0.5
    active = (hidden * half_erf).astype(BF)
    slope = half_erf + hidden * (jnp.exp(-0.5 * hidden * hidden) * 0.3989422804014327)
    racc_s[...] += mm(active, down_ref[0])
    grad_pre = mm_nt(dr, down_ref[0]) * slope
    low_pre = grad_pre.astype(BF)
    dacc_s[...] += mm_nt(low_pre, up_ref[0])
    gup = mm(flatT_s[...], low_pre)
    gdn = mm(drT_s[...], active)
    gbias = jnp.sum(low_pre.astype(F32), axis=0, keepdims=True)
    if not first:
        gup = gup_in[...] + gup
        gdn = gdn_in[...] + gdn
        gbias = gb_in[...] + gbias
    gup_ref[...] = gup
    gdn_ref[...] = gdn
    gb_ref[...] = gbias
    if last:
        for at, (low, (begin, end)) in enumerate(zip(lows, PIECES)):
            value = gup if at < len(UP_PIECES) else gdn

            @pl.when((step >= begin) & (step < end))
            def _(low=low, value=value):
                low[...] = value.astype(BF)

    @pl.when(step == pl.num_programs(0) - 1)
    def _():
        result = (racc_s[...] + db_ref[...].astype(F32)).astype(BF)
        for e in range(groups):
            block = result[e * room : (e + 1) * room]
            if shift:
                older = iota((8, 1), 0) < shift
                head = jnp.where(older, r_in[e, :8].astype(F32), block[:8].astype(F32))
                r_ref[e, :8] = head.astype(BF)
                r_ref[e, 8:] = block[8:]
            else:
                r_ref[e] = block
        dy = dyb_ref[...].astype(F32).reshape(slots, width)
        dgate = jnp.sum(dy * result.astype(F32), axis=1, keepdims=True).reshape(groups, room, 1)
        spread = jnp.where(
            iota((groups, room, LANES), 2) == iota((groups, room, LANES), 1), dgate, 0.0
        )
        as_row = jnp.sum(spread, axis=1, keepdims=True)
        high = as_row.astype(BF).astype(F32)
        tail = jnp.zeros((groups, 1, width - 2 * LANES), F32)
        as_row = jnp.concatenate([high, as_row - high, tail], axis=2)
        back = dacc_s[...].reshape(groups, room, width)
        back = jnp.where(iota((groups, room, 1), 1) == room - 1, as_row, back).astype(BF)
        for e in range(groups):
            dbuf_ref[e] = back[e]


def backward_kernel(cfg, mb, first, last, *refs):
    images, local_len, seq_count, width, experts, room, capacity = cfg
    (
        meta_ref,
        len_ref,
        dback_ref,
        pcol_ref,
        gate_ref,
        middle_ref,
        second_ref,
        dy_ref,
        oT_ref,
        w_ref,
        q_ref,
        k_ref,
        v_ref,
        lse_ref,
        n1T_ref,
        own_ref,
        oth_ref,
    ) = refs[:17]
    refs = refs[17:]
    if not first:
        g_in, mrow_in = refs[:2]
        refs = refs[2:]
    down_own, down_oth, dm_ref = refs[:3]
    refs = refs[3:]
    if last:
        low_ref = refs[0]
        refs = refs[1:]
    else:
        g_ref = refs[0]
        refs = refs[1:]
    mrow_ref, do_s, dqT_s, dkv_s = refs

    def add_dense(at, value):
        if not first:
            value = g_in[:, at] + value
        if last:
            low_ref[:, at] = value.astype(BF)
        else:
            g_ref[:, at] = value

    full_len = local_len * seq_count
    tokens = images * local_len
    slots = experts * room
    misc_at = 4 * width
    rows = misc_rows(w_ref, misc_at)
    here = meta_ref[1]

    def vec(j):
        return rows[experts + j : experts + j + 1, :]

    dback = dback_ref[...].astype(F32)
    back_rows = dback.reshape(slots, width).astype(BF)
    slot_of = iota((tokens, slots), 1)
    hot = jnp.where(
        (slot_of == pcol_ref[0, :, 0:1]) | (slot_of == pcol_ref[0, :, 1:2]), 1.0, 0.0
    ).astype(BF)
    from_experts = mm(hot, back_rows)
    spare = jnp.where(iota((experts, room, 1), 1) == room - 1, dback[:, :, : 2 * LANES], 0.0)
    spare = jnp.sum(spare, axis=1)
    spare = jnp.concatenate(
        [spare, jnp.zeros((LANES - experts, 2 * LANES), F32)], axis=0
    ).astype(BF)
    lane = iota((tokens, LANES), 1)
    pulled = jnp.zeros((tokens, LANES), F32)
    for k in range(TOP):
        within = jnp.where(lane == pcol_ref[0, :, 4 + k : 5 + k], 1.0, 0.0).astype(BF)
        found = mm_nt(jnp.concatenate([within, within], axis=1), spare)
        pulled = pulled + jnp.where(lane == pcol_ref[0, :, 2 + k : 3 + k], found, 0.0)
    gate = gate_ref[...]
    dlogit = gate * (pulled - jnp.sum(gate * pulled, axis=1, keepdims=True))
    dlogit_low = dlogit.astype(BF)
    mrow_ref[...] = mm(jnp.transpose(dlogit_low.astype(F32)).astype(BF), second_ref[...])
    dn2 = from_experts + mm_nt(dlogit_low, w_ref[:, misc_at : misc_at + LANES])
    unit, scale = norm_parts(middle_ref[...])
    dy = dy_ref[...].reshape(tokens, width).astype(F32)
    dm = dy + norm_pull(unit, scale, vec(5), dn2)
    dm_ref[...] = dm
    da = dm.astype(BF)
    gproj = mm(oT_ref[...], da)
    proj = slice(3 * width, 4 * width)
    add_dense(proj, gproj)
    do_s[...] = mm_nt(da, w_ref[:, proj]).astype(BF)
    half_lane = iota((1, LANES), 1)
    low_half = (half_lane < HD).astype(BF)
    high_half = (half_lane >= HD).astype(BF)
    gqkv = [None, None]
    bias_q = jnp.zeros((1, width), F32)
    bias_v = jnp.zeros((1, width), F32)
    gain_sum = jnp.zeros((1, width), F32)
    shift_sum = jnp.zeros((1, width), F32)
    for b in range(images):
        span = slice(b * local_len, (b + 1) * local_len)
        wide = slice(b * full_len, (b + 1) * full_len)
        kpos = iota((full_len, 1), 0)
        shift = jnp.zeros((full_len, 1), jnp.int32)
        for j in range(seq_count):
            origin = lax.rem(here + j, seq_count) * local_len - j * local_len
            shift = jnp.where(kpos >= j * local_len, origin, shift)
        valid = (kpos + shift) < len_ref[mb * images + b]

        def heads(blk, carry):
            at = pl.ds(pl.multiple_of(blk * LANES, LANES), LANES)
            q_blk = q_ref[span, at]
            k_blk = k_ref[wide, at]
            v_blk = v_ref[wide, at]
            do_blk = do_s[span, at]
            kT_blk = jnp.transpose(k_blk)
            dvs = []
            dks = []
            dqs = []
            for side, keep in enumerate((low_half, high_half)):
                scores = mm_nt(k_blk, q_blk * keep)
                logs = lse_ref[pl.ds(b * 8 + 2 * blk + side, 1), :]
                probs = jnp.where(valid, jnp.exp(scores - logs), 0.0)
                dprobs = mm_nt(v_blk, do_blk * keep)
                inner = jnp.sum(probs * dprobs, axis=0, keepdims=True)
                dscores = (probs * (dprobs - inner)).astype(BF)
                dvs.append(mm(probs.astype(BF), do_blk))
                dks.append(mm(dscores, q_blk))
                dqs.append(mm(kT_blk[side * HD : (side + 1) * HD], dscores))
            dqT_s[pl.ds(pl.multiple_of(blk * LANES, LANES), HD), :] = dqs[0]
            dqT_s[pl.ds(pl.multiple_of(blk * LANES + HD, HD), HD), :] = dqs[1]
            left = half_lane < HD
            dkv_s[:, at] = jnp.where(left, dks[0], dks[1]).astype(BF)
            vat = pl.ds(pl.multiple_of(width + blk * LANES, LANES), LANES)
            dkv_s[:, vat] = jnp.where(left, dvs[0], dvs[1]).astype(BF)
            return carry

        lax.fori_loop(0, width // LANES, heads, 0)
        dq = (jnp.transpose(dqT_s[...]) * HD**-0.5).astype(BF)
        dkv = dkv_s[...]
        part_q = mm(n1T_ref[:, b * full_len : b * full_len + local_len], dq)
        part_kv = mm(n1T_ref[:, wide], dkv)
        gqkv[0] = part_q if b == 0 else gqkv[0] + part_q
        gqkv[1] = part_kv if b == 0 else gqkv[1] + part_kv
        bias_q = bias_q + jnp.sum(dq.astype(F32), axis=0, keepdims=True)
        bias_v = bias_v + jnp.sum(dkv[:, width:].astype(F32), axis=0, keepdims=True)
        down = mm_nt(dkv, w_ref[:, width : 3 * width])
        down_own[span, :] = mm_nt(dq, w_ref[:, :width])
        down_own[span, :] += down[:local_len]
        for j in range(seq_count):
            part = down_own[span, :] if j == 0 else down[j * local_len : (j + 1) * local_len]
            tokens_in = own_ref[b] if j == 0 else oth_ref[j - 1, b]
            first_unit, _ = norm_parts(tokens_in.astype(F32))
            gain_sum = gain_sum + jnp.sum(part * first_unit, axis=0, keepdims=True)
            shift_sum = shift_sum + jnp.sum(part, axis=0, keepdims=True)
            if j > 0:
                down_oth[j - 1, span, :] = part.astype(BF)
    add_dense(slice(0, width), gqkv[0])
    add_dense(slice(width, 3 * width), gqkv[1])
    row = iota((LANES, 1), 0)
    mrow = jnp.where(row < experts, mrow_ref[...], 0.0)
    sums = (
        gain_sum,
        shift_sum,
        bias_q,
        bias_v,
        jnp.sum(da.astype(F32), axis=0, keepdims=True),
        jnp.sum(dn2 * unit, axis=0, keepdims=True),
        jnp.sum(dn2, axis=0, keepdims=True),
    )
    for j, value in enumerate(sums):
        mrow = jnp.where(row == experts + j, value, mrow)
    if not first:
        mrow = mrow_in[...] + mrow
    mrow_ref[...] = mrow
    if last:
        low_ref[:, misc_at : misc_at + LANES] = jnp.transpose(mrow).astype(BF)


def input_kernel(cfg, own_ref, got_ref, x_ref, dm_ref, wm_ref, *refs):
    out_ref = refs[-1]
    images, local_len, seq_count, width, experts = cfg
    tokens = images * local_len
    rows = jnp.transpose(wm_ref[...].astype(F32))
    dn1 = own_ref[...]
    for j in range(seq_count - 1):
        dn1 = dn1 + got_ref[j].astype(F32)
    unit, scale = norm_parts(x_ref[...].reshape(tokens, width).astype(F32))
    grad = dm_ref[...] + norm_pull(unit, scale, rows[experts : experts + 1, :], dn1)
    out_ref[...] = grad.astype(BF).reshape(images, local_len, width)


def mix_kernel(cfg, back_ref, pcol_ref, *refs):
    for mb in range(MICRO):

        @pl.when(pl.program_id(0) == mb)
        def _():
            mix_part(cfg, back_ref, pcol_ref, refs[2 * mb], refs[2 * mb + 1], refs[-1])


def mix_part(cfg, back_ref, pcol_ref, gate_ref, middle_ref, out_ref):
    images, local_len, width, experts, room = cfg
    tokens = images * local_len
    slots = experts * room
    back = back_ref[...].astype(F32).reshape(slots, width).astype(BF)
    slot_of = iota((tokens, slots), 1)
    lane = iota((tokens, LANES), 1)
    gate = gate_ref[...]
    total = middle_ref[...]
    for k in range(TOP):
        hot = jnp.where(slot_of == pcol_ref[0, :, k : k + 1], 1.0, 0.0).astype(BF)
        chosen = jnp.where(lane == pcol_ref[0, :, 2 + k : 3 + k], gate, 0.0)
        total = total + jnp.sum(chosen, axis=1, keepdims=True) * mm(hot, back)
    out_ref[...] = total.astype(BF).reshape(images, local_len, width)


def sum_kernel(gup_ref, gdn_ref, *refs):
    up_ref, dn_ref = refs[-2:]
    step = pl.program_id(0)
    ups = refs[: len(UP_PIECES)]
    downs = refs[len(UP_PIECES) : -2]
    got_up = ups[0][...]
    for ref, (begin, _) in zip(ups[1:], UP_PIECES[1:]):
        got_up = jnp.where(step >= begin, ref[...], got_up)
    got_dn = downs[0][...]
    for ref, (begin, _) in zip(downs[1:], DOWN_PIECES[1:]):
        got_dn = jnp.where(step >= begin, ref[...], got_dn)
    up_ref[0] = gup_ref[...] + got_up.astype(F32)
    dn_ref[0] = jnp.transpose(gdn_ref[...] + got_dn.astype(F32))


def smem_spec():
    return pl.BlockSpec(memory_space=pltpu.SMEM)


def params():
    return pltpu.CompilerParams(vmem_limit_bytes=VMEM_LIMIT)


def cost(micros):
    return pl.CostEstimate(
        flops=int(micros * 1e9), transcendentals=0, bytes_accessed=int(micros * 2e6)
    )


def struct(shape, kind):
    return jax.ShapeDtypeStruct(shape, kind)


def after(value, *others):
    return lax.optimization_barrier((value, *others))[0]


def on_device(
    images,
    cotangent,
    lengths,
    routes,
    attn_norm_gain,
    attn_norm_bias,
    qkv_weight,
    query_value_bias,
    proj_weight,
    proj_bias,
    moe_norm_gain,
    moe_norm_bias,
    router_weight,
    up_weight,
    up_bias,
    down_weight,
    down_bias,
):
    seq_count = lax.axis_size("seq")
    dp_count = lax.axis_size("dp")
    count = images.shape[0] // MICRO
    local_len = images.shape[1]
    width = images.shape[2]
    tokens = count * local_len
    full_len = local_len * seq_count
    experts = router_weight.shape[1]
    hidden = up_weight.shape[2]
    capacity = (5 * tokens * TOP + 4 * experts - 1) // (4 * experts)
    room = (capacity + window(capacity, MICRO - 1)[1] + 8) // 8 * 8
    assert all(window(capacity, mb)[1] + capacity < room for mb in range(MICRO))
    assert window(capacity, 1)[0] + room <= window(capacity, 2)[0] + 8
    slots = experts * room
    assert up_weight.shape[0] == 1 and experts == dp_count
    assert experts + VEC <= LANES and capacity <= LANES
    meta = jnp.stack([lax.axis_index("dp"), lax.axis_index("seq")]).astype(jnp.int32)
    packed_width = 4 * width + LANES

    def full(shape):
        return pl.BlockSpec(shape, lambda i: (0,) * len(shape))

    def token_spec(mb):
        return pl.BlockSpec((count, local_len, width), lambda i: (mb, 0, 0))

    def table_spec(mb, shape):
        return pl.BlockSpec((1, *shape), lambda i: (mb, 0, 0))

    def block_spec(mb):
        return pl.BlockSpec((experts, room, width), lambda i: (0, mb, 0))

    def window_spec(mb=None):
        def at(i):
            return (0, (capacity * (i if mb is None else mb)) // 8 * 8, 0)

        return pl.BlockSpec((pl.Element(experts), pl.Element(room), pl.Element(width)), at)

    any_spec = pl.BlockSpec(memory_space=pl.ANY)
    other_spec = lambda mb: pl.BlockSpec(
        (seq_count - 1, count, local_len, width), lambda i: (0, max(mb - 1, 0), 0, 0)
    )
    assert hidden // FF_BLOCK == UP_PIECES[-1][1] == DOWN_PIECES[-1][1]

    def piece_spec(begin, end):
        return pl.BlockSpec(
            (width, FF_BLOCK), lambda i: (0, jnp.clip(i - begin, 0, end - begin - 1))
        )

    misc_spec = pl.BlockSpec((width, LANES), lambda i: (0, 4 * width // LANES))
    moved = struct((experts, room, width), BF)
    merged = struct((experts, window(capacity, MICRO - 1)[0] + room, width), BF)
    tailed = struct((experts, (MICRO - 1) * room, width), BF)

    def seq_shift(array, j):
        return lax.ppermute(array, "seq", [((i + j) % seq_count, i) for i in range(seq_count)])

    others = []
    for part in (images[:count], images[count:]):
        moved_images = jnp.stack([seq_shift(part, j) for j in range(1, seq_count)])
        others.append(moved_images)

    sent_dy, prow, pcol = pl.pallas_call(
        functools.partial(place_kernel, experts, room, capacity),
        grid=(MICRO,),
        in_specs=[
            pl.BlockSpec((1, 1, 1, TOP, tokens), lambda i: (0, i, 0, 0, 0)),
            pl.BlockSpec((count, local_len, width), lambda i: (i, 0, 0)),
        ],
        out_specs=[
            pl.BlockSpec(merged.shape, lambda i: (0, 0, 0)),
            pl.BlockSpec((1, TOP, tokens), lambda i: (i, 0, 0)),
            pl.BlockSpec((1, tokens, 8), lambda i: (i, 0, 0)),
        ],
        out_shape=[
            merged,
            struct((MICRO, TOP, tokens), jnp.int32),
            struct((MICRO, tokens, 8), jnp.int32),
        ],
        compiler_params=params(),
        cost_estimate=cost(8),
        name="place",
    )(jnp.swapaxes(routes, 3, 4), cotangent)

    vectors = jnp.concatenate(
        [
            jnp.stack([attn_norm_gain, attn_norm_bias]),
            query_value_bias,
            jnp.stack([proj_bias, moe_norm_gain, moe_norm_bias, jnp.zeros_like(proj_bias)]),
        ],
        axis=0,
    )
    shard = router_weight.shape[0]
    bits = dp_count.bit_length() - 1
    assert dp_count == 1 << bits

    def across(value, offset):
        return lax.ppermute(value, "dp", [(i, i ^ offset) for i in range(dp_count)])

    def gather_rows(own, gate):
        quarter = dp_count // 4
        pieces = [own, *[across(own, k * quarter) for k in (1, 2, 3)]]
        held = [jnp.stack(pieces)]
        offsets = [[0, quarter, 2 * quarter, 3 * quarter]]
        for bit in reversed(range(bits - 2)):
            if bit == 0:
                held[-1] = after(held[-1], gate)
            held += [across(h, 1 << bit) for h in held]
            offsets += [[k ^ (1 << bit) for k in known] for known in offsets]
        return pl.pallas_call(
            functools.partial(assemble_kernel, offsets, shard),
            grid=(1,),
            in_specs=[smem_spec(), *[full(h.shape) for h in held]],
            out_specs=full((dp_count * shard, packed_width)),
            out_shape=struct((dp_count * shard, packed_width), BF),
            compiler_params=params(),
            cost_estimate=cost(3),
            name="assemble",
        )(meta, *held), pieces[1:]

    def halve(value, bit):
        mine = lax.bitwise_and(lax.shift_right_logical(lax.axis_index("dp"), bit), 1)
        value = value.reshape(-1, 2, shard, packed_width)
        keep = lax.dynamic_index_in_dim(value, mine, 1, keepdims=False)
        give = lax.dynamic_index_in_dim(value, 1 - mine, 1, keepdims=False).astype(BF)
        return keep.astype(F32) + across(give, 1 << bit).astype(F32)

    def scatter_far(value):
        high = lax.shift_right_logical(lax.axis_index("dp"), bits - 2)
        result = lax.dynamic_index_in_dim(value, high, 0, keepdims=False)
        for offset in (1, 2, 3):
            give = lax.dynamic_index_in_dim(
                value, lax.bitwise_xor(high, offset), 0, keepdims=False
            )
            result = result + across(give.astype(BF), offset << (bits - 2)).astype(F32)
        return result

    pack_args = (qkv_weight, proj_weight, router_weight.T, vectors)
    packed_shard = pl.pallas_call(
        functools.partial(pack_kernel, experts),
        grid=(1,),
        in_specs=[full(a.shape) for a in pack_args],
        out_specs=full((shard, packed_width)),
        out_shape=struct((shard, packed_width), BF),
        compiler_params=params(),
        cost_estimate=cost(1),
        name="pack",
    )(*pack_args)

    def exchange(array):
        return lax.all_to_all(array, "dp", split_axis=0, concat_axis=0, tiled=True)

    packed, near = gather_rows(packed_shard, others[1])
    dyb = exchange(after(sent_dy, *near, others[0]))

    def forward(mb):
        cfg = (count, local_len, seq_count, width, experts, room)
        outs = [
            ((experts, room, width), BF),
            ((tokens, width), F32),
            ((tokens, LANES), F32),
            ((tokens, width), BF),
            ((width, tokens), BF),
            ((tokens, width), BF),
            ((count * full_len, width), BF),
            ((count * full_len, width), BF),
            ((count * 8, local_len), F32),
            ((width, count * full_len), BF),
        ]
        return pl.pallas_call(
            functools.partial(forward_kernel, cfg, mb),
            grid=(1,),
            in_specs=[
                smem_spec(),
                smem_spec(),
                token_spec(mb),
                other_spec(mb),
                full((width, packed_width)),
                table_spec(mb, (TOP, tokens)),
            ],
            out_specs=[full(s) for s, _ in outs],
            out_shape=[struct(s, k) for s, k in outs],
            scratch_shapes=[
                pltpu.VMEM((tokens, width), BF),
                pltpu.VMEM((local_len, LANES), F32),
            ],
            compiler_params=params(),
            cost_estimate=cost(11),
            name="forward",
        )(meta, lengths, images, others[min(mb, 1)], packed, prow)

    def expert(mb, buf, results, tail_back, totals):
        first = mb == 0
        last = mb == MICRO - 1
        cfg = (experts, room, capacity, window(capacity, mb)[1], width)
        wide = lambda: pl.BlockSpec((width, FF_BLOCK), lambda i: (0, i))
        thin = lambda: pl.BlockSpec((1, FF_BLOCK), lambda i: (0, i))
        in_specs = [
            smem_spec(),
            full((experts, room, width)),
            window_spec(mb),
            misc_spec,
            pl.BlockSpec((1, width, FF_BLOCK), lambda i: (0, 0, i)),
            thin(),
            pl.BlockSpec((1, FF_BLOCK, width), lambda i: (0, i, 0)),
            full((1, width)),
        ]
        total_specs = [wide(), wide(), thin(), full((1, width))]
        args = [meta, buf, dyb, packed, up_weight, up_bias, down_weight, down_bias]
        aliases = {}
        if not first:
            aliases = {len(args): 0}
            aliases.update({len(args) + 1 + j: 2 + j for j in range(4)})
            in_specs += [window_spec(mb), *total_specs]
            args += [results, *totals]
        if mb >= 2:
            aliases[len(args)] = 1
            in_specs += [any_spec]
            args += [tail_back]
        outs = pl.pallas_call(
            functools.partial(expert_kernel, cfg, first, last),
            grid=(hidden // FF_BLOCK,),
            in_specs=in_specs,
            out_specs=[window_spec(mb), block_spec(max(mb - 1, 0)), *total_specs]
            + ([piece_spec(*p) for p in PIECES] if last else []),
            out_shape=[
                merged,
                moved if first else tailed,
                struct((width, hidden), F32),
                struct((width, hidden), F32),
                struct((1, hidden), F32),
                struct((1, width), F32),
            ]
            + (
                [struct((width, (end - begin) * FF_BLOCK), BF) for begin, end in PIECES]
                if last
                else []
            ),
            scratch_shapes=[
                pltpu.VMEM((slots, width), BF),
                pltpu.VMEM((width, slots), BF),
                pltpu.VMEM((slots, width), BF),
                pltpu.VMEM((width, slots), BF),
                pltpu.VMEM((slots, width), F32),
                pltpu.VMEM((slots, width), F32),
            ],
            input_output_aliases=aliases,
            compiler_params=params(),
            cost_estimate=cost(19),
            name="expert",
        )(*args)
        return outs[0], outs[1], tuple(outs[2:])

    def backward(mb, dback, saved, totals):
        first = mb == 0
        last = mb == MICRO - 1
        cfg = (count, local_len, seq_count, width, experts, room, capacity)
        middle, gate, second, oT, q, k, v, lse, n1T = saved
        whole = [gate, middle, second]
        heads = [oT, packed, q, k, v, lse, n1T]
        args = [meta, lengths, dback, pcol, *whole, cotangent, *heads, images, others[min(mb, 1)]]
        in_specs = [
            smem_spec(),
            smem_spec(),
            block_spec(max(mb - 1, 0)),
            table_spec(mb, (tokens, 8)),
            *[full(a.shape) for a in whole],
            token_spec(mb),
            *[full(a.shape) for a in heads],
            token_spec(mb),
            other_spec(mb),
        ]
        aliases = {}
        if not first:
            in_specs += [full(a.shape) for a in totals]
            args += list(totals)
            if not last:
                aliases = {len(args) - 2: 3, len(args) - 1: 4}
        outs = [
            ((tokens, width), F32),
            ((seq_count - 1, tokens, width), BF),
            ((tokens, width), F32),
            ((width, packed_width), BF) if last else ((width, 4 * width), F32),
            ((LANES, width), F32),
        ]
        return pl.pallas_call(
            functools.partial(backward_kernel, cfg, mb, first, last),
            grid=(1,),
            in_specs=in_specs,
            out_specs=[full(s) for s, _ in outs],
            out_shape=[struct(s, t) for s, t in outs],
            scratch_shapes=[
                pltpu.VMEM((tokens, width), BF),
                pltpu.VMEM((width, local_len), F32),
                pltpu.VMEM((full_len, 2 * width), BF),
            ],
            input_output_aliases=aliases,
            compiler_params=params(),
            cost_estimate=cost(0.1 if last else 17),
            name="backward",
        )(*args)

    def into(kernel, mb, args, specs, previous, micros, name):
        aliases = {}
        if previous is not None:
            aliases = {len(args): 0}
            args = [*args, previous]
            specs = [*specs, any_spec]
        return pl.pallas_call(
            kernel,
            grid=(1,),
            in_specs=specs,
            out_specs=token_spec(mb),
            out_shape=struct(images.shape, BF),
            input_output_aliases=aliases,
            compiler_params=params(),
            cost_estimate=cost(micros),
            name=name,
        )(*args)

    def finish(mb, own, got, dm, previous):
        cfg = (count, local_len, seq_count, width, experts)
        specs = [full(own.shape), full(got.shape), token_spec(mb), full(dm.shape), misc_spec]
        return into(
            functools.partial(input_kernel, cfg),
            mb,
            [own, got, images, dm, packed],
            specs,
            previous,
            0.1,
            "finish",
        )

    def mix(back):
        cfg = (count, local_len, width, experts, room)
        tables = sum([[saved[mb][1], saved[mb][0]] for mb in range(MICRO)], [])
        return pl.pallas_call(
            functools.partial(mix_kernel, cfg),
            grid=(MICRO,),
            in_specs=[
                window_spec(),
                pl.BlockSpec((1, tokens, 8), lambda i: (i, 0, 0)),
                *[full(t.shape) for t in tables],
            ],
            out_specs=pl.BlockSpec((count, local_len, width), lambda i: (i, 0, 0)),
            out_shape=struct(images.shape, BF),
            compiler_params=params(),
            cost_estimate=cost(0.1),
            name="mix",
        )(back, pcol, *tables)

    swap = [(i, (i + 1) % seq_count) for i in range(seq_count)]

    def seq_sum(value):
        if seq_count == 2:
            return value + lax.ppermute(value.astype(BF), "seq", swap).astype(F32)
        return lax.psum(value.astype(BF), "seq").astype(F32)

    passed = [forward(mb) for mb in range(MICRO)]
    saved = [outs[1:] for outs in passed]
    bufs = []
    for mb in range(MICRO):
        first_gate = (dyb,) if mb == 0 else ()
        bufs.append(exchange(after(passed[mb][0], *first_gate)))
    totals = None
    results = None
    ready = [None, None]
    for mb in range(MICRO):
        results, ready[min(mb, 1)], totals = expert(mb, bufs[mb], results, ready[1], totals)
    gup, gdn, gbias, gdbias, *pieces = totals
    arrived = []
    if seq_count == 2:
        arrived = [lax.ppermute(piece, "seq", swap) for piece in pieces]
    dense = None
    owns = []
    gots = []
    dms = []
    dbacks = [exchange(ready[0]), exchange(ready[1])]
    if arrived:
        dbacks[1], arrived[0] = lax.optimization_barrier((dbacks[1], arrived[0]))
    for mb in range(MICRO):
        dback = dbacks[min(mb, 1)]
        if mb == 2 and arrived:
            dense, arrived[1] = lax.optimization_barrier((dense, arrived[1]))
        own, oth, dm, *dense = backward(mb, dback, saved[mb], dense)
        owns.append(own)
        dms.append(dm)
        gots.append(
            jnp.stack(
                [
                    lax.ppermute(
                        oth[j - 1], "seq", [(i, (i + j) % seq_count) for i in range(seq_count)]
                    )
                    for j in range(1, seq_count)
                ]
            )
        )
    back = exchange(after(results, dbacks[1]))
    part = halve(after(dense[0], *arrived[2:4]), 0)
    mid = part

    if seq_count == 2:
        wide = lambda: pl.BlockSpec((width, FF_BLOCK), lambda i: (0, i))
        final_up, final_down = pl.pallas_call(
            sum_kernel,
            grid=(hidden // FF_BLOCK,),
            in_specs=[wide(), wide(), *[piece_spec(*p) for p in PIECES]],
            out_specs=[
                pl.BlockSpec((1, width, FF_BLOCK), lambda i: (0, 0, i)),
                pl.BlockSpec((1, FF_BLOCK, width), lambda i: (0, i, 0)),
            ],
            out_shape=[struct((1, width, hidden), F32), struct((1, hidden, width), F32)],
            compiler_params=params(),
            cost_estimate=cost(0.1),
            name="sum_experts",
        )(after(gup, mid), gdn, *arrived)
    else:
        sums = [lax.psum(piece, "seq").astype(F32) for piece in pieces]
        ups, downs = sums[: len(UP_PIECES)], sums[len(UP_PIECES) :]
        final_up = jnp.concatenate(ups, axis=1)[None]
        final_down = jnp.swapaxes(jnp.concatenate(downs, axis=1), 0, 1)[None]
    biases = seq_sum(jnp.concatenate([gbias, gdbias], axis=1))
    for bit in range(1, bits - 2):
        part = halve(part, bit)
    part, final_up, biases, back = lax.optimization_barrier((part, final_up, biases, back))
    shards = scatter_far(part)
    out = mix(back)
    grads = None
    for mb in range(MICRO):
        if mb == MICRO - 1:
            shards, out, grads = lax.optimization_barrier((shards, out, grads))
        grads = finish(mb, after(owns[mb], part), gots[mb], dms[mb], grads)
    final_up_shift = biases[:, :hidden]
    final_down_shift = biases[:, hidden:]

    shards = seq_sum(shards)
    misc = 4 * width + experts
    return (
        out,
        grads,
        shards[:, misc],
        shards[:, misc + 1],
        shards[:, : 3 * width],
        jnp.stack([shards[:, misc + 2], shards[:, misc + 3]]),
        shards[:, 3 * width : 4 * width],
        shards[:, misc + 4],
        shards[:, misc + 5],
        shards[:, misc + 6],
        shards[:, 4 * width : misc],
        final_up,
        final_up_shift,
        final_down,
        final_down_shift,
    )


def solution(mesh):
    return jax.shard_map(
        on_device,
        mesh=mesh,
        in_specs=(
            P("dp", "seq", None),
            P("dp", "seq", None),
            P("dp"),
            P("dp", None, "seq", None, None),
            P("dp"),
            P("dp"),
            P("dp", None),
            P(None, "dp"),
            P("dp", None),
            P("dp"),
            P("dp"),
            P("dp"),
            P("dp", None),
            P("dp", None, None),
            P("dp", None),
            P("dp", None, None),
            P("dp", None),
        ),
        out_specs=(
            P("dp", "seq", None),
            P("dp", "seq", None),
            P("dp"),
            P("dp"),
            P("dp", None),
            P(None, "dp"),
            P("dp", None),
            P("dp"),
            P("dp"),
            P("dp"),
            P("dp", None),
            P("dp", None, None),
            P("dp", None),
            P("dp", None, None),
            P("dp", None),
        ),
        check_vma=False,
    )
```

```python
import functools

import jax
import jax.numpy as jnp
from jax import lax
from jax.experimental import pallas as pl
from jax.experimental.pallas import tpu as pltpu
from jax.sharding import PartitionSpec as P

HD = 64
TOP = 2
MICRO = 3
BF = jnp.bfloat16
F32 = jnp.float32
EPS = 1e-06
LANES = 128
VEC = 8
FF_BLOCK = 512
UP_PIECES = ((0, 2), (2, 4))
DOWN_PIECES = ((0, 2), (2, 3), (3, 4))
PIECES = UP_PIECES + DOWN_PIECES
VMEM_LIMIT = 60 * 1024 * 1024


def mm(left, right):
    return jnp.dot(left, right, preferred_element_type=F32)


def mm_nt(left, right):
    return lax.dot_general(
        left, right, (((1,), (1,)), ((), ())), preferred_element_type=F32
    )


def iota(shape, dim):
    return lax.broadcasted_iota(jnp.int32, shape, dim)


def norm_parts(values):
    average = jnp.mean(values, axis=-1, keepdims=True)
    centred = values - average
    spread = jnp.mean(centred * centred, axis=-1, keepdims=True)
    scale = lax.rsqrt(spread + EPS)
    return centred * scale, scale


def norm_pull(unit, scale, gain, cotangent):
    inner = cotangent * gain
    mean_inner = jnp.mean(inner, axis=-1, keepdims=True)
    mean_unit = jnp.mean(inner * unit, axis=-1, keepdims=True)
    return scale * (inner - mean_inner - unit * mean_unit)


def misc_rows(w_ref, start):
    return jnp.transpose(w_ref[:, start : start + LANES].astype(F32))


def pack_kernel(experts, qkv_ref, proj_ref, router_ref, vec_ref, out_ref):
    width = proj_ref.shape[1]
    shard = proj_ref.shape[0]
    out_ref[:, : 3 * width] = qkv_ref[...]
    out_ref[:, 3 * width : 4 * width] = proj_ref[...]
    rows = jnp.concatenate([router_ref[...].astype(F32), vec_ref[...].astype(F32)], axis=0)
    columns = jnp.transpose(rows)
    tail = jnp.zeros((shard, LANES - columns.shape[1]), F32)
    out_ref[:, 4 * width :] = jnp.concatenate([columns, tail], axis=1).astype(BF)


def assemble_kernel(sources, shard, meta_ref, *refs):
    out_ref = refs[-1]
    for ref, offsets in zip(refs[:-1], sources):
        for at, offset in enumerate(offsets):
            row = jnp.bitwise_xor(meta_ref[0], offset) * shard
            out_ref[pl.ds(pl.multiple_of(row, shard), shard), :] = ref[at]


def window(capacity, mb):
    start = capacity * mb // 8 * 8
    return start, capacity * mb - start


def place_kernel(experts, room, capacity, routes_ref, dy_ref, send_ref, prow_ref, pcol_ref):
    for mb in range(MICRO):

        @pl.when(pl.program_id(0) == mb)
        def _():
            place_part(
                experts, room, window(capacity, mb), routes_ref, dy_ref, send_ref, prow_ref, pcol_ref
            )


def place_part(experts, room, where, routes_ref, dy_ref, send_ref, prow_ref, pcol_ref):
    start, shift = where
    tokens = routes_ref.shape[4]
    slots = experts * room
    rows = routes_ref[0, 0, 0]
    first_row = rows[0:1]
    second_row = rows[1:2]
    tall = jnp.concatenate([rows.astype(F32), jnp.zeros((LANES - TOP, tokens), F32)], axis=0)
    cols = jnp.transpose(tall)[:, 0:8].astype(jnp.int32)
    hot_first = (iota((experts, tokens), 0) == first_row).astype(F32)
    hot_second = (iota((experts, tokens), 0) == second_row).astype(F32)
    earlier = (iota((tokens, tokens), 0) < iota((tokens, tokens), 1)).astype(BF)
    before = mm((hot_first + hot_second).astype(BF), earlier)
    in_first = jnp.sum(before * hot_first, axis=0, keepdims=True).astype(jnp.int32)
    in_second = jnp.sum((before + hot_first) * hot_second, axis=0, keepdims=True).astype(jnp.int32)
    place_first = first_row * room + in_first + shift
    place_second = second_row * room + in_second + shift
    prow_ref[0, 0:1, :] = place_first
    prow_ref[0, 1:2, :] = place_second
    slot_of = iota((slots, tokens), 0)
    hot = jnp.where((slot_of == place_first) | (slot_of == place_second), 1.0, 0.0).astype(BF)
    flat = dy_ref[...].reshape(tokens, dy_ref.shape[-1])
    rows = mm(hot, flat)
    for e in range(experts):
        block = rows[e * room : (e + 1) * room].astype(BF)
        if shift:
            send_ref[e, start : start + 8] = send_ref[e, start : start + 8] + block[:8]
            send_ref[e, start + 8 : start + room] = block[8:]
        else:
            send_ref[e, start : start + room] = block
    first_col = cols[:, 0:1]
    second_col = cols[:, 1:2]
    hot_first = (iota((tokens, experts), 1) == first_col).astype(F32)
    hot_second = (iota((tokens, experts), 1) == second_col).astype(F32)
    later = (iota((tokens, tokens), 1) < iota((tokens, tokens), 0)).astype(BF)
    before = mm(later, (hot_first + hot_second).astype(BF))
    in_first = jnp.sum(before * hot_first, axis=1, keepdims=True).astype(jnp.int32)
    in_second = jnp.sum((before + hot_first) * hot_second, axis=1, keepdims=True).astype(jnp.int32)
    lane = iota((tokens, 8), 1)
    table = jnp.zeros((tokens, 8), jnp.int32)
    for at, col in enumerate(
        (
            first_col * room + in_first + shift,
            second_col * room + in_second + shift,
            first_col,
            second_col,
            in_first + shift,
            in_second + shift,
        )
    ):
        table = jnp.where(lane == at, col, table)
    pcol_ref[0] = table


def forward_kernel(
    cfg,
    mb,
    meta_ref,
    len_ref,
    own_ref,
    oth_ref,
    w_ref,
    prow_ref,
    send_ref,
    middle_ref,
    gate_ref,
    second_ref,
    oT_ref,
    q_ref,
    k_ref,
    v_ref,
    lse_ref,
    n1T_ref,
    att_ref,
    logs_ref,
):
    images, local_len, seq_count, width, experts, room = cfg
    full_len = local_len * seq_count
    tokens = images * local_len
    slots = experts * room
    misc_at = 4 * width
    rows = misc_rows(w_ref, misc_at)

    def vec(j):
        return rows[experts + j : experts + j + 1, :]

    here = meta_ref[1]
    lane = iota((1, LANES), 1)
    low_half = (lane < HD).astype(BF)
    high_half = (lane >= HD).astype(BF)
    for b in range(images):
        blocks = [own_ref[b]] + [oth_ref[j, b] for j in range(seq_count - 1)]
        full = jnp.concatenate(blocks, axis=0).astype(F32)
        unit, _ = norm_parts(full)
        normed = (unit * vec(0) + vec(1)).astype(BF)
        n1T_ref[:, b * full_len : (b + 1) * full_len] = jnp.transpose(normed)
        span = slice(b * local_len, (b + 1) * local_len)
        wide = slice(b * full_len, (b + 1) * full_len)
        queries = (mm(normed[:local_len], w_ref[:, :width]) + vec(2)).astype(BF)
        q_ref[span, :] = queries * jnp.asarray(HD**-0.5, BF)
        k_ref[wide, :] = mm(normed, w_ref[:, width : 2 * width]).astype(BF)
        v_ref[wide, :] = (mm(normed, w_ref[:, 2 * width : 3 * width]) + vec(3)).astype(BF)
        kpos = iota((1, full_len), 1)
        shift = jnp.zeros((1, full_len), jnp.int32)
        for j in range(seq_count):
            origin = lax.rem(here + j, seq_count) * local_len - j * local_len
            shift = jnp.where(kpos >= j * local_len, origin, shift)
        valid = (kpos + shift) < len_ref[mb * images + b]
        logs_ref[...] = jnp.zeros_like(logs_ref)

        def heads(blk, carry):
            at = pl.ds(pl.multiple_of(blk * LANES, LANES), LANES)
            q_blk = q_ref[span, at]
            k_blk = k_ref[wide, at]
            v_blk = v_ref[wide, at]
            outs = []
            for side, keep in enumerate((low_half, high_half)):
                scores = mm_nt(q_blk * keep, k_blk)
                scores = jnp.where(valid, scores, -1e30)
                highest = jnp.max(scores, axis=1, keepdims=True)
                powers = jnp.exp(scores - highest)
                total = jnp.sum(powers, axis=1, keepdims=True)
                probs = (powers * (1.0 / total)).astype(BF)
                outs.append(mm(probs, v_blk))
                logs_ref[...] = jnp.where(
                    lane == 2 * blk + side, highest + jnp.log(total), logs_ref[...]
                )
            att_ref[span, at] = jnp.where(lane < HD, outs[0], outs[1]).astype(BF)
            return carry

        lax.fori_loop(0, width // LANES, heads, 0)
        lse_ref[b * 8 : b * 8 + 8, :] = jnp.transpose(logs_ref[...])[0:8, :]
    attended = att_ref[...]
    oT_ref[...] = jnp.transpose(attended)
    branch = mm(attended, w_ref[:, 3 * width : 4 * width]) + vec(4)
    middle = own_ref[...].reshape(tokens, width).astype(F32) + branch
    middle_ref[...] = middle
    unit, _ = norm_parts(middle)
    second = (unit * vec(5) + vec(6)).astype(BF)
    second_ref[...] = second
    gate_ref[...] = gates(mm(second, w_ref[:, misc_at : misc_at + LANES]), experts)
    slot_of = iota((slots, tokens), 0)
    hot = jnp.where(
        (slot_of == prow_ref[0, 0:1, :]) | (slot_of == prow_ref[0, 1:2, :]), 1.0, 0.0
    ).astype(BF)
    sent = mm(hot, second)
    for e in range(experts):
        send_ref[e] = sent[e * room : (e + 1) * room].astype(BF)


def gates(logits, experts):
    real = iota((1, LANES), 1) < experts
    logits = jnp.where(real, logits, -1e30)
    powers = jnp.where(real, jnp.exp(logits - jnp.max(logits, axis=1, keepdims=True)), 0.0)
    return powers / jnp.sum(powers, axis=1, keepdims=True)


def expert_kernel(cfg, first, last, *refs):
    groups, room, capacity, shift, width = cfg
    meta_ref, buf_ref, dyb_ref, wm_ref, up_ref, ub_ref, down_ref, db_ref = refs[:8]
    refs = refs[8:]
    if not first:
        r_in, gup_in, gdn_in, gb_in, gdb_in = refs[:5]
        refs = refs[6 if last else 5 :]
    r_ref, dbuf_ref, gup_ref, gdn_ref, gb_ref, gdb_ref = refs[:6]
    refs = refs[6:]
    if last:
        lows = refs[: len(PIECES)]
        refs = refs[len(PIECES) :]
    (
        flat_s,
        flatT_s,
        dr_s,
        drT_s,
        racc_s,
        dacc_s,
    ) = refs
    slots = groups * room
    step = pl.program_id(0)
    experts = groups

    @pl.when(step == 0)
    def _():
        flat = buf_ref[...].astype(F32).reshape(slots, width).astype(BF)
        flat_s[...] = flat
        flatT_s[...] = jnp.transpose(flat)
        gate = gates(mm(flat, wm_ref[...]), experts)
        mine = iota((1, LANES), 1) == meta_ref[0]
        mine_gate = jnp.sum(jnp.where(mine, gate, 0.0), axis=1, keepdims=True)
        at = iota((groups, room, 1), 1)
        own = (at >= shift) & (at < shift + capacity)
        dy = jnp.where(own, dyb_ref[...].astype(F32), 0.0)
        dr = (dy.reshape(slots, width) * mine_gate).astype(BF)
        dr_s[...] = dr
        drT_s[...] = jnp.transpose(dr)
        shift_sum = jnp.sum(dr.astype(F32), axis=0, keepdims=True)
        gdb_ref[...] = shift_sum if first else gdb_in[...] + shift_sum
        racc_s[...] = jnp.zeros_like(racc_s)
        dacc_s[...] = jnp.zeros_like(dacc_s)

    flat = flat_s[...]
    dr = dr_s[...]
    hidden = mm(flat, up_ref[0]) + ub_ref[...].astype(F32)
    half_erf = 0.5 * lax.erf(hidden * (0.5**0.5)) + 0.5
    active = (hidden * half_erf).astype(BF)
    slope = half_erf + hidden * (jnp.exp(-0.5 * hidden * hidden) * 0.3989422804014327)
    racc_s[...] += mm(active, down_ref[0])
    grad_pre = mm_nt(dr, down_ref[0]) * slope
    low_pre = grad_pre.astype(BF)
    dacc_s[...] += mm_nt(low_pre, up_ref[0])
    gup = mm(flatT_s[...], low_pre)
    gdn = mm(drT_s[...], active)
    gbias = jnp.sum(low_pre.astype(F32), axis=0, keepdims=True)
    if not first:
        gup = gup_in[...] + gup
        gdn = gdn_in[...] + gdn
        gbias = gb_in[...] + gbias
    gup_ref[...] = gup
    gdn_ref[...] = gdn
    gb_ref[...] = gbias
    if last:
        for at, (low, (begin, end)) in enumerate(zip(lows, PIECES)):
            value = gup if at < len(UP_PIECES) else gdn

            @pl.when((step >= begin) & (step < end))
            def _(low=low, value=value):
                low[...] = value.astype(BF)

    @pl.when(step == pl.num_programs(0) - 1)
    def _():
        result = (racc_s[...] + db_ref[...].astype(F32)).astype(BF)
        for e in range(groups):
            block = result[e * room : (e + 1) * room]
            if shift:
                older = iota((8, 1), 0) < shift
                head = jnp.where(older, r_in[e, :8].astype(F32), block[:8].astype(F32))
                r_ref[e, :8] = head.astype(BF)
                r_ref[e, 8:] = block[8:]
            else:
                r_ref[e] = block
        dy = dyb_ref[...].astype(F32).reshape(slots, width)
        dgate = jnp.sum(dy * result.astype(F32), axis=1, keepdims=True).reshape(groups, room, 1)
        spread = jnp.where(
            iota((groups, room, LANES), 2) == iota((groups, room, LANES), 1), dgate, 0.0
        )
        as_row = jnp.sum(spread, axis=1, keepdims=True)
        high = as_row.astype(BF).astype(F32)
        tail = jnp.zeros((groups, 1, width - 2 * LANES), F32)
        as_row = jnp.concatenate([high, as_row - high, tail], axis=2)
        back = dacc_s[...].reshape(groups, room, width)
        back = jnp.where(iota((groups, room, 1), 1) == room - 1, as_row, back).astype(BF)
        for e in range(groups):
            dbuf_ref[e] = back[e]


def backward_kernel(cfg, mb, first, last, *refs):
    images, local_len, seq_count, width, experts, room, capacity = cfg
    (
        meta_ref,
        len_ref,
        dback_ref,
        pcol_ref,
        gate_ref,
        middle_ref,
        second_ref,
        dy_ref,
        oT_ref,
        w_ref,
        q_ref,
        k_ref,
        v_ref,
        lse_ref,
        n1T_ref,
        own_ref,
        oth_ref,
    ) = refs[:17]
    refs = refs[17:]
    if not first:
        g_in, mrow_in = refs[:2]
        refs = refs[2:]
    down_own, down_oth, dm_ref = refs[:3]
    refs = refs[3:]
    if last:
        low_ref = refs[0]
        refs = refs[1:]
    else:
        g_ref = refs[0]
        refs = refs[1:]
    mrow_ref, do_s, dqT_s, dkv_s = refs

    def add_dense(at, value):
        if not first:
            value = g_in[:, at] + value
        if last:
            low_ref[:, at] = value.astype(BF)
        else:
            g_ref[:, at] = value

    full_len = local_len * seq_count
    tokens = images * local_len
    slots = experts * room
    misc_at = 4 * width
    rows = misc_rows(w_ref, misc_at)
    here = meta_ref[1]

    def vec(j):
        return rows[experts + j : experts + j + 1, :]

    dback = dback_ref[...].astype(F32)
    back_rows = dback.reshape(slots, width).astype(BF)
    slot_of = iota((tokens, slots), 1)
    hot = jnp.where(
        (slot_of == pcol_ref[0, :, 0:1]) | (slot_of == pcol_ref[0, :, 1:2]), 1.0, 0.0
    ).astype(BF)
    from_experts = mm(hot, back_rows)
    spare = jnp.where(iota((experts, room, 1), 1) == room - 1, dback[:, :, : 2 * LANES], 0.0)
    spare = jnp.sum(spare, axis=1)
    spare = jnp.concatenate(
        [spare, jnp.zeros((LANES - experts, 2 * LANES), F32)], axis=0
    ).astype(BF)
    lane = iota((tokens, LANES), 1)
    pulled = jnp.zeros((tokens, LANES), F32)
    for k in range(TOP):
        within = jnp.where(lane == pcol_ref[0, :, 4 + k : 5 + k], 1.0, 0.0).astype(BF)
        found = mm_nt(jnp.concatenate([within, within], axis=1), spare)
        pulled = pulled + jnp.where(lane == pcol_ref[0, :, 2 + k : 3 + k], found, 0.0)
    gate = gate_ref[...]
    dlogit = gate * (pulled - jnp.sum(gate * pulled, axis=1, keepdims=True))
    dlogit_low = dlogit.astype(BF)
    mrow_ref[...] = mm(jnp.transpose(dlogit_low.astype(F32)).astype(BF), second_ref[...])
    dn2 = from_experts + mm_nt(dlogit_low, w_ref[:, misc_at : misc_at + LANES])
    unit, scale = norm_parts(middle_ref[...])
    dy = dy_ref[...].reshape(tokens, width).astype(F32)
    dm = dy + norm_pull(unit, scale, vec(5), dn2)
    dm_ref[...] = dm
    da = dm.astype(BF)
    gproj = mm(oT_ref[...], da)
    proj = slice(3 * width, 4 * width)
    add_dense(proj, gproj)
    do_s[...] = mm_nt(da, w_ref[:, proj]).astype(BF)
    half_lane = iota((1, LANES), 1)
    low_half = (half_lane < HD).astype(BF)
    high_half = (half_lane >= HD).astype(BF)
    gqkv = [None, None]
    bias_q = jnp.zeros((1, width), F32)
    bias_v = jnp.zeros((1, width), F32)
    gain_sum = jnp.zeros((1, width), F32)
    shift_sum = jnp.zeros((1, width), F32)
    for b in range(images):
        span = slice(b * local_len, (b + 1) * local_len)
        wide = slice(b * full_len, (b + 1) * full_len)
        kpos = iota((full_len, 1), 0)
        shift = jnp.zeros((full_len, 1), jnp.int32)
        for j in range(seq_count):
            origin = lax.rem(here + j, seq_count) * local_len - j * local_len
            shift = jnp.where(kpos >= j * local_len, origin, shift)
        valid = (kpos + shift) < len_ref[mb * images + b]

        def heads(blk, carry):
            at = pl.ds(pl.multiple_of(blk * LANES, LANES), LANES)
            q_blk = q_ref[span, at]
            k_blk = k_ref[wide, at]
            v_blk = v_ref[wide, at]
            do_blk = do_s[span, at]
            kT_blk = jnp.transpose(k_blk)
            dvs = []
            dks = []
            dqs = []
            for side, keep in enumerate((low_half, high_half)):
                scores = mm_nt(k_blk, q_blk * keep)
                logs = lse_ref[pl.ds(b * 8 + 2 * blk + side, 1), :]
                probs = jnp.where(valid, jnp.exp(scores - logs), 0.0)
                dprobs = mm_nt(v_blk, do_blk * keep)
                inner = jnp.sum(probs * dprobs, axis=0, keepdims=True)
                dscores = (probs * (dprobs - inner)).astype(BF)
                dvs.append(mm(probs.astype(BF), do_blk))
                dks.append(mm(dscores, q_blk))
                dqs.append(mm(kT_blk[side * HD : (side + 1) * HD], dscores))
            dqT_s[pl.ds(pl.multiple_of(blk * LANES, LANES), HD), :] = dqs[0]
            dqT_s[pl.ds(pl.multiple_of(blk * LANES + HD, HD), HD), :] = dqs[1]
            left = half_lane < HD
            dkv_s[:, at] = jnp.where(left, dks[0], dks[1]).astype(BF)
            vat = pl.ds(pl.multiple_of(width + blk * LANES, LANES), LANES)
            dkv_s[:, vat] = jnp.where(left, dvs[0], dvs[1]).astype(BF)
            return carry

        lax.fori_loop(0, width // LANES, heads, 0)
        dq = (jnp.transpose(dqT_s[...]) * HD**-0.5).astype(BF)
        dkv = dkv_s[...]
        part_q = mm(n1T_ref[:, b * full_len : b * full_len + local_len], dq)
        part_kv = mm(n1T_ref[:, wide], dkv)
        gqkv[0] = part_q if b == 0 else gqkv[0] + part_q
        gqkv[1] = part_kv if b == 0 else gqkv[1] + part_kv
        bias_q = bias_q + jnp.sum(dq.astype(F32), axis=0, keepdims=True)
        bias_v = bias_v + jnp.sum(dkv[:, width:].astype(F32), axis=0, keepdims=True)
        down = mm_nt(dkv, w_ref[:, width : 3 * width])
        down_own[span, :] = mm_nt(dq, w_ref[:, :width])
        down_own[span, :] += down[:local_len]
        for j in range(seq_count):
            part = down_own[span, :] if j == 0 else down[j * local_len : (j + 1) * local_len]
            tokens_in = own_ref[b] if j == 0 else oth_ref[j - 1, b]
            first_unit, _ = norm_parts(tokens_in.astype(F32))
            gain_sum = gain_sum + jnp.sum(part * first_unit, axis=0, keepdims=True)
            shift_sum = shift_sum + jnp.sum(part, axis=0, keepdims=True)
            if j > 0:
                down_oth[j - 1, span, :] = part.astype(BF)
    add_dense(slice(0, width), gqkv[0])
    add_dense(slice(width, 3 * width), gqkv[1])
    row = iota((LANES, 1), 0)
    mrow = jnp.where(row < experts, mrow_ref[...], 0.0)
    sums = (
        gain_sum,
        shift_sum,
        bias_q,
        bias_v,
        jnp.sum(da.astype(F32), axis=0, keepdims=True),
        jnp.sum(dn2 * unit, axis=0, keepdims=True),
        jnp.sum(dn2, axis=0, keepdims=True),
    )
    for j, value in enumerate(sums):
        mrow = jnp.where(row == experts + j, value, mrow)
    if not first:
        mrow = mrow_in[...] + mrow
    mrow_ref[...] = mrow
    if last:
        low_ref[:, misc_at : misc_at + LANES] = jnp.transpose(mrow).astype(BF)


def input_kernel(cfg, own_ref, got_ref, x_ref, dm_ref, wm_ref, *refs):
    out_ref = refs[-1]
    images, local_len, seq_count, width, experts = cfg
    tokens = images * local_len
    rows = jnp.transpose(wm_ref[...].astype(F32))
    dn1 = own_ref[...]
    for j in range(seq_count - 1):
        dn1 = dn1 + got_ref[j].astype(F32)
    unit, scale = norm_parts(x_ref[...].reshape(tokens, width).astype(F32))
    grad = dm_ref[...] + norm_pull(unit, scale, rows[experts : experts + 1, :], dn1)
    out_ref[...] = grad.astype(BF).reshape(images, local_len, width)


def mix_kernel(cfg, back_ref, pcol_ref, *refs):
    for mb in range(MICRO):

        @pl.when(pl.program_id(0) == mb)
        def _():
            mix_part(cfg, back_ref, pcol_ref, refs[2 * mb], refs[2 * mb + 1], refs[-1])


def mix_part(cfg, back_ref, pcol_ref, gate_ref, middle_ref, out_ref):
    images, local_len, width, experts, room = cfg
    tokens = images * local_len
    slots = experts * room
    back = back_ref[...].astype(F32).reshape(slots, width).astype(BF)
    slot_of = iota((tokens, slots), 1)
    lane = iota((tokens, LANES), 1)
    gate = gate_ref[...]
    total = middle_ref[...]
    for k in range(TOP):
        hot = jnp.where(slot_of == pcol_ref[0, :, k : k + 1], 1.0, 0.0).astype(BF)
        chosen = jnp.where(lane == pcol_ref[0, :, 2 + k : 3 + k], gate, 0.0)
        total = total + jnp.sum(chosen, axis=1, keepdims=True) * mm(hot, back)
    out_ref[...] = total.astype(BF).reshape(images, local_len, width)


def sum_kernel(gup_ref, gdn_ref, *refs):
    up_ref, dn_ref = refs[-2:]
    step = pl.program_id(0)
    ups = refs[: len(UP_PIECES)]
    downs = refs[len(UP_PIECES) : -2]
    got_up = ups[0][...]
    for ref, (begin, _) in zip(ups[1:], UP_PIECES[1:]):
        got_up = jnp.where(step >= begin, ref[...], got_up)
    got_dn = downs[0][...]
    for ref, (begin, _) in zip(downs[1:], DOWN_PIECES[1:]):
        got_dn = jnp.where(step >= begin, ref[...], got_dn)
    up_ref[0] = gup_ref[...] + got_up.astype(F32)
    dn_ref[0] = jnp.transpose(gdn_ref[...] + got_dn.astype(F32))


def smem_spec():
    return pl.BlockSpec(memory_space=pltpu.SMEM)


def params():
    return pltpu.CompilerParams(vmem_limit_bytes=VMEM_LIMIT)


def cost(micros):
    return pl.CostEstimate(
        flops=int(micros * 1e9), transcendentals=0, bytes_accessed=int(micros * 2e6)
    )


def struct(shape, kind):
    return jax.ShapeDtypeStruct(shape, kind)


def after(value, *others):
    return lax.optimization_barrier((value, *others))[0]


def on_device(
    images,
    cotangent,
    lengths,
    routes,
    attn_norm_gain,
    attn_norm_bias,
    qkv_weight,
    query_value_bias,
    proj_weight,
    proj_bias,
    moe_norm_gain,
    moe_norm_bias,
    router_weight,
    up_weight,
    up_bias,
    down_weight,
    down_bias,
):
    seq_count = lax.axis_size("seq")
    dp_count = lax.axis_size("dp")
    count = images.shape[0] // MICRO
    local_len = images.shape[1]
    width = images.shape[2]
    tokens = count * local_len
    full_len = local_len * seq_count
    experts = router_weight.shape[1]
    hidden = up_weight.shape[2]
    capacity = (5 * tokens * TOP + 4 * experts - 1) // (4 * experts)
    room = (capacity + window(capacity, MICRO - 1)[1] + 8) // 8 * 8
    assert all(window(capacity, mb)[1] + capacity < room for mb in range(MICRO))
    assert window(capacity, 1)[0] + room <= window(capacity, 2)[0] + 8
    slots = experts * room
    assert up_weight.shape[0] == 1 and experts == dp_count
    assert experts + VEC <= LANES and capacity <= LANES
    meta = jnp.stack([lax.axis_index("dp"), lax.axis_index("seq")]).astype(jnp.int32)
    packed_width = 4 * width + LANES

    def full(shape):
        return pl.BlockSpec(shape, lambda i: (0,) * len(shape))

    def token_spec(mb):
        return pl.BlockSpec((count, local_len, width), lambda i: (mb, 0, 0))

    def table_spec(mb, shape):
        return pl.BlockSpec((1, *shape), lambda i: (mb, 0, 0))

    def block_spec(mb):
        return pl.BlockSpec((experts, room, width), lambda i: (0, mb, 0))

    def window_spec(mb=None):
        def at(i):
            return (0, (capacity * (i if mb is None else mb)) // 8 * 8, 0)

        return pl.BlockSpec((pl.Element(experts), pl.Element(room), pl.Element(width)), at)

    any_spec = pl.BlockSpec(memory_space=pl.ANY)
    other_spec = lambda mb: pl.BlockSpec(
        (seq_count - 1, count, local_len, width), lambda i: (0, max(mb - 1, 0), 0, 0)
    )
    assert hidden // FF_BLOCK == UP_PIECES[-1][1] == DOWN_PIECES[-1][1]

    def piece_spec(begin, end):
        return pl.BlockSpec(
            (width, FF_BLOCK), lambda i: (0, jnp.clip(i - begin, 0, end - begin - 1))
        )

    misc_spec = pl.BlockSpec((width, LANES), lambda i: (0, 4 * width // LANES))
    moved = struct((experts, room, width), BF)
    merged = struct((experts, window(capacity, MICRO - 1)[0] + room, width), BF)
    tailed = struct((experts, (MICRO - 1) * room, width), BF)

    def seq_shift(array, j):
        return lax.ppermute(array, "seq", [((i + j) % seq_count, i) for i in range(seq_count)])

    others = []
    for part in (images[:count], images[count:]):
        moved_images = jnp.stack([seq_shift(part, j) for j in range(1, seq_count)])
        others.append(moved_images)

    sent_dy, prow, pcol = pl.pallas_call(
        functools.partial(place_kernel, experts, room, capacity),
        grid=(MICRO,),
        in_specs=[
            pl.BlockSpec((1, 1, 1, TOP, tokens), lambda i: (0, i, 0, 0, 0)),
            pl.BlockSpec((count, local_len, width), lambda i: (i, 0, 0)),
        ],
        out_specs=[
            pl.BlockSpec(merged.shape, lambda i: (0, 0, 0)),
            pl.BlockSpec((1, TOP, tokens), lambda i: (i, 0, 0)),
            pl.BlockSpec((1, tokens, 8), lambda i: (i, 0, 0)),
        ],
        out_shape=[
            merged,
            struct((MICRO, TOP, tokens), jnp.int32),
            struct((MICRO, tokens, 8), jnp.int32),
        ],
        compiler_params=params(),
        cost_estimate=cost(8),
        name="place",
    )(jnp.swapaxes(routes, 3, 4), cotangent)

    vectors = jnp.concatenate(
        [
            jnp.stack([attn_norm_gain, attn_norm_bias]),
            query_value_bias,
            jnp.stack([proj_bias, moe_norm_gain, moe_norm_bias, jnp.zeros_like(proj_bias)]),
        ],
        axis=0,
    )
    shard = router_weight.shape[0]
    bits = dp_count.bit_length() - 1
    assert dp_count == 1 << bits

    def across(value, offset):
        return lax.ppermute(value, "dp", [(i, i ^ offset) for i in range(dp_count)])

    def gather_rows(own, gate):
        quarter = dp_count // 4
        pieces = [own, *[across(own, k * quarter) for k in (1, 2, 3)]]
        held = [jnp.stack(pieces)]
        offsets = [[0, quarter, 2 * quarter, 3 * quarter]]
        for bit in reversed(range(bits - 2)):
            if bit == 0:
                held[-1] = after(held[-1], gate)
            held += [across(h, 1 << bit) for h in held]
            offsets += [[k ^ (1 << bit) for k in known] for known in offsets]
        return pl.pallas_call(
            functools.partial(assemble_kernel, offsets, shard),
            grid=(1,),
            in_specs=[smem_spec(), *[full(h.shape) for h in held]],
            out_specs=full((dp_count * shard, packed_width)),
            out_shape=struct((dp_count * shard, packed_width), BF),
            compiler_params=params(),
            cost_estimate=cost(3),
            name="assemble",
        )(meta, *held), pieces[1:]

    def halve(value, bit):
        mine = lax.bitwise_and(lax.shift_right_logical(lax.axis_index("dp"), bit), 1)
        value = value.reshape(-1, 2, shard, packed_width)
        keep = lax.dynamic_index_in_dim(value, mine, 1, keepdims=False)
        give = lax.dynamic_index_in_dim(value, 1 - mine, 1, keepdims=False).astype(BF)
        return keep.astype(F32) + across(give, 1 << bit).astype(F32)

    def scatter_far(value):
        high = lax.shift_right_logical(lax.axis_index("dp"), bits - 2)
        result = lax.dynamic_index_in_dim(value, high, 0, keepdims=False)
        for offset in (1, 2, 3):
            give = lax.dynamic_index_in_dim(
                value, lax.bitwise_xor(high, offset), 0, keepdims=False
            )
            result = result + across(give.astype(BF), offset << (bits - 2)).astype(F32)
        return result

    pack_args = (qkv_weight, proj_weight, router_weight.T, vectors)
    packed_shard = pl.pallas_call(
        functools.partial(pack_kernel, experts),
        grid=(1,),
        in_specs=[full(a.shape) for a in pack_args],
        out_specs=full((shard, packed_width)),
        out_shape=struct((shard, packed_width), BF),
        compiler_params=params(),
        cost_estimate=cost(1),
        name="pack",
    )(*pack_args)

    def exchange(array):
        return lax.all_to_all(array, "dp", split_axis=0, concat_axis=0, tiled=True)

    packed, near = gather_rows(packed_shard, others[1])
    dyb = exchange(after(sent_dy, *near, others[0]))

    def forward(mb):
        cfg = (count, local_len, seq_count, width, experts, room)
        outs = [
            ((experts, room, width), BF),
            ((tokens, width), F32),
            ((tokens, LANES), F32),
            ((tokens, width), BF),
            ((width, tokens), BF),
            ((tokens, width), BF),
            ((count * full_len, width), BF),
            ((count * full_len, width), BF),
            ((count * 8, local_len), F32),
            ((width, count * full_len), BF),
        ]
        return pl.pallas_call(
            functools.partial(forward_kernel, cfg, mb),
            grid=(1,),
            in_specs=[
                smem_spec(),
                smem_spec(),
                token_spec(mb),
                other_spec(mb),
                full((width, packed_width)),
                table_spec(mb, (TOP, tokens)),
            ],
            out_specs=[full(s) for s, _ in outs],
            out_shape=[struct(s, k) for s, k in outs],
            scratch_shapes=[
                pltpu.VMEM((tokens, width), BF),
                pltpu.VMEM((local_len, LANES), F32),
            ],
            compiler_params=params(),
            cost_estimate=cost(11),
            name="forward",
        )(meta, lengths, images, others[min(mb, 1)], packed, prow)

    def expert(mb, buf, results, tail_back, totals):
        first = mb == 0
        last = mb == MICRO - 1
        cfg = (experts, room, capacity, window(capacity, mb)[1], width)
        wide = lambda: pl.BlockSpec((width, FF_BLOCK), lambda i: (0, i))
        thin = lambda: pl.BlockSpec((1, FF_BLOCK), lambda i: (0, i))
        in_specs = [
            smem_spec(),
            full((experts, room, width)),
            window_spec(mb),
            misc_spec,
            pl.BlockSpec((1, width, FF_BLOCK), lambda i: (0, 0, i)),
            thin(),
            pl.BlockSpec((1, FF_BLOCK, width), lambda i: (0, i, 0)),
            full((1, width)),
        ]
        total_specs = [wide(), wide(), thin(), full((1, width))]
        args = [meta, buf, dyb, packed, up_weight, up_bias, down_weight, down_bias]
        aliases = {}
        if not first:
            aliases = {len(args): 0}
            aliases.update({len(args) + 1 + j: 2 + j for j in range(4)})
            in_specs += [window_spec(mb), *total_specs]
            args += [results, *totals]
        if mb >= 2:
            aliases[len(args)] = 1
            in_specs += [any_spec]
            args += [tail_back]
        outs = pl.pallas_call(
            functools.partial(expert_kernel, cfg, first, last),
            grid=(hidden // FF_BLOCK,),
            in_specs=in_specs,
            out_specs=[window_spec(mb), block_spec(max(mb - 1, 0)), *total_specs]
            + ([piece_spec(*p) for p in PIECES] if last else []),
            out_shape=[
                merged,
                moved if first else tailed,
                struct((width, hidden), F32),
                struct((width, hidden), F32),
                struct((1, hidden), F32),
                struct((1, width), F32),
            ]
            + (
                [struct((width, (end - begin) * FF_BLOCK), BF) for begin, end in PIECES]
                if last
                else []
            ),
            scratch_shapes=[
                pltpu.VMEM((slots, width), BF),
                pltpu.VMEM((width, slots), BF),
                pltpu.VMEM((slots, width), BF),
                pltpu.VMEM((width, slots), BF),
                pltpu.VMEM((slots, width), F32),
                pltpu.VMEM((slots, width), F32),
            ],
            input_output_aliases=aliases,
            compiler_params=params(),
            cost_estimate=cost(19),
            name="expert",
        )(*args)
        return outs[0], outs[1], tuple(outs[2:])

    def backward(mb, dback, saved, totals):
        first = mb == 0
        last = mb == MICRO - 1
        cfg = (count, local_len, seq_count, width, experts, room, capacity)
        middle, gate, second, oT, q, k, v, lse, n1T = saved
        whole = [gate, middle, second]
        heads = [oT, packed, q, k, v, lse, n1T]
        args = [meta, lengths, dback, pcol, *whole, cotangent, *heads, images, others[min(mb, 1)]]
        in_specs = [
            smem_spec(),
            smem_spec(),
            block_spec(max(mb - 1, 0)),
            table_spec(mb, (tokens, 8)),
            *[full(a.shape) for a in whole],
            token_spec(mb),
            *[full(a.shape) for a in heads],
            token_spec(mb),
            other_spec(mb),
        ]
        aliases = {}
        if not first:
            in_specs += [full(a.shape) for a in totals]
            args += list(totals)
            if not last:
                aliases = {len(args) - 2: 3, len(args) - 1: 4}
        outs = [
            ((tokens, width), F32),
            ((seq_count - 1, tokens, width), BF),
            ((tokens, width), F32),
            ((width, packed_width), BF) if last else ((width, 4 * width), F32),
            ((LANES, width), F32),
        ]
        return pl.pallas_call(
            functools.partial(backward_kernel, cfg, mb, first, last),
            grid=(1,),
            in_specs=in_specs,
            out_specs=[full(s) for s, _ in outs],
            out_shape=[struct(s, t) for s, t in outs],
            scratch_shapes=[
                pltpu.VMEM((tokens, width), BF),
                pltpu.VMEM((width, local_len), F32),
                pltpu.VMEM((full_len, 2 * width), BF),
            ],
            input_output_aliases=aliases,
            compiler_params=params(),
            cost_estimate=cost(0.1 if last else 17),
            name="backward",
        )(*args)

    def into(kernel, mb, args, specs, previous, micros, name):
        aliases = {}
        if previous is not None:
            aliases = {len(args): 0}
            args = [*args, previous]
            specs = [*specs, any_spec]
        return pl.pallas_call(
            kernel,
            grid=(1,),
            in_specs=specs,
            out_specs=token_spec(mb),
            out_shape=struct(images.shape, BF),
            input_output_aliases=aliases,
            compiler_params=params(),
            cost_estimate=cost(micros),
            name=name,
        )(*args)

    def finish(mb, own, got, dm, previous):
        cfg = (count, local_len, seq_count, width, experts)
        specs = [full(own.shape), full(got.shape), token_spec(mb), full(dm.shape), misc_spec]
        return into(
            functools.partial(input_kernel, cfg),
            mb,
            [own, got, images, dm, packed],
            specs,
            previous,
            0.1,
            "finish",
        )

    def mix(back):
        cfg = (count, local_len, width, experts, room)
        tables = sum([[saved[mb][1], saved[mb][0]] for mb in range(MICRO)], [])
        return pl.pallas_call(
            functools.partial(mix_kernel, cfg),
            grid=(MICRO,),
            in_specs=[
                window_spec(),
                pl.BlockSpec((1, tokens, 8), lambda i: (i, 0, 0)),
                *[full(t.shape) for t in tables],
            ],
            out_specs=pl.BlockSpec((count, local_len, width), lambda i: (i, 0, 0)),
            out_shape=struct(images.shape, BF),
            compiler_params=params(),
            cost_estimate=cost(0.1),
            name="mix",
        )(back, pcol, *tables)

    swap = [(i, (i + 1) % seq_count) for i in range(seq_count)]

    def seq_sum(value):
        if seq_count == 2:
            return value + lax.ppermute(value.astype(BF), "seq", swap).astype(F32)
        return lax.psum(value.astype(BF), "seq").astype(F32)

    passed = [forward(mb) for mb in range(MICRO)]
    saved = [outs[1:] for outs in passed]
    bufs = []
    for mb in range(MICRO):
        first_gate = (dyb,) if mb == 0 else ()
        bufs.append(exchange(after(passed[mb][0], *first_gate)))
    totals = None
    results = None
    ready = [None, None]
    for mb in range(MICRO):
        results, ready[min(mb, 1)], totals = expert(mb, bufs[mb], results, ready[1], totals)
    gup, gdn, gbias, gdbias, *pieces = totals
    arrived = []
    if seq_count == 2:
        arrived = [lax.ppermute(piece, "seq", swap) for piece in pieces]
    dense = None
    owns = []
    gots = []
    dms = []
    dbacks = [exchange(ready[0]), exchange(ready[1])]
    if arrived:
        dbacks[1], arrived[0] = lax.optimization_barrier((dbacks[1], arrived[0]))
    for mb in range(MICRO):
        dback = dbacks[min(mb, 1)]
        if mb == 2 and arrived:
            dense, arrived[1] = lax.optimization_barrier((dense, arrived[1]))
        own, oth, dm, *dense = backward(mb, dback, saved[mb], dense)
        owns.append(own)
        dms.append(dm)
        gots.append(
            jnp.stack(
                [
                    lax.ppermute(
                        oth[j - 1], "seq", [(i, (i + j) % seq_count) for i in range(seq_count)]
                    )
                    for j in range(1, seq_count)
                ]
            )
        )
    back = exchange(after(results, dbacks[1]))
    part = halve(after(dense[0], *arrived[2:4]), 0)
    mid = part

    if seq_count == 2:
        wide = lambda: pl.BlockSpec((width, FF_BLOCK), lambda i: (0, i))
        final_up, final_down = pl.pallas_call(
            sum_kernel,
            grid=(hidden // FF_BLOCK,),
            in_specs=[wide(), wide(), *[piece_spec(*p) for p in PIECES]],
            out_specs=[
                pl.BlockSpec((1, width, FF_BLOCK), lambda i: (0, 0, i)),
                pl.BlockSpec((1, FF_BLOCK, width), lambda i: (0, i, 0)),
            ],
            out_shape=[struct((1, width, hidden), F32), struct((1, hidden, width), F32)],
            compiler_params=params(),
            cost_estimate=cost(0.1),
            name="sum_experts",
        )(after(gup, mid), gdn, *arrived)
    else:
        sums = [lax.psum(piece, "seq").astype(F32) for piece in pieces]
        ups, downs = sums[: len(UP_PIECES)], sums[len(UP_PIECES) :]
        final_up = jnp.concatenate(ups, axis=1)[None]
        final_down = jnp.swapaxes(jnp.concatenate(downs, axis=1), 0, 1)[None]
    biases = seq_sum(jnp.concatenate([gbias, gdbias], axis=1))
    for bit in range(1, bits - 2):
        part = halve(part, bit)
    part, final_up, final_up_shift, final_down_shift, back = lax.optimization_barrier(
        (part, final_up, biases[:, :hidden], biases[:, hidden:], back)
    )
    shards = scatter_far(part)
    out = mix(back)
    grads = None
    for mb in range(MICRO):
        if mb == MICRO - 1:
            shards, out, grads = lax.optimization_barrier((shards, out, grads))
        grads = finish(mb, after(owns[mb], part), gots[mb], dms[mb], grads)

    shards = seq_sum(shards)
    misc = 4 * width + experts
    return (
        out,
        grads,
        shards[:, misc],
        shards[:, misc + 1],
        shards[:, : 3 * width],
        jnp.stack([shards[:, misc + 2], shards[:, misc + 3]]),
        shards[:, 3 * width : 4 * width],
        shards[:, misc + 4],
        shards[:, misc + 5],
        shards[:, misc + 6],
        shards[:, 4 * width : misc],
        final_up,
        final_up_shift,
        final_down,
        final_down_shift,
    )


def solution(mesh):
    return jax.shard_map(
        on_device,
        mesh=mesh,
        in_specs=(
            P("dp", "seq", None),
            P("dp", "seq", None),
            P("dp"),
            P("dp", None, "seq", None, None),
            P("dp"),
            P("dp"),
            P("dp", None),
            P(None, "dp"),
            P("dp", None),
            P("dp"),
            P("dp"),
            P("dp"),
            P("dp", None),
            P("dp", None, None),
            P("dp", None),
            P("dp", None, None),
            P("dp", None),
        ),
        out_specs=(
            P("dp", "seq", None),
            P("dp", "seq", None),
            P("dp"),
            P("dp"),
            P("dp", None),
            P(None, "dp"),
            P("dp", None),
            P("dp"),
            P("dp"),
            P("dp"),
            P("dp", None),
            P("dp", None, None),
            P("dp", None),
            P("dp", None, None),
            P("dp", None),
        ),
        check_vma=False,
    )
```
